256 devices in a mesh: row: 16 (over y, x), col: 16 (over z, core).
Axes of the slice: x: 4, y: 4, z: 8, core: 2. Of those that a mesh axis runs over, the one named last changes fastest.
Arguments:
- rhs: float32 [128, 32768], P('row', 'col'), may hold values from -60 to 60
- flex_tiles: float32 [131072, 2048], P('row', 'col'), may hold values from -0.25 to 0.25
- flex_cols: int32 [256, 64], P('row', 'col'), may hold values from 0 to 15, as said below
- stiff_tiles: float32 [131072, 2048], P('row', 'col'), may hold values from -0.25 to 0.25
- stiff_cols: int32 [256, 64], P('row', 'col'), may hold values from 0 to 15, as said below
- deflation: float32 [512, 32768], P('row', 'col'), may hold values from -0.375 to 0.375
- coarse_rows: float32 [8192, 8192], P(('row', 'col')), may hold values from -5 to 5, as said below
- face_rows: int32 [64, 2048], P('row', 'col'), may hold values from 0 to 2047, as said below
- face_len: int32 [16, 64], P('row', 'col'), may hold values from 0 to 128, as said below
Outputs:
- solution: float32 [128, 32768], P('row', 'col')
- residual: float32 [128, 32768], P('row', 'col')
- correction: float32 [128, 32768], P('row', 'col')
The draws below stay inside these ranges and needn't reach their ends.
Inputs may be any that keep to these rules, and one draw needn't show every extreme that they name: `flex_cols`: row b of a subdomain's block list names 4 different block columns, the first being b. `stiff_cols`: row b of a subdomain's block list names 4 different block columns, the first being b. `coarse_rows`: the whole matrix is symmetric. `face_rows`: the four lists of a subdomain name 512 different multipliers of it. `face_len`: the two subdomains of a face give it the same length; faces on the grid's boundary have length 0, inner faces at least 32.
All inputs are finite; a program needn't handle non-finite values.
Results may differ from the reference program's by a relative error of at most 0.0003.
Values sent between devices are 32-bit elements; how exact they have to be, the bound alone decides.
A program may use at most 64 MiB of HBM per device.

```python
import math
import jax
import jax.numpy as jnp
from jax import lax

M = 2048
TILE = 128
TPR = 4
FACE = 128
DEFL = 32
LOADS = 8
ITERS = 3
NB = 16
GRID_ROWS = 16
GRID_COLS = 16
COARSE = 8192


def draw_rhs(key, part):
    first_key, second_key = jax.random.split(jax.random.fold_in(key, 7), 2)
    shape = (GRID_ROWS, LOADS, GRID_COLS, M)
    how_many = GRID_ROWS * GRID_COLS
    position = (jnp.arange(GRID_ROWS)[:, None] * GRID_COLS + jnp.arange(GRID_COLS)[None, :]).astype(jnp.float32) / (how_many - 1)
    position = position[:, None, :, None]
    column_spread = jnp.exp(jax.random.uniform(second_key, (GRID_ROWS, 1, GRID_COLS, M), jnp.float32, 0.0, 2.302585)) / 3.1623
    base_draw = jnp.clip(jax.random.normal(first_key, shape, jnp.float32), -6.0, 6.0)
    values = base_draw * column_spread * 3.0 ** position
    return values.reshape(GRID_ROWS * LOADS, GRID_COLS * M)


def block_lists(key):
    how_many = GRID_ROWS * GRID_COLS * NB
    subkeys = jax.random.split(key, how_many)
    others = jax.vmap(lambda single: jax.random.permutation(single, NB - 1)[:TPR - 1])(subkeys)
    row_ids = (jnp.arange(how_many, dtype=jnp.int32) % NB)[:, None]
    col_ids = jnp.concatenate([row_ids, (row_ids + 1 + others) % NB], axis=1)
    shaped = col_ids.reshape(GRID_ROWS, GRID_COLS, NB, TPR).transpose(0, 2, 1, 3)
    return shaped.reshape(GRID_ROWS * NB, GRID_COLS * TPR).astype(jnp.int32)


def draw_flex_cols(key, part):
    return block_lists(jax.random.fold_in(key, 11))


def draw_stiff_cols(key, part):
    return block_lists(jax.random.fold_in(key, 13))


def draw_coarse_rows(key, part):
    first_key = jax.random.fold_in(jax.random.fold_in(key, 23), 0)
    raw_draw = jnp.clip(jax.random.normal(first_key, (COARSE, COARSE), jnp.float32), -6.0, 6.0)
    symmetric = (raw_draw + raw_draw.T) * (0.5 / math.sqrt(COARSE)) + jnp.eye(COARSE, dtype=jnp.float32)
    return symmetric


def draw_face_rows(key, part):
    subkeys = jax.random.split(jax.random.fold_in(key, 17), GRID_ROWS * GRID_COLS)
    picked = jax.vmap(lambda single: jax.random.permutation(single, M)[:4 * FACE])(subkeys)
    shaped = picked.reshape(GRID_ROWS, GRID_COLS, 4, FACE).transpose(0, 2, 1, 3)
    return shaped.reshape(GRID_ROWS * 4, GRID_COLS * FACE).astype(jnp.int32)


def draw_face_len(key, part):
    first_key, second_key = jax.random.split(jax.random.fold_in(key, 19))
    across = jax.random.randint(first_key, (GRID_ROWS, GRID_COLS - 1), FACE // 4, FACE + 1, jnp.int32)
    across = across.at[0, 0].set(FACE)
    downward = jax.random.randint(second_key, (GRID_ROWS - 1, GRID_COLS), FACE // 4, FACE + 1, jnp.int32)
    padded_down = jnp.pad(downward, ((1, 1), (0, 0)))
    padded_across = jnp.pad(across, ((0, 0), (1, 1)))
    stacked = jnp.stack([padded_down[:-1], padded_down[1:], padded_across[:, :-1], padded_across[:, 1:]], axis=-1)
    return stacked.reshape(GRID_ROWS, GRID_COLS * 4).astype(jnp.int32)


def block_levels(stream_key, shape, shards, low, high):
    def one(dim, blocks):
        heights = jax.random.uniform(jax.random.fold_in(jax.random.fold_in(stream_key, 6), dim), (blocks,), jnp.float32, low / len(shards), high / len(shards))
        return jnp.repeat(jnp.exp(heights), shape[dim] // blocks).reshape((-1,) + (1,) * (len(shape) - dim - 1))

    factor_of = one(*shards[0])
    for cut in shards[1:]:
        factor_of = factor_of * one(*cut)
    return factor_of


def centred(key, extent, scale, reach, cuts=(), kind=jnp.bfloat16):
    level = block_levels(key, extent, cuts, -0.22, 0.18) if cuts else 1.0
    drawn = jax.random.normal(key, extent, jnp.float32) * scale * level
    return jnp.minimum(jnp.maximum(drawn, -reach), reach).astype(kind)


def setup_inputs(seed: int = 0) -> dict:
    keys = jax.random.split(jax.random.key(seed), 10)
    return {
        "rhs": draw_rhs(jax.random.fold_in(keys[9], 71), 0),
        "flex_tiles": centred(keys[1], (GRID_ROWS * NB * TPR * TILE, GRID_COLS * TILE), (TILE * TPR) ** -0.5, 0.25, ((0, 16), (1, 16)), jnp.float32),
        "flex_cols": draw_flex_cols(jax.random.fold_in(keys[9], 71), 0),
        "stiff_tiles": centred(keys[3], (GRID_ROWS * NB * TPR * TILE, GRID_COLS * TILE), (TILE * TPR) ** -0.5, 0.25, ((0, 16), (1, 16)), jnp.float32),
        "stiff_cols": draw_stiff_cols(jax.random.fold_in(keys[9], 71), 0),
        "deflation": centred(keys[5], (GRID_ROWS * DEFL, GRID_COLS * M), (DEFL * 8) ** -0.5, 0.375, ((0, 16), (1, 16)), jnp.float32),
        "coarse_rows": draw_coarse_rows(jax.random.fold_in(keys[9], 71), 0),
        "face_rows": draw_face_rows(jax.random.fold_in(keys[9], 71), 0),
        "face_len": draw_face_len(jax.random.fold_in(keys[9], 71), 0),
    }


PRECISE = lax.Precision.HIGHEST


def sparse_forward(vector, tile_set, columns):
    load_count = vector.shape[0]
    blocks, per_row = columns.shape
    tile_width = tile_set.shape[-1]
    pieces = vector.reshape(load_count, blocks, tile_width)
    picked = jnp.take(pieces, columns.reshape(-1), axis=1).reshape(load_count, blocks, per_row, tile_width)
    product = jnp.einsum("lbkw,bkwv->lbv", picked, tile_set, precision=PRECISE)
    return product.reshape(load_count, blocks * tile_width)


def sparse_backward(vector, tile_set, columns):
    load_count = vector.shape[0]
    blocks, per_row = columns.shape
    tile_width = tile_set.shape[-1]
    pieces = vector.reshape(load_count, blocks, tile_width)
    product = jnp.einsum("lbv,bkwv->lbkw", pieces, tile_set, precision=PRECISE)
    onehot = (columns[:, :, None] == jnp.arange(blocks, dtype=jnp.int32)[None, None, :]).astype(jnp.float32)
    summed = jnp.einsum("lbkw,bkj->ljw", product, onehot, precision=PRECISE)
    return summed.reshape(load_count, blocks * tile_width)


def local_operator(vector, flex_set, flex_list, stiff_set, stiff_list):
    after_flex = sparse_forward(vector, flex_set, flex_list)
    after_stiff = sparse_forward(after_flex, stiff_set, stiff_list)
    back_stiff = sparse_backward(after_stiff, stiff_set, stiff_list)
    return sparse_backward(back_stiff, flex_set, flex_list)


def take_traces(field, face_index):
    return field[:, face_index]


def add_traces(face_index, jump_values):
    return jnp.zeros((LOADS, M), jnp.float32).at[:, face_index].add(jump_values)


def face_term(fields, face_index, live_len):
    traces = jax.vmap(jax.vmap(take_traces))(fields, face_index)
    zero_row = jnp.zeros_like(traces[:1, :, :, 0])
    from_north = jnp.concatenate([zero_row, traces[:-1, :, :, 1]], axis=0)
    from_south = jnp.concatenate([traces[1:, :, :, 0], zero_row], axis=0)
    zero_col = jnp.zeros_like(traces[:, :1, :, 0])
    from_west = jnp.concatenate([zero_col, traces[:, :-1, :, 3]], axis=1)
    from_east = jnp.concatenate([traces[:, 1:, :, 2], zero_col], axis=1)
    partner = jnp.stack([from_north, from_south, from_west, from_east], axis=3)
    slots = jnp.arange(FACE, dtype=jnp.int32)
    live_mask = (slots[None, None, None, :] < live_len[:, :, :, None]).astype(jnp.float32)
    jump_values = (traces - partner) * live_mask[:, :, None]
    return jax.vmap(jax.vmap(add_traces))(face_index, jump_values)


def reference(rhs, flex_tiles, flex_cols, stiff_tiles, stiff_cols, deflation, coarse_rows, face_rows, face_len):
    flex_whole = flex_tiles.reshape(GRID_ROWS, NB, TPR, TILE, GRID_COLS, TILE)
    stiff_whole = stiff_tiles.reshape(GRID_ROWS, NB, TPR, TILE, GRID_COLS, TILE)
    flex_lists = flex_cols.reshape(GRID_ROWS, NB, GRID_COLS, TPR)
    stiff_lists = stiff_cols.reshape(GRID_ROWS, NB, GRID_COLS, TPR)
    basis = deflation.reshape(GRID_ROWS, DEFL, GRID_COLS, M).transpose(0, 2, 1, 3)
    face_index = face_rows.reshape(GRID_ROWS, 4, GRID_COLS, FACE).transpose(0, 2, 1, 3)
    live_len = face_len.reshape(GRID_ROWS, GRID_COLS, 4)

    def one_local(packed):
        index, field = packed
        sub_row = index // GRID_COLS
        sub_col = index % GRID_COLS

        def pick_tiles(whole):
            row_part = lax.dynamic_index_in_dim(whole, sub_row, 0, False)
            return lax.dynamic_index_in_dim(row_part, sub_col, 3, False)

        def pick_list(whole):
            row_part = lax.dynamic_index_in_dim(whole, sub_row, 0, False)
            return lax.dynamic_index_in_dim(row_part, sub_col, 1, False)

        return local_operator(field, pick_tiles(flex_whole), pick_list(flex_lists),
                              pick_tiles(stiff_whole), pick_list(stiff_lists))

    def operate(fields):
        flat = fields.reshape(GRID_ROWS * GRID_COLS, LOADS, M)
        indices = jnp.arange(GRID_ROWS * GRID_COLS, dtype=jnp.int32)
        local_part = lax.map(one_local, (indices, flat)).reshape(fields.shape)
        return fields + local_part + face_term(fields, face_index, live_len)

    def precondition(fields):
        coefficients = jnp.einsum("rclm,rcdm->lrcd", fields, basis, precision=PRECISE)
        flat = coefficients.reshape(LOADS, COARSE)
        energy = jnp.dot(flat, coarse_rows.T, precision=PRECISE).reshape(LOADS, GRID_ROWS, GRID_COLS, DEFL)
        return fields + jnp.einsum("lrcd,rcdm->rclm", energy, basis, precision=PRECISE)

    def totals(first_field, second_field):
        return jnp.sum(first_field * second_field, axis=(0, 1, 3))

    def spread(values):
        return values[None, None, :, None]

    residual = rhs.reshape(GRID_ROWS, LOADS, GRID_COLS, M).transpose(0, 2, 1, 3)
    solution = jnp.zeros_like(residual)
    correction = precondition(residual)
    direction = correction
    image = operate(direction)
    curvature_sum = totals(direction, image)
    descent_sum = totals(residual, direction)
    for iteration in range(ITERS):
        step_size = descent_sum / curvature_sum
        solution = solution + spread(step_size) * direction
        residual = residual - spread(step_size) * image
        correction = precondition(residual)
        if iteration + 1 < ITERS:
            blend = -totals(correction, image) / curvature_sum
            direction = correction + spread(blend) * direction
            image = operate(direction)
            curvature_sum = totals(direction, image)
            descent_sum = totals(residual, direction)

    def to_global(fields):
        return fields.transpose(0, 2, 1, 3).reshape(GRID_ROWS * LOADS, GRID_COLS * M)

    return to_global(solution), to_global(residual), to_global(correction)
```

```python
import functools

import jax
import jax.numpy as jnp
from jax import lax
from jax.experimental import pallas as pl
from jax.experimental.pallas import tpu as pltpu
from jax.sharding import PartitionSpec as P

ITERS = 3
GRID = 16
LOADS = 8
NB = 16
TPR = 4
TILE = 128
M = 2048
DEFL = 32
FACE = 128
SLOTS = 4 * FACE
KROW = GRID * DEFL
MESH = pl.DeviceIdType.MESH
F32 = jnp.float32
BF16 = jnp.bfloat16


def dot_nn(a, b):
    return lax.dot_general(a, b, (((1,), (0,)), ((), ())), preferred_element_type=F32)


def dot_nt(a, b):
    return lax.dot_general(a, b, (((1,), (1,)), ((), ())), preferred_element_type=F32)


def parts(value):
    high = value.astype(BF16).astype(F32)
    return jnp.concatenate([high, value - high], axis=0).astype(BF16)


def fold(value):
    half = value.shape[0] // 2
    return value[:half] + value[half:]


def lane_ids(shape):
    return lax.broadcasted_iota(jnp.int32, shape, 1)


def row_ids(shape):
    return lax.broadcasted_iota(jnp.int32, shape, 0)


def kernel(
    rhs, flex, flex_cols, stiff, stiff_cols, defl, coarse, face_rows, face_len,
    x_ref, r_ref, z_ref,
    flex_f, stiff_f, defl_f, coarse_f, faces,
    flex_t, stiff_t, flex_s, stiff_s, defl_t, trace_t, coarse_h, coarse_l, pick,
    blocks_a, blocks_b, spread,
    p_ref, q_ref, w_ref, tr_r, tr_z, tr_p, tr_q, e_r, e_q, s1_ref,
    recv1, send2, recv2, halo_out, halo_in,
    load_sem, wsend, wrecv, send1_sem, recv1_sem, send2_sem, recv2_sem, hsend_sem, hrecv_sem,
):
    i = lax.axis_index("row")
    j = lax.axis_index("col")

    loads = [
        pltpu.make_async_copy(rhs, r_ref, load_sem.at[0]),
        pltpu.make_async_copy(defl, defl_f, load_sem.at[1]),
        pltpu.make_async_copy(face_rows, faces, load_sem.at[2]),
        pltpu.make_async_copy(flex, flex_f, load_sem.at[3]),
        pltpu.make_async_copy(stiff, stiff_f, load_sem.at[4]),
        pltpu.make_async_copy(
            coarse.at[:, pl.ds(pl.multiple_of(i * KROW, KROW), KROW)], coarse_f.at[i], load_sem.at[5]
        ),
    ]
    for load in loads:
        load.start()

    barrier = pltpu.get_barrier_semaphore()

    def greet(step, carry):
        pl.semaphore_signal(barrier, inc=1, device_id=((i + step) % GRID, j), device_id_type=MESH)
        pl.semaphore_signal(barrier, inc=1, device_id=(i, (j + step) % GRID), device_id_type=MESH)
        return carry

    lax.fori_loop(1, GRID, greet, 0)
    pl.semaphore_wait(barrier, 2 * (GRID - 1))

    def coarse_copy(there, slot):
        return pltpu.make_async_remote_copy(
            src_ref=coarse.at[:, pl.ds(pl.multiple_of(there * KROW, KROW), KROW)],
            dst_ref=coarse_f.at[slot],
            send_sem=wsend.at[there],
            recv_sem=wrecv.at[slot],
            device_id=(there, j),
            device_id_type=MESH,
        )

    def send_coarse(step, carry):
        coarse_copy((i + step) % GRID, i).start()
        return carry

    lax.fori_loop(1, GRID, send_coarse, 0)

    lane8 = lane_ids((LOADS, 128))

    def copy1(phase, there, slot):
        return pltpu.make_async_remote_copy(
            src_ref=recv1.at[phase, j],
            dst_ref=recv1.at[phase, slot],
            send_sem=send1_sem.at[there],
            recv_sem=recv1_sem.at[phase, slot],
            device_id=(i, there),
            device_id_type=MESH,
        )

    def copy2(phase, there, slot):
        return pltpu.make_async_remote_copy(
            src_ref=send2.at[there],
            dst_ref=recv2.at[phase, slot],
            send_sem=send2_sem.at[there],
            recv_sem=recv2_sem.at[phase, slot],
            device_id=(there, j),
            device_id_type=MESH,
        )

    def gather_start(phase, coefficients, sums):
        payload = jnp.where(lane8 < DEFL, coefficients, 0.0)
        for place, value in enumerate(sums):
            payload = jnp.where(lane8 == DEFL + place, value, payload)
        recv1[phase, j] = payload

        def go(step, carry):
            copy1(phase, (j + step) % GRID, j).start()
            return carry

        lax.fori_loop(1, GRID, go, 0)

    def gather_finish(phase, before_matmul=None):
        def take(step, carry):
            other = (j + step) % GRID
            copy1(phase, other, other).wait_recv()
            return carry

        lax.fori_loop(1, GRID, take, 0)
        total = jnp.zeros((LOADS, 128), F32)
        groups = []
        for group in range(4):
            gathered = None
            for place in range(4):
                payload = recv1[phase, group * 4 + place]
                total = total + payload
                moved = jnp.where(lane8 < DEFL, payload, 0.0)
                if place:
                    moved = pltpu.roll(moved, place * DEFL, 1)
                gathered = moved if gathered is None else gathered + moved
            groups.append(gathered)
        if before_matmul is not None:
            before_matmul()
        operand = parts(jnp.concatenate(groups, axis=1))
        partial = fold(dot_nt(operand, coarse_h[...]) + dot_nt(operand, coarse_l[...]))
        total = jnp.where((lane8 >= DEFL) & (lane8 < 2 * DEFL), total, 0.0)
        rolled = [total] + [pltpu.roll(total, place * DEFL, 1) for place in range(1, 4)]
        for target in range(GRID):
            tile = partial[:, (target // 4) * 128 : (target // 4 + 1) * 128]
            send2[target] = jnp.where(lane8 // DEFL == target % 4, tile, rolled[target % 4])

        def go(step, carry):
            copy2(phase, (i + step) % GRID, i).start()
            return carry

        lax.fori_loop(1, GRID, go, 0)
        recv2[phase, i] = send2[i]

        def settle(step, carry):
            other = (j + step) % GRID
            copy1(phase, other, other).wait_send()
            return carry

        lax.fori_loop(1, GRID, settle, 0)

        def take2(step, carry):
            other = (i + step) % GRID
            copy2(phase, other, other).wait_recv()
            return carry

        lax.fori_loop(1, GRID, take2, 0)
        result = recv2[phase, 0]
        for source in range(1, GRID):
            result = result + recv2[phase, source]
        turned = result
        for place in range(1, 4):
            turned = jnp.where(i % 4 == place, pltpu.roll(result, 128 - place * DEFL, 1), turned)

        def settle2(step, carry):
            other = (i + step) % GRID
            copy2(phase, other, other).wait_send()
            return carry

        lax.fori_loop(1, GRID, settle2, 0)
        return turned

    def coefficients_of(product):
        summed = fold(product)
        return summed + pltpu.roll(summed, 128 - DEFL, 1)

    loads[0].wait()
    loads[1].wait()
    defl_high = defl_f[...].astype(BF16)
    defl_low = (defl_f[...] - defl_high.astype(F32)).astype(BF16)
    defl_t[0:DEFL] = defl_high
    defl_t[DEFL : 2 * DEFL] = defl_low
    defl_t[2 * DEFL :] = jnp.zeros((128 - 2 * DEFL, M), BF16)
    start_parts = parts(r_ref[...])
    gather_start(0, coefficients_of(dot_nt(start_parts, defl_t[...])), ())

    loads[2].wait()

    def build_pick(block, carry):
        start = pl.multiple_of(block * TILE, TILE)
        rows = row_ids((TILE, FACE)) + start
        for face in range(4):
            hit = rows == faces[face : face + 1, :]
            pick[pl.ds(start, TILE), face * FACE : (face + 1) * FACE] = jnp.where(hit, 1.0, 0.0).astype(BF16)
        return carry

    lax.fori_loop(0, NB, build_pick, 0)
    both = dot_nn(jnp.concatenate([start_parts, defl_t[0 : 2 * DEFL]], axis=0), pick[...])
    tr_r[...] = both[0:LOADS] + both[LOADS : 2 * LOADS]
    trace_t[0 : 2 * DEFL] = parts(both[2 * LOADS : 2 * LOADS + DEFL] + both[2 * LOADS + DEFL :])
    trace_t[2 * DEFL :] = jnp.zeros((128 - 2 * DEFL, SLOTS), BF16)

    def build_spread(columns, target):
        lanes = lane_ids((LOADS, 128))
        rows = row_ids((NB * LOADS, 128))
        wide = lane_ids((NB * LOADS, 128))
        for tile in range(4):
            named = jnp.zeros((LOADS, 128), jnp.int32)
            for place in range(16):
                index = tile * 16 + place
                named = jnp.where(lanes // LOADS == place, columns[index // TPR, index % TPR], named)
            hit = (rows // LOADS == named[0:1, :]) & (rows % LOADS == wide % LOADS)
            target[:, tile * 128 : (tile + 1) * 128] = jnp.where(hit, 1.0, 0.0).astype(BF16)

    build_spread(flex_cols, flex_s)
    build_spread(stiff_cols, stiff_s)

    def convert(source, target):
        def one(block, carry):
            tiles = source[pl.ds(pl.multiple_of(block * TPR * TILE, TPR * TILE), TPR * TILE), :]
            high = tiles.astype(BF16)
            target[block, :, 0:TILE] = high
            target[block, :, TILE : 2 * TILE] = (tiles - high.astype(F32)).astype(BF16)
            return carry

        lax.fori_loop(0, NB, one, 0)

    loads[3].wait()
    convert(flex_f, flex_t)
    loads[4].wait()
    convert(stiff_f, stiff_t)

    def coarse_ready():
        loads[5].wait()

        def take(step, carry):
            other = (i + step) % GRID
            coarse_copy(other, other).wait_recv()
            return carry

        lax.fori_loop(1, GRID, take, 0)

        def one(block, carry):
            rows = coarse_f[block]
            high = rows.astype(BF16)
            start = pl.multiple_of(block * DEFL, DEFL)
            coarse_h[pl.ds(start, DEFL), :] = high
            coarse_l[pl.ds(start, DEFL), :] = (rows - high.astype(F32)).astype(BF16)
            return carry

        lax.fori_loop(0, GRID, one, 0)

    zeros = jnp.zeros((LOADS, M), F32)
    p_ref[...] = zeros
    q_ref[...] = zeros
    x_ref[...] = zeros
    tr_p[...] = jnp.zeros((LOADS, SLOTS), F32)
    tr_q[...] = jnp.zeros((LOADS, SLOTS), F32)
    e_q[...] = jnp.zeros((LOADS, 128), F32)
    s1_ref[...] = jnp.ones((LOADS, 128), F32)

    first = gather_finish(0, coarse_ready)
    e_r[...] = jnp.where(lane8 < DEFL, first, 0.0)

    def settle_coarse(step, carry):
        other = (i + step) % GRID
        coarse_copy(other, other).wait_send()
        return carry

    lax.fori_loop(1, GRID, settle_coarse, 0)

    def energy_parts():
        energy = e_r[...]
        return parts(energy + pltpu.roll(energy, DEFL, 1))[:, 0 : 2 * DEFL]

    def face_copy(step, face, device, slot):
        return pltpu.make_async_remote_copy(
            src_ref=halo_out.at[face],
            dst_ref=halo_in.at[step, slot],
            send_sem=hsend_sem.at[face],
            recv_sem=hrecv_sem.at[step, slot],
            device_id=device,
            device_id_type=MESH,
        )

    sides = (
        (i > 0, (i - 1, j), 1),
        (i < GRID - 1, (i + 1, j), 0),
        (j > 0, (i, j - 1), 3),
        (j < GRID - 1, (i, j + 1), 2),
    )

    def store_blocks(target, block, value):
        target[block] = parts(value)

    def forward(source, tiles, columns, target):
        for block in range(NB):
            operand = jnp.concatenate([source[columns[block, k]] for k in range(TPR)], axis=1)
            product = fold(dot_nn(operand, tiles[block]))
            store_blocks(target, block, product[:, 0:TILE] + product[:, TILE : 2 * TILE])

    def backward(source, tiles, selector):
        for block in range(NB):
            piece = source[block]
            product = fold(dot_nt(jnp.concatenate([piece, piece], axis=1), tiles[block]))
            stacked = jnp.concatenate(
                [product[:, k * TILE : (k + 1) * TILE] for k in range(TPR)], axis=0
            )
            high = stacked.astype(BF16)
            rows = slice(block * TPR * LOADS, (block + 1) * TPR * LOADS)
            spread[rows, 0:TILE] = high
            spread[rows, TILE : 2 * TILE] = (stacked - high.astype(F32)).astype(BF16)
        summed = dot_nn(selector[...], spread[...])
        return summed[:, 0:TILE] + summed[:, TILE : 2 * TILE]

    def correct(energy):
        z_ref[...] = r_ref[...] + fold(dot_nn(energy, defl_t[0 : 2 * DEFL]))

    live = jnp.concatenate(
        [jnp.where(lane8 < face_len[0, face], 1.0, 0.0) for face in range(4)], axis=1
    )

    def iterate(step, carry):
        energy = energy_parts()
        traces = tr_r[...] + fold(dot_nn(energy, trace_t[0 : 2 * DEFL]))
        tr_z[...] = traces
        for face in range(4):
            halo_out[face] = traces[:, face * FACE : (face + 1) * FACE]
        for face, (inside, device, slot) in enumerate(sides):

            @pl.when(inside)
            def _():
                face_copy(step, face, device, slot).start()

        correct(energy)
        z = z_ref[...]
        for block in range(NB):
            store_blocks(blocks_a, block, z[:, block * TILE : (block + 1) * TILE])
        forward(blocks_a, flex_t, flex_cols, blocks_b)
        forward(blocks_b, stiff_t, stiff_cols, blocks_a)
        middle = backward(blocks_a, stiff_t, stiff_s)
        for block in range(NB):
            store_blocks(blocks_b, block, middle[block * LOADS : (block + 1) * LOADS])
        local = backward(blocks_b, flex_t, flex_s)
        local = jnp.concatenate(
            [local[block * LOADS : (block + 1) * LOADS] for block in range(NB)], axis=1
        )
        u = z_ref[...] + local
        w_ref[...] = u
        z = z_ref[...]
        p = p_ref[...]
        r = r_ref[...]
        sum_zu = jnp.sum(z * u, axis=1, keepdims=True)
        sum_pu = jnp.sum(p * u, axis=1, keepdims=True)
        sum_rz = jnp.sum(r * z, axis=1, keepdims=True)
        sum_rp = jnp.sum(r * p, axis=1, keepdims=True)
        sum_zq = jnp.sum(z * q_ref[...], axis=1, keepdims=True)
        product = dot_nt(parts(u), defl_t[...])

        for face, (inside, device, slot) in enumerate(sides):

            @pl.when(inside)
            def _():
                face_copy(step, slot, device, face).wait_recv()

        partner = jnp.concatenate([halo_in[step, face] for face in range(4)], axis=1)
        jump = jnp.where(live > 0.5, tr_z[...] - partner, 0.0)
        jump_parts = parts(jump)
        product = product + dot_nt(jump_parts, trace_t[...])
        sum_zw = sum_zu + jnp.sum(tr_z[...] * jump, axis=1, keepdims=True)
        sum_pw = sum_pu + jnp.sum(tr_p[...] * jump, axis=1, keepdims=True)
        gather_start(step + 1, coefficients_of(product), (sum_zw, sum_pw, sum_rz, sum_rp, sum_zq))

        w = w_ref[...] + fold(dot_nt(jump_parts, pick[...]))
        w_ref[...] = w
        traced = fold(dot_nn(parts(w), pick[...]))
        for face, (inside, device, slot) in enumerate(sides):

            @pl.when(inside)
            def _():
                face_copy(step, face, device, slot).wait_send()

        gathered = gather_finish(step + 1)

        def total(place):
            return gathered[:, DEFL + place : DEFL + place + 1]

        beta = -total(4) / s1_ref[:, 0:1]
        curvature = total(0) + beta * total(1)
        alpha = (total(2) + beta * total(3)) / curvature
        s1_ref[...] = jnp.broadcast_to(curvature, (LOADS, 128))
        energy_q = jnp.where(lane8 < DEFL, gathered, 0.0) + beta * e_q[...]
        e_q[...] = energy_q
        e_r[...] = e_r[...] - alpha * energy_q
        trace_q = traced + beta * tr_q[...]
        tr_q[...] = trace_q
        tr_p[...] = tr_z[...] + beta * tr_p[...]
        tr_r[...] = tr_r[...] - alpha * trace_q
        direction = z_ref[...] + beta * p_ref[...]
        image = w_ref[...] + beta * q_ref[...]
        p_ref[...] = direction
        q_ref[...] = image
        x_ref[...] = x_ref[...] + alpha * direction
        r_ref[...] = r_ref[...] - alpha * image
        return carry

    lax.fori_loop(0, ITERS, iterate, 0)
    correct(energy_parts())


def shards(*args):
    anywhere = pl.BlockSpec(memory_space=pl.ANY)
    scalars = pl.BlockSpec(memory_space=pltpu.SMEM)
    vector = pl.BlockSpec(memory_space=pltpu.VMEM)
    field = jax.ShapeDtypeStruct((LOADS, M), F32)
    vmem = pltpu.VMEM
    dma = pltpu.SemaphoreType.DMA
    return pl.pallas_call(
        kernel,
        out_shape=(field, field, field),
        in_specs=[
            anywhere, anywhere, scalars, anywhere, scalars, anywhere, anywhere, anywhere, scalars,
        ],
        out_specs=(vector, vector, vector),
        scratch_shapes=[
            vmem((NB * TPR * TILE, TILE), F32),
            vmem((NB * TPR * TILE, TILE), F32),
            vmem((DEFL, M), F32),
            vmem((GRID, DEFL, KROW), F32),
            vmem((4, FACE), jnp.int32),
            vmem((NB, TPR * TILE, 2 * TILE), BF16),
            vmem((NB, TPR * TILE, 2 * TILE), BF16),
            vmem((NB * LOADS, NB * TPR * LOADS), BF16),
            vmem((NB * LOADS, NB * TPR * LOADS), BF16),
            vmem((128, M), BF16),
            vmem((128, SLOTS), BF16),
            vmem((KROW, KROW), BF16),
            vmem((KROW, KROW), BF16),
            vmem((M, SLOTS), BF16),
            vmem((NB, 2 * LOADS, TILE), BF16),
            vmem((NB, 2 * LOADS, TILE), BF16),
            vmem((NB * TPR * LOADS, 2 * TILE), BF16),
            vmem((LOADS, M), F32),
            vmem((LOADS, M), F32),
            vmem((LOADS, M), F32),
            vmem((LOADS, SLOTS), F32),
            vmem((LOADS, SLOTS), F32),
            vmem((LOADS, SLOTS), F32),
            vmem((LOADS, SLOTS), F32),
            vmem((LOADS, 128), F32),
            vmem((LOADS, 128), F32),
            vmem((LOADS, 128), F32),
            vmem((ITERS + 1, GRID, LOADS, 128), F32),
            vmem((GRID, LOADS, 128), F32),
            vmem((ITERS + 1, GRID, LOADS, 128), F32),
            vmem((4, LOADS, FACE), F32),
            vmem((ITERS, 4, LOADS, FACE), F32),
            dma((6,)),
            dma((GRID,)),
            dma((GRID,)),
            dma((GRID,)),
            dma((ITERS + 1, GRID)),
            dma((GRID,)),
            dma((ITERS + 1, GRID)),
            dma((4,)),
            dma((ITERS, 4)),
        ],
        compiler_params=pltpu.CompilerParams(
            collective_id=0, has_side_effects=True, vmem_limit_bytes=56 * 1024 * 1024
        ),
        name="feti",
    )(*args)


def solution(mesh):
    return jax.shard_map(
        shards,
        mesh=mesh,
        in_specs=(
            P("row", "col"),
            P("row", "col"),
            P("row", "col"),
            P("row", "col"),
            P("row", "col"),
            P("row", "col"),
            P(("row", "col"), None),
            P("row", "col"),
            P("row", "col"),
        ),
        out_specs=(P("row", "col"), P("row", "col"), P("row", "col")),
        check_vma=False,
    )
```

```python
import functools

import jax
import jax.numpy as jnp
from jax import lax
from jax.experimental import pallas as pl
from jax.experimental.pallas import tpu as pltpu
from jax.sharding import PartitionSpec as P

ITERS = 3
GRID = 16
LOADS = 8
NB = 16
TPR = 4
TILE = 128
M = 2048
DEFL = 32
FACE = 128
SLOTS = 4 * FACE
KROW = GRID * DEFL
MESH = pl.DeviceIdType.MESH
F32 = jnp.float32
BF16 = jnp.bfloat16


def dot_nn(a, b):
    return lax.dot_general(a, b, (((1,), (0,)), ((), ())), preferred_element_type=F32)


def dot_nt(a, b):
    return lax.dot_general(a, b, (((1,), (1,)), ((), ())), preferred_element_type=F32)


def parts(value):
    high = value.astype(BF16).astype(F32)
    return jnp.concatenate([high, value - high], axis=0).astype(BF16)


def fold(value):
    half = value.shape[0] // 2
    return value[:half] + value[half:]


def lane_ids(shape):
    return lax.broadcasted_iota(jnp.int32, shape, 1)


def row_ids(shape):
    return lax.broadcasted_iota(jnp.int32, shape, 0)


def kernel(
    rhs, flex, flex_cols, stiff, stiff_cols, defl, coarse, face_rows, face_len,
    x_ref, r_ref, z_ref,
    flex_f, stiff_f, defl_f, coarse_f, faces,
    flex_t, stiff_t, flex_s, stiff_s, defl_t, image_t, trace_t, coarse_h, coarse_l, pick,
    wide_a, wide_b, wide_spread, blocks_a, blocks_b, spread,
    a_ref, b_ref, bw_ref, p_ref, q_ref, w_ref, tr_r, tr_z, tr_w, tr_p, tr_q,
    e_r, e_q, s1_ref, alpha_ref, beta_ref,
    recv1, send2, recv2, halo_out, halo_in,
    load_sem, wsend, wrecv, send1_sem, recv1_sem, send2_sem, recv2_sem, hsend_sem, hrecv_sem,
):
    i = lax.axis_index("row")
    j = lax.axis_index("col")
    chunk = NB * TPR * TILE // 4

    def part_of(ref, index):
        return ref.at[pl.ds(index * chunk, chunk), :]

    load_r = pltpu.make_async_copy(rhs, r_ref, load_sem.at[0])
    load_z = pltpu.make_async_copy(defl, defl_f, load_sem.at[1])
    load_faces = pltpu.make_async_copy(face_rows, faces, load_sem.at[2])
    load_coarse = pltpu.make_async_copy(
        coarse.at[:, pl.ds(pl.multiple_of(i * KROW, KROW), KROW)], coarse_f.at[i], load_sem.at[3]
    )
    load_flex = [
        pltpu.make_async_copy(part_of(flex, n), part_of(flex_f, n), load_sem.at[4 + n]) for n in range(4)
    ]
    load_stiff = [
        pltpu.make_async_copy(part_of(stiff, n), part_of(stiff_f, n), load_sem.at[8 + n]) for n in range(4)
    ]
    for load in [load_r, load_z, load_faces] + load_flex + load_stiff + [load_coarse]:
        load.start()

    row_partners = []
    for dy, dx in sorted(
        [(dy, dx) for dy in range(4) for dx in range(4) if dy or dx],
        key=lambda pair: -(min(pair[0], 4 - pair[0]) + min(pair[1], 4 - pair[1])),
    ):
        row_partners.append(((i // 4 + dy) % 4) * 4 + (i % 4 + dx) % 4)
    col_partners = [
        (j + offset) % GRID for offset in sorted(range(1, GRID), key=lambda o: -min(o, GRID - o))
    ]

    barrier = pltpu.get_barrier_semaphore()
    for there in row_partners:
        pl.semaphore_signal(barrier, inc=1, device_id=(there, j), device_id_type=MESH)
    for there in col_partners:
        pl.semaphore_signal(barrier, inc=1, device_id=(i, there), device_id_type=MESH)
    pl.semaphore_wait(barrier, 2 * (GRID - 1))

    def coarse_copy(there, slot):
        return pltpu.make_async_remote_copy(
            src_ref=coarse.at[:, pl.ds(pl.multiple_of(there * KROW, KROW), KROW)],
            dst_ref=coarse_f.at[slot],
            send_sem=wsend,
            recv_sem=wrecv,
            device_id=(there, j),
            device_id_type=MESH,
        )

    for there in row_partners:
        coarse_copy(there, i).start()

    lane8 = lane_ids((LOADS, 128))

    def copy1(phase, there):
        return pltpu.make_async_remote_copy(
            src_ref=recv1.at[phase, j],
            dst_ref=recv1.at[phase, j],
            send_sem=send1_sem,
            recv_sem=recv1_sem.at[phase],
            device_id=(i, there),
            device_id_type=MESH,
        )

    def copy2(phase, there):
        return pltpu.make_async_remote_copy(
            src_ref=send2.at[there],
            dst_ref=recv2.at[phase, i],
            send_sem=send2_sem,
            recv_sem=recv2_sem.at[phase],
            device_id=(there, j),
            device_id_type=MESH,
        )

    def whole1(phase):
        slots = recv1.at[phase, pl.ds(0, GRID - 1)]
        return pltpu.make_async_remote_copy(
            src_ref=slots,
            dst_ref=slots,
            send_sem=send1_sem,
            recv_sem=recv1_sem.at[phase],
            device_id=(i, j),
            device_id_type=MESH,
        )

    def whole2(phase):
        return pltpu.make_async_remote_copy(
            src_ref=send2.at[pl.ds(0, GRID - 1)],
            dst_ref=recv2.at[phase, pl.ds(0, GRID - 1)],
            send_sem=send2_sem,
            recv_sem=recv2_sem.at[phase],
            device_id=(i, j),
            device_id_type=MESH,
        )

    def whole_coarse():
        slots = coarse_f.at[pl.ds(0, GRID - 1)]
        return pltpu.make_async_remote_copy(
            src_ref=slots,
            dst_ref=slots,
            send_sem=wsend,
            recv_sem=wrecv,
            device_id=(i, j),
            device_id_type=MESH,
        )

    def gather_start(phase, coefficients, sums):
        payload = jnp.where(lane8 < DEFL, coefficients, 0.0)
        for place, value in enumerate(sums):
            payload = jnp.where(lane8 == DEFL + place, value, payload)
        recv1[phase, j] = payload
        for there in col_partners:
            copy1(phase, there).start()

    def gather_middle(phase, before_matmul=None):
        whole1(phase).wait_recv()
        total = jnp.zeros((LOADS, 128), F32)
        groups = []
        for group in range(4):
            gathered = None
            for place in range(4):
                payload = recv1[phase, group * 4 + place]
                total = total + payload
                moved = jnp.where(lane8 < DEFL, payload, 0.0)
                if place:
                    moved = pltpu.roll(moved, place * DEFL, 1)
                gathered = moved if gathered is None else gathered + moved
            groups.append(gathered)
        if before_matmul is not None:
            before_matmul()
        operand = parts(jnp.concatenate(groups, axis=1))
        partial = fold(dot_nt(operand, coarse_h[...]) + dot_nt(operand, coarse_l[...]))
        total = jnp.where((lane8 >= DEFL) & (lane8 < 2 * DEFL), total, 0.0)
        rolled = [total] + [pltpu.roll(total, place * DEFL, 1) for place in range(1, 4)]
        for target in range(GRID):
            tile = partial[:, (target // 4) * 128 : (target // 4 + 1) * 128]
            send2[target] = jnp.where(lane8 // DEFL == target % 4, tile, rolled[target % 4])
        for there in row_partners:
            copy2(phase, there).start()
        recv2[phase, i] = send2[i]

    def gather_end(phase):
        whole2(phase).wait_recv()
        level = [recv2[phase, source] for source in range(GRID)]
        while len(level) > 1:
            level = [level[n] + level[n + 1] for n in range(0, len(level), 2)]
        result = level[0]
        turned = result
        for place in range(1, 4):
            turned = jnp.where(i % 4 == place, pltpu.roll(result, 128 - place * DEFL, 1), turned)
        whole1(phase).wait_send()
        whole2(phase).wait_send()
        return turned

    def coefficients_of(product):
        summed = fold(product)
        return summed + pltpu.roll(summed, 128 - DEFL, 1)

    load_r.wait()
    load_z.wait()
    defl_high = defl_f[...].astype(BF16)
    defl_low = (defl_f[...] - defl_high.astype(F32)).astype(BF16)
    defl_t[0:DEFL] = defl_high
    defl_t[DEFL : 2 * DEFL] = defl_low
    defl_t[2 * DEFL :] = jnp.zeros((128 - 2 * DEFL, M), BF16)
    gather_start(0, coefficients_of(dot_nt(parts(r_ref[...]), defl_t[...])), ())

    load_faces.wait()

    def build_pick(block, carry):
        start = pl.multiple_of(block * TILE, TILE)
        rows = row_ids((TILE, FACE)) + start
        for face in range(4):
            hit = rows == faces[face : face + 1, :]
            pick[pl.ds(start, TILE), face * FACE : (face + 1) * FACE] = jnp.where(hit, 1.0, 0.0).astype(BF16)
        return carry

    lax.fori_loop(0, NB, build_pick, 0)
    wide = LOADS + DEFL
    basis = parts(jnp.concatenate([r_ref[...], defl_f[...]], axis=0))
    for block in range(NB):
        wide_a[block] = basis[:, block * TILE : (block + 1) * TILE]
    both = fold(dot_nn(basis, pick[...]))
    tr_r[...] = both[0:LOADS]
    trace_t[0 : 2 * DEFL] = parts(both[LOADS:])
    trace_t[2 * DEFL :] = jnp.zeros((128 - 2 * DEFL, SLOTS), BF16)

    def build_spread(columns, target):
        lanes = lane_ids((LOADS, 128))
        rows = row_ids((NB * LOADS, 128))
        across = lane_ids((NB * LOADS, 128))
        for tile in range(4):
            named = jnp.zeros((LOADS, 128), jnp.int32)
            for place in range(16):
                index = tile * 16 + place
                named = jnp.where(lanes // LOADS == place, columns[index % TPR, index // TPR], named)
            hit = (rows // LOADS == named[0:1, :]) & (rows % LOADS == across % LOADS)
            target[:, tile * 128 : (tile + 1) * 128] = jnp.where(hit, 1.0, 0.0).astype(BF16)

    build_spread(flex_cols, flex_s)
    build_spread(stiff_cols, stiff_s)

    def convert(pending, source, target):
        for n, load in enumerate(pending):
            load.wait()

            def one(block, carry):
                tiles = source[pl.ds(pl.multiple_of(block * TPR * TILE, TPR * TILE), TPR * TILE), :]
                high = tiles.astype(BF16)
                target[block, :, 0:TILE] = high
                target[block, :, TILE : 2 * TILE] = (tiles - high.astype(F32)).astype(BF16)
                return carry

            lax.fori_loop(n * NB // 4, (n + 1) * NB // 4, one, 0)

    convert(load_flex, flex_f, flex_t)
    convert(load_stiff, stiff_f, stiff_t)

    def coarse_ready():
        load_coarse.wait()
        whole_coarse().wait_recv()

        def one(block, carry):
            rows = coarse_f[block]
            high = rows.astype(BF16)
            start = pl.multiple_of(block * DEFL, DEFL)
            coarse_h[pl.ds(start, DEFL), :] = high
            coarse_l[pl.ds(start, DEFL), :] = (rows - high.astype(F32)).astype(BF16)
            return carry

        lax.fori_loop(0, GRID, one, 0)

    def forward(source, tiles, columns, target):
        for block in range(NB):
            operand = jnp.concatenate([source[columns[k, block]] for k in range(TPR)], axis=1)
            product = fold(dot_nn(operand, tiles[block]))
            target[block] = parts(product[:, 0:TILE] + product[:, TILE : 2 * TILE])

    def backward(source, tiles, selector, space):
        groups = space.shape[0]
        for block in range(NB):
            piece = source[block]
            product = fold(dot_nt(jnp.concatenate([piece, piece], axis=1), tiles[block]))
            rows = slice(block * TPR * LOADS, (block + 1) * TPR * LOADS)
            for group in range(groups):
                loads = product[group * LOADS : (group + 1) * LOADS]
                stacked = jnp.concatenate(
                    [loads[:, k * TILE : (k + 1) * TILE] for k in range(TPR)], axis=0
                )
                high = stacked.astype(BF16)
                space[group, rows, 0:TILE] = high
                space[group, rows, TILE : 2 * TILE] = (stacked - high.astype(F32)).astype(BF16)
        summed = []
        for group in range(groups):
            product = dot_nn(selector[...], space[group])
            summed.append(product[:, 0:TILE] + product[:, TILE : 2 * TILE])
        return [
            jnp.concatenate([one[block * LOADS : (block + 1) * LOADS] for one in summed], axis=0)
            for block in range(NB)
        ]

    forward(wide_a, flex_t, flex_cols, wide_b)
    forward(wide_b, stiff_t, stiff_cols, wide_a)
    gather_middle(0, coarse_ready)
    middle = backward(wide_a, stiff_t, stiff_s, wide_spread)
    for block in range(NB):
        wide_b[block] = parts(middle[block])
    applied = backward(wide_b, flex_t, flex_s, wide_spread)
    for block in range(NB):
        cut = slice(block * TILE, (block + 1) * TILE)
        a_ref[:, cut] = r_ref[:, cut] + applied[block][0:LOADS]
        image_t[:, cut] = parts(defl_f[:, cut] + applied[block][LOADS:wide])

    zeros = jnp.zeros((LOADS, M), F32)
    for ref in (b_ref, bw_ref, p_ref, q_ref, w_ref, x_ref, z_ref):
        ref[...] = zeros
    tr_p[...] = jnp.zeros((LOADS, SLOTS), F32)
    tr_q[...] = jnp.zeros((LOADS, SLOTS), F32)
    tr_z[...] = jnp.zeros((LOADS, SLOTS), F32)
    e_q[...] = jnp.zeros((LOADS, 128), F32)
    s1_ref[...] = jnp.ones((LOADS, 128), F32)
    alpha_ref[...] = jnp.zeros((LOADS, 128), F32)
    beta_ref[...] = jnp.zeros((LOADS, 128), F32)

    e_r[...] = jnp.where(lane8 < DEFL, gather_end(0), 0.0)
    whole_coarse().wait_send()

    def energy_parts():
        energy = e_r[...]
        return parts(energy + pltpu.roll(energy, DEFL, 1))[:, 0 : 2 * DEFL]

    def face_copy(step, face, device, slot):
        return pltpu.make_async_remote_copy(
            src_ref=halo_out.at[face],
            dst_ref=halo_in.at[step, slot],
            send_sem=hsend_sem.at[face],
            recv_sem=hrecv_sem.at[step, slot],
            device_id=device,
            device_id_type=MESH,
        )

    sides = (
        (i > 0, (i - 1, j), 1),
        (i < GRID - 1, (i + 1, j), 0),
        (j > 0, (i, j - 1), 3),
        (j < GRID - 1, (i, j + 1), 2),
    )

    live = jnp.concatenate(
        [jnp.where(lane8 < face_len[0, face], 1.0, 0.0) for face in range(4)], axis=1
    )

    def advance():
        alpha = alpha_ref[:, 0:1]
        beta = beta_ref[:, 0:1]
        direction = z_ref[...] + beta * p_ref[...]
        image = w_ref[...] + beta * q_ref[...]
        p_ref[...] = direction
        q_ref[...] = image
        x_ref[...] = x_ref[...] + alpha * direction
        residual = r_ref[...] - alpha * image
        r_ref[...] = residual
        return alpha, beta, direction, image, residual

    def row_sum(value):
        return jnp.sum(value, axis=1, keepdims=True)

    def iterate(step, carry):
        energy = energy_parts()
        old_traces = tr_z[...]
        traces = tr_r[...] + fold(dot_nn(energy, trace_t[0 : 2 * DEFL]))
        tr_z[...] = traces
        for face in range(4):
            halo_out[face] = traces[:, face * FACE : (face + 1) * FACE]
        for face, (inside, device, slot) in enumerate(sides):

            @pl.when(inside)
            def _():
                face_copy(step, face, device, slot).start()

        alpha, beta, p, q, r = advance()
        tr_p[...] = old_traces + beta * tr_p[...]
        applied = bw_ref[...] + beta * b_ref[...]
        b_ref[...] = applied
        a = a_ref[...] - alpha * applied
        a_ref[...] = a
        z = r + fold(dot_nn(energy, defl_t[0 : 2 * DEFL]))
        z_ref[...] = z
        u = a + fold(dot_nn(energy, image_t[...]))
        w_ref[...] = u
        product = dot_nt(parts(u), defl_t[...])
        sum_zu = row_sum(z * u)
        sum_pu = row_sum(p * u)
        sum_rz = row_sum(r * z)
        sum_rp = row_sum(r * p)
        sum_zq = row_sum(z * q)

        for face, (inside, device, slot) in enumerate(sides):

            @pl.when(inside)
            def _():
                face_copy(step, slot, device, face).wait_recv()

        partner = jnp.concatenate([halo_in[step, face] for face in range(4)], axis=1)
        jump = jnp.where(live > 0.5, tr_z[...] - partner, 0.0)
        jump_parts = parts(jump)
        product = product + dot_nt(jump_parts, trace_t[...])
        sum_zw = sum_zu + row_sum(tr_z[...] * jump)
        sum_pw = sum_pu + row_sum(tr_p[...] * jump)
        gather_start(step + 1, coefficients_of(product), (sum_zw, sum_pw, sum_rz, sum_rp, sum_zq))

        w = w_ref[...] + fold(dot_nt(jump_parts, pick[...]))
        w_ref[...] = w
        split = parts(w)
        for block in range(NB):
            blocks_a[block] = split[:, block * TILE : (block + 1) * TILE]
        for face, (inside, device, slot) in enumerate(sides):

            @pl.when(inside)
            def _():
                face_copy(step, face, device, slot).wait_send()

        @pl.when(step < ITERS - 1)
        def _():
            tr_w[...] = fold(dot_nn(split, pick[...]))
            forward(blocks_a, flex_t, flex_cols, blocks_b)

        gather_middle(step + 1)

        @pl.when(step < ITERS - 1)
        def _():
            forward(blocks_b, stiff_t, stiff_cols, blocks_a)
            middle = backward(blocks_a, stiff_t, stiff_s, spread)
            for block in range(NB):
                blocks_b[block] = parts(middle[block])
            local = backward(blocks_b, flex_t, flex_s, spread)
            bw_ref[...] = w_ref[...] + jnp.concatenate(local, axis=1)

        gathered = gather_end(step + 1)

        def total(place):
            return gathered[:, DEFL + place : DEFL + place + 1]

        new_beta = -total(4) / s1_ref[:, 0:1]
        curvature = total(0) + new_beta * total(1)
        new_alpha = (total(2) + new_beta * total(3)) / curvature
        s1_ref[...] = jnp.broadcast_to(curvature, (LOADS, 128))
        alpha_ref[...] = jnp.broadcast_to(new_alpha, (LOADS, 128))
        beta_ref[...] = jnp.broadcast_to(new_beta, (LOADS, 128))
        energy_q = jnp.where(lane8 < DEFL, gathered, 0.0) + new_beta * e_q[...]
        e_q[...] = energy_q
        e_r[...] = e_r[...] - new_alpha * energy_q
        trace_q = tr_w[...] + new_beta * tr_q[...]
        tr_q[...] = trace_q
        tr_r[...] = tr_r[...] - new_alpha * trace_q
        return carry

    tr_w[...] = jnp.zeros((LOADS, SLOTS), F32)
    lax.fori_loop(0, ITERS, iterate, 0)
    advance()
    z_ref[...] = r_ref[...] + fold(dot_nn(energy_parts(), defl_t[0 : 2 * DEFL]))


def publish(x_in, r_in, z_in, x_out, r_out, z_out):
    x_out[...] = x_in[...]
    r_out[...] = r_in[...]
    z_out[...] = z_in[...]


def shards(rhs, flex, flex_cols, stiff, stiff_cols, defl, coarse, face_rows, face_len):
    anywhere = pl.BlockSpec(memory_space=pl.ANY)
    scalars = pl.BlockSpec(memory_space=pltpu.SMEM)
    vector = pl.BlockSpec(memory_space=pltpu.VMEM)
    field = jax.ShapeDtypeStruct((LOADS, M), F32)
    vmem = pltpu.VMEM
    dma = pltpu.SemaphoreType.DMA
    wide = 2 * (LOADS + DEFL)
    found = pl.pallas_call(
        kernel,
        out_shape=(field, field, field),
        in_specs=[
            anywhere, anywhere, scalars, anywhere, scalars, anywhere, anywhere, anywhere, scalars,
        ],
        out_specs=(vector, vector, vector),
        scratch_shapes=[
            vmem((NB * TPR * TILE, TILE), F32),
            vmem((NB * TPR * TILE, TILE), F32),
            vmem((DEFL, M), F32),
            vmem((GRID, DEFL, KROW), F32),
            vmem((4, FACE), jnp.int32),
            vmem((NB, TPR * TILE, 2 * TILE), BF16),
            vmem((NB, TPR * TILE, 2 * TILE), BF16),
            vmem((NB * LOADS, NB * TPR * LOADS), BF16),
            vmem((NB * LOADS, NB * TPR * LOADS), BF16),
            vmem((128, M), BF16),
            vmem((2 * DEFL, M), BF16),
            vmem((128, SLOTS), BF16),
            vmem((KROW, KROW), BF16),
            vmem((KROW, KROW), BF16),
            vmem((M, SLOTS), BF16),
            vmem((NB, wide, TILE), BF16),
            vmem((NB, wide, TILE), BF16),
            vmem((wide // 16, NB * TPR * LOADS, 2 * TILE), BF16),
            vmem((NB, 2 * LOADS, TILE), BF16),
            vmem((NB, 2 * LOADS, TILE), BF16),
            vmem((1, NB * TPR * LOADS, 2 * TILE), BF16),
            *[vmem((LOADS, M), F32)] * 6,
            *[vmem((LOADS, SLOTS), F32)] * 5,
            *[vmem((LOADS, 128), F32)] * 5,
            vmem((ITERS + 1, GRID, LOADS, 128), F32),
            vmem((GRID, LOADS, 128), F32),
            vmem((ITERS + 1, GRID, LOADS, 128), F32),
            vmem((4, LOADS, FACE), F32),
            vmem((ITERS, 4, LOADS, FACE), F32),
            dma((12,)),
            dma,
            dma,
            dma,
            dma((ITERS + 1,)),
            dma,
            dma((ITERS + 1,)),
            dma((4,)),
            dma((ITERS, 4)),
        ],
        compiler_params=pltpu.CompilerParams(
            collective_id=0, has_side_effects=True, vmem_limit_bytes=66_500_000
        ),
        name="feti",
    )(rhs, flex, flex_cols.T, stiff, stiff_cols.T, defl, coarse, face_rows, face_len)
    return pl.pallas_call(
        publish,
        out_shape=(field, field, field),
        in_specs=[vector, vector, vector],
        out_specs=(vector, vector, vector),
        compiler_params=pltpu.CompilerParams(vmem_limit_bytes=66_500_000),
        name="publish",
    )(*found)


def solution(mesh):
    return jax.shard_map(
        shards,
        mesh=mesh,
        in_specs=(
            P("row", "col"),
            P("row", "col"),
            P("row", "col"),
            P("row", "col"),
            P("row", "col"),
            P("row", "col"),
            P(("row", "col"), None),
            P("row", "col"),
            P("row", "col"),
        ),
        out_specs=(P("row", "col"), P("row", "col"), P("row", "col")),
        check_vma=False,
    )
```

```python
import functools

import jax
import jax.numpy as jnp
from jax import lax
from jax.experimental import pallas as pl
from jax.experimental.pallas import tpu as pltpu
from jax.sharding import PartitionSpec as P

ITERS = 3
GRID = 16
LOADS = 8
NB = 16
TPR = 4
TILE = 128
M = 2048
DEFL = 32
FACE = 128
SLOTS = 4 * FACE
KROW = GRID * DEFL
MESH = pl.DeviceIdType.MESH
F32 = jnp.float32
BF16 = jnp.bfloat16


def dot_nn(a, b):
    return lax.dot_general(a, b, (((1,), (0,)), ((), ())), preferred_element_type=F32)


def dot_nt(a, b):
    return lax.dot_general(a, b, (((1,), (1,)), ((), ())), preferred_element_type=F32)


def parts(value):
    high = value.astype(BF16).astype(F32)
    return jnp.concatenate([high, value - high], axis=0).astype(BF16)


def fold(value):
    half = value.shape[0] // 2
    return value[:half] + value[half:]


def lane_ids(shape):
    return lax.broadcasted_iota(jnp.int32, shape, 1)


def row_ids(shape):
    return lax.broadcasted_iota(jnp.int32, shape, 0)


def row_sum(value):
    return jnp.sum(value, axis=1, keepdims=True)


def turn(value, place):
    moved = value
    for groups in range(1, 4):
        moved = jnp.where(place == groups, pltpu.roll(value, groups * DEFL, 1), moved)
    return moved


def kernel(
    rhs, flex, flex_cols, stiff, stiff_cols, defl, coarse, face_rows, face_len,
    x_ref, r_ref, z_ref,
    flex_f, stiff_f, defl_f, coarse_f, faces,
    flex_t, stiff_t, flex_s, stiff_s, defl_t, image_t, trace_t, coarse_h, coarse_l, pick, couple_t,
    wide_a, wide_b, wide_spread, blocks_a, blocks_b, spread,
    a_ref, b_ref, bw_ref, p_ref, q_ref, w_ref, tr_r, tr_w, tr_q, jump_r, jump_w, jump_q,
    e_r, e_q, s1_ref, alpha_ref, beta_ref, gr_ref, gq_ref, gw_ref, own_ref, c_ref, cq_ref,
    row_g, recv1, send2, recv2, first_out, first_in, halo_out, halo_in,
    load_sem, wsend, wrecv, send1_sem, recv1_sem, send2_sem, recv2_sem, fsend_sem, frecv_sem,
    hsend_sem, hrecv_sem,
):
    i = lax.axis_index("row")
    j = lax.axis_index("col")
    place = j % 4
    chunk = NB * TPR * TILE // 4

    def part_of(ref, index):
        return ref.at[pl.ds(index * chunk, chunk), :]

    load_r = pltpu.make_async_copy(rhs, r_ref, load_sem.at[0])
    load_z = pltpu.make_async_copy(defl, defl_f, load_sem.at[1])
    load_faces = pltpu.make_async_copy(face_rows, faces, load_sem.at[2])
    load_coarse = pltpu.make_async_copy(
        coarse.at[:, pl.ds(pl.multiple_of(i * KROW, KROW), KROW)], coarse_f.at[i], load_sem.at[3]
    )
    load_flex = [
        pltpu.make_async_copy(part_of(flex, n), part_of(flex_f, n), load_sem.at[4 + n]) for n in range(4)
    ]
    load_stiff = [
        pltpu.make_async_copy(part_of(stiff, n), part_of(stiff_f, n), load_sem.at[8 + n]) for n in range(4)
    ]

    row_partners = []
    for dy, dx in sorted(
        [(dy, dx) for dy in range(4) for dx in range(4) if dy or dx],
        key=lambda pair: -(min(pair[0], 4 - pair[0]) + min(pair[1], 4 - pair[1])),
    ):
        row_partners.append(((i // 4 + dy) % 4) * 4 + (i % 4 + dx) % 4)
    col_partners = [
        (j + offset) % GRID for offset in sorted(range(1, GRID), key=lambda o: -min(o, GRID - o))
    ]

    load_r.start()
    load_z.start()
    barrier = pltpu.get_barrier_semaphore()
    for there in row_partners:
        pl.semaphore_signal(barrier, inc=1, device_id=(there, j), device_id_type=MESH)
    for there in col_partners:
        pl.semaphore_signal(barrier, inc=1, device_id=(i, there), device_id_type=MESH)
    for load in [load_faces] + load_flex + load_stiff + [load_coarse]:
        load.start()

    def coarse_copy(there, slot):
        return pltpu.make_async_remote_copy(
            src_ref=coarse.at[:, pl.ds(pl.multiple_of(there * KROW, KROW), KROW)],
            dst_ref=coarse_f.at[slot],
            send_sem=wsend,
            recv_sem=wrecv,
            device_id=(there, j),
            device_id_type=MESH,
        )

    lane8 = lane_ids((LOADS, 128))
    group8 = lane8 // DEFL

    def copy1(phase, there):
        return pltpu.make_async_remote_copy(
            src_ref=recv1.at[phase, j],
            dst_ref=recv1.at[phase, j],
            send_sem=send1_sem,
            recv_sem=recv1_sem.at[phase],
            device_id=(i, there),
            device_id_type=MESH,
        )

    def copy2(phase, there):
        return pltpu.make_async_remote_copy(
            src_ref=send2.at[there],
            dst_ref=recv2.at[phase, i],
            send_sem=send2_sem,
            recv_sem=recv2_sem.at[phase],
            device_id=(there, j),
            device_id_type=MESH,
        )

    def whole1(phase):
        slots = recv1.at[phase, pl.ds(0, GRID - 1)]
        return pltpu.make_async_remote_copy(
            src_ref=slots,
            dst_ref=slots,
            send_sem=send1_sem,
            recv_sem=recv1_sem.at[phase],
            device_id=(i, j),
            device_id_type=MESH,
        )

    def whole2(phase):
        return pltpu.make_async_remote_copy(
            src_ref=send2.at[pl.ds(0, GRID - 1)],
            dst_ref=recv2.at[phase, pl.ds(0, GRID - 1)],
            send_sem=send2_sem,
            recv_sem=recv2_sem.at[phase],
            device_id=(i, j),
            device_id_type=MESH,
        )

    def whole_coarse():
        slots = coarse_f.at[pl.ds(0, GRID - 1)]
        return pltpu.make_async_remote_copy(
            src_ref=slots,
            dst_ref=slots,
            send_sem=wsend,
            recv_sem=wrecv,
            device_id=(i, j),
            device_id_type=MESH,
        )

    def gather_start(phase, coefficients, energy, sums):
        recv1[phase, j, 0:LOADS] = coefficients
        second = jnp.where(group8 == 1, energy, 0.0)
        for index, value in enumerate(sums):
            second = jnp.where(lane8 == 3 * DEFL + index, value, second)
        recv1[phase, j, LOADS : 2 * LOADS] = second
        for there in col_partners:
            copy1(phase, there).start()

    def gather_middle(phase, before_matmul=None):
        whole1(phase).wait_recv()
        first = [recv1[phase, source, 0:LOADS] for source in range(GRID)]
        groups = []
        for quarter in range(4):
            gathered = None
            for offset in range(4):
                source = quarter * 4 + offset
                value = first[source]
                if source:
                    value = value + first[source - 1]
                if source < GRID - 1:
                    value = value + first[source + 1]
                gathered = value if gathered is None else jnp.where(group8 == offset, value, gathered)
            groups.append(gathered)
        if before_matmul is not None:
            before_matmul()
        operand = parts(jnp.concatenate(groups, axis=1))
        partial = fold(dot_nt(operand, coarse_h[...]) + dot_nt(operand, coarse_l[...]))
        total = None
        crossed = None
        for quarter in range(4):
            energies = None
            for offset in range(4):
                second = recv1[phase, quarter * 4 + offset, LOADS : 2 * LOADS]
                total = second if total is None else total + second
                shift = ((offset + 3) % 4) * DEFL
                moved = pltpu.roll(second, shift, 1) if shift else second
                energies = moved if energies is None else jnp.where(group8 == offset, moved, energies)
            crossed = groups[quarter] * energies + (0.0 if crossed is None else crossed)
        total = total + jnp.where(lane8 == 3 * DEFL, row_sum(crossed), 0.0)
        tiles = [partial[:, n * 128 : (n + 1) * 128] for n in range(4)]
        turned = [
            [tile if not n else pltpu.roll(tile, 128 - n * DEFL, 1) for n in range(4)] for tile in tiles
        ]
        for target in range(GRID):
            before = (target + GRID - 1) % GRID
            quarter, offset = before // 4, before % 4
            value = turned[quarter][offset]
            if offset > 1:
                value = jnp.where(group8 < 4 - offset, value, turned[(quarter + 1) % 4][offset])
            send2[target] = jnp.where(group8 < 3, value, total)
        for there in row_partners:
            copy2(phase, there).start()
        recv2[phase, i] = send2[i]
        for quarter in range(4):
            row_g[quarter] = groups[quarter]
        mine = jnp.where(group8 == place, row_g[j // 4], 0.0)
        own_ref[...] = turn(mine, (5 - place) % 4)

    def gather_end(phase):
        whole2(phase).wait_recv()
        level = [recv2[phase, source] for source in range(GRID)]
        while len(level) > 1:
            level = [level[n] + level[n + 1] for n in range(0, len(level), 2)]
        whole1(phase).wait_send()
        whole2(phase).wait_send()
        return level[0]

    def coefficients_of(product):
        summed = fold(product)
        summed = summed + pltpu.roll(summed, 128 - DEFL, 1)
        return jnp.where(lane8 < DEFL, summed, 0.0)

    load_r.wait()
    load_z.wait()
    defl_high = defl_f[...].astype(BF16)
    defl_low = (defl_f[...] - defl_high.astype(F32)).astype(BF16)
    defl_t[0:DEFL] = defl_high
    defl_t[DEFL : 2 * DEFL] = defl_low
    defl_t[2 * DEFL :] = jnp.zeros((128 - 2 * DEFL, M), BF16)
    started = coefficients_of(dot_nt(parts(r_ref[...]), defl_t[...]))
    c_ref[...] = pltpu.roll(started, DEFL, 1)
    pl.semaphore_wait(barrier, 2 * (GRID - 1))
    for there in row_partners:
        coarse_copy(there, i).start()
    gather_start(0, turn(started, place), jnp.zeros((LOADS, 128), F32), ())

    sides = (
        (i > 0, (i - 1, j), 1),
        (i < GRID - 1, (i + 1, j), 0),
        (j > 0, (i, j - 1), 3),
        (j < GRID - 1, (i, j + 1), 2),
    )

    def first_copy(face, device, slot):
        return pltpu.make_async_remote_copy(
            src_ref=first_out.at[face],
            dst_ref=first_in.at[slot],
            send_sem=fsend_sem.at[face],
            recv_sem=frecv_sem.at[slot],
            device_id=device,
            device_id_type=MESH,
        )

    def face_copy(step, kind, face, device, slot):
        return pltpu.make_async_remote_copy(
            src_ref=halo_out.at[kind, face],
            dst_ref=halo_in.at[step, kind, slot],
            send_sem=hsend_sem.at[kind, face],
            recv_sem=hrecv_sem.at[step, kind, slot],
            device_id=device,
            device_id_type=MESH,
        )

    def send_faces(step, kind, traces):
        for face in range(4):
            halo_out[kind, face] = traces[:, face * FACE : (face + 1) * FACE]
        for face, (inside, device, slot) in enumerate(sides):

            @pl.when(inside)
            def _():
                face_copy(step, kind, face, device, slot).start()

    def take_faces(step, kind, traces):
        for face, (inside, device, slot) in enumerate(sides):

            @pl.when(inside)
            def _():
                face_copy(step, kind, slot, device, face).wait_recv()
                face_copy(step, kind, face, device, slot).wait_send()

        partner = jnp.concatenate([halo_in[step, kind, face] for face in range(4)], axis=1)
        return jnp.where(live > 0.5, traces - partner, 0.0)

    live = jnp.concatenate(
        [jnp.where(lane8 < face_len[0, face], 1.0, 0.0) for face in range(4)], axis=1
    )
    load_faces.wait()

    def build_pick(block, carry):
        start = pl.multiple_of(block * TILE, TILE)
        rows = row_ids((TILE, FACE)) + start
        for face in range(4):
            hit = rows == faces[face : face + 1, :]
            pick[pl.ds(start, TILE), face * FACE : (face + 1) * FACE] = jnp.where(hit, 1.0, 0.0).astype(BF16)
        return carry

    lax.fori_loop(0, NB, build_pick, 0)
    wide = LOADS + DEFL
    basis = parts(jnp.concatenate([r_ref[...], defl_f[...]], axis=0))
    for block in range(NB):
        wide_a[block] = basis[:, block * TILE : (block + 1) * TILE]
    both = fold(dot_nn(basis, pick[...]))
    tr_r[...] = both[0:LOADS]
    trace_t[0 : 2 * DEFL] = parts(both[LOADS:])
    trace_t[2 * DEFL :] = jnp.zeros((128 - 2 * DEFL, SLOTS), BF16)
    for face in range(4):
        first_out[face] = both[:, face * FACE : (face + 1) * FACE]
    for face, (inside, device, slot) in enumerate(sides):

        @pl.when(inside)
        def _():
            first_copy(face, device, slot).start()

    def build_spread(columns, target):
        lanes = lane_ids((LOADS, 128))
        rows = row_ids((NB * LOADS, 128))
        across = lane_ids((NB * LOADS, 128))
        for tile in range(4):
            named = jnp.zeros((LOADS, 128), jnp.int32)
            for spot in range(16):
                index = tile * 16 + spot
                named = jnp.where(lanes // LOADS == spot, columns[index % TPR, index // TPR], named)
            hit = (rows // LOADS == named[0:1, :]) & (rows % LOADS == across % LOADS)
            target[:, tile * 128 : (tile + 1) * 128] = jnp.where(hit, 1.0, 0.0).astype(BF16)

    build_spread(flex_cols, flex_s)
    build_spread(stiff_cols, stiff_s)

    def convert(pending, source, target):
        for n, load in enumerate(pending):
            load.wait()

            def one(block, carry):
                tiles = source[pl.ds(pl.multiple_of(block * TPR * TILE, TPR * TILE), TPR * TILE), :]
                high = tiles.astype(BF16)
                target[block, :, 0:TILE] = high
                target[block, :, TILE : 2 * TILE] = (tiles - high.astype(F32)).astype(BF16)
                return carry

            lax.fori_loop(n * NB // 4, (n + 1) * NB // 4, one, 0)

    convert(load_flex, flex_f, flex_t)
    convert(load_stiff, stiff_f, stiff_t)

    def coarse_ready():
        load_coarse.wait()
        whole_coarse().wait_recv()

        def one(block, carry):
            rows = coarse_f[block]
            high = rows.astype(BF16)
            start = pl.multiple_of(block * DEFL, DEFL)
            coarse_h[pl.ds(start, DEFL), :] = high
            coarse_l[pl.ds(start, DEFL), :] = (rows - high.astype(F32)).astype(BF16)
            return carry

        lax.fori_loop(0, GRID, one, 0)

    def forward(source, tiles, columns, target):
        for block in range(NB):
            operand = jnp.concatenate([source[columns[k, block]] for k in range(TPR)], axis=1)
            product = fold(dot_nn(operand, tiles[block]))
            target[block] = parts(product[:, 0:TILE] + product[:, TILE : 2 * TILE])

    def backward(source, tiles, selector, space):
        groups = space.shape[0]
        for block in range(NB):
            piece = source[block]
            product = fold(dot_nt(jnp.concatenate([piece, piece], axis=1), tiles[block]))
            rows = slice(block * TPR * LOADS, (block + 1) * TPR * LOADS)
            for group in range(groups):
                loads = product[group * LOADS : (group + 1) * LOADS]
                stacked = jnp.concatenate(
                    [loads[:, k * TILE : (k + 1) * TILE] for k in range(TPR)], axis=0
                )
                high = stacked.astype(BF16)
                space[group, rows, 0:TILE] = high
                space[group, rows, TILE : 2 * TILE] = (stacked - high.astype(F32)).astype(BF16)
        summed = []
        for group in range(groups):
            product = dot_nn(selector[...], space[group])
            summed.append(product[:, 0:TILE] + product[:, TILE : 2 * TILE])
        return [
            jnp.concatenate([one[block * LOADS : (block + 1) * LOADS] for one in summed], axis=0)
            for block in range(NB)
        ]

    forward(wide_a, flex_t, flex_cols, wide_b)
    forward(wide_b, stiff_t, stiff_cols, wide_a)
    gather_middle(0, coarse_ready)
    middle = backward(wide_a, stiff_t, stiff_s, wide_spread)
    for block in range(NB):
        wide_b[block] = parts(middle[block])
    applied = backward(wide_b, flex_t, flex_s, wide_spread)
    for block in range(NB):
        span = slice(block * TILE, (block + 1) * TILE)
        a_ref[:, span] = r_ref[:, span] + applied[block][0:LOADS]
        image_t[:, span] = parts(defl_f[:, span] + applied[block][LOADS:wide])

    for face, (inside, device, slot) in enumerate(sides):

        @pl.when(inside)
        def _():
            first_copy(slot, device, face).wait_recv()
            first_copy(face, device, slot).wait_send()

    def operator_coefficients(field, jump):
        return coefficients_of(dot_nt(parts(field), defl_t[...]) + dot_nt(parts(jump), trace_t[...]))

    partner = jnp.concatenate([first_in[face, 0:LOADS] for face in range(4)], axis=1)
    jump = jnp.where(live > 0.5, tr_r[...] - partner, 0.0)
    jump_r[...] = jump
    found = operator_coefficients(a_ref[...], jump)
    gr_ref[0] = turn(found, place)
    gr_ref[1] = pltpu.roll(found, DEFL, 1)

    traces = [first_out[face, LOADS:wide] for face in range(4)]
    others = [
        jnp.where(live[0:1, face * FACE : (face + 1) * FACE] > 0.5, first_in[face, LOADS:wide], 0.0)
        for face in range(4)
    ]
    masked = [
        jnp.where(live[0:1, face * FACE : (face + 1) * FACE] > 0.5, traces[face], 0.0)
        for face in range(4)
    ]
    lane32 = lane_ids((DEFL, 128))

    def paired(product):
        summed = fold(product)
        summed = summed + pltpu.roll(summed, 128 - DEFL, 1)
        return jnp.where(lane32 < DEFL, summed, 0.0)

    def against(value):
        return jnp.concatenate([parts(value), jnp.zeros((2 * DEFL, FACE), BF16)], axis=0)

    own = dot_nt(image_t[...], defl_t[...])
    for face in range(4):
        own = own + dot_nt(parts(masked[face]), trace_t[:, face * FACE : (face + 1) * FACE])
    north = paired(dot_nt(parts(others[0]), trace_t[:, 0:FACE]))
    south = paired(dot_nt(parts(others[1]), trace_t[:, FACE : 2 * FACE]))
    west = paired(dot_nt(parts(masked[2]), against(others[2])))
    east = paired(dot_nt(parts(masked[3]), against(others[3])))
    couple = jnp.concatenate(
        [
            -turn(north, place),
            turn(paired(own), place) - turn(west, (place + 3) % 4) - turn(east, (place + 1) % 4),
            -turn(south, place),
            jnp.zeros((DEFL, 128), F32),
        ],
        axis=0,
    )
    couple_t[...] = parts(couple)

    zeros = jnp.zeros((LOADS, M), F32)
    for ref in (b_ref, bw_ref, p_ref, q_ref, w_ref, x_ref, z_ref):
        ref[...] = zeros
    short = jnp.zeros((LOADS, SLOTS), F32)
    for ref in (tr_w, tr_q, jump_w, jump_q):
        ref[...] = short
    none = jnp.zeros((LOADS, 128), F32)
    for ref in (e_q, alpha_ref, beta_ref, cq_ref):
        ref[...] = none
    for layout in range(2):
        gq_ref[layout] = none
        gw_ref[layout] = none
    s1_ref[...] = jnp.ones((LOADS, 128), F32)

    e_r[...] = jnp.where(group8 < 3, gather_end(0), 0.0)
    own_ref[...] = none
    whole_coarse().wait_send()

    def energy_parts():
        energy = jnp.where(group8 == 1, e_r[...], 0.0)
        return parts(energy + pltpu.roll(energy, 128 - DEFL, 1))[:, 0 : 2 * DEFL]

    def advance():
        alpha = alpha_ref[:, 0:1]
        beta = beta_ref[:, 0:1]
        direction = z_ref[...] + beta * p_ref[...]
        image = w_ref[...] + beta * q_ref[...]
        p_ref[...] = direction
        q_ref[...] = image
        residual = r_ref[...] - alpha * image
        r_ref[...] = residual
        return alpha, beta, direction, image, residual

    def iterate(step, carry):
        energies = e_r[...]
        doubled = parts(energies)
        coefficients = fold(dot_nn(jnp.concatenate([doubled, doubled], axis=1), couple_t[...]))
        alpha, beta, p, q, r = advance()
        applied = bw_ref[...] + beta * b_ref[...]
        b_ref[...] = applied
        a = a_ref[...] - alpha * applied
        a_ref[...] = a
        for layout in range(2):
            image = gw_ref[layout] + beta * gq_ref[layout]
            gq_ref[layout] = image
            gr_ref[layout] = gr_ref[layout] - alpha * image
        image = own_ref[...] + beta * cq_ref[...]
        cq_ref[...] = image
        c = c_ref[...] - alpha * image
        c_ref[...] = c
        trace_q = tr_w[...] + beta * tr_q[...]
        tr_q[...] = trace_q
        tr = tr_r[...] - alpha * trace_q
        tr_r[...] = tr
        jump_q_now = jump_w[...] + beta * jump_q[...]
        jump_q[...] = jump_q_now
        jump_now = jump_r[...] - alpha * jump_q_now
        jump_r[...] = jump_now
        sum_zar = row_sum(r * a) + row_sum(tr * jump_now) + row_sum(energies * gr_ref[1])
        sum_rz = row_sum(r * r) + row_sum(energies * c)
        sum_rp = row_sum(r * p)
        sum_zq = row_sum(r * q) + row_sum(energies * image)
        gather_start(
            step + 1, coefficients + gr_ref[0], energies, (sum_zar, sum_rz, sum_rp, sum_zq)
        )

        energy = energy_parts()
        traces = tr + fold(dot_nn(energy, trace_t[0 : 2 * DEFL]))
        send_faces(step, 0, traces)
        x_ref[...] = x_ref[...] + alpha * p
        z_ref[...] = r_ref[...] + fold(dot_nn(energy, defl_t[0 : 2 * DEFL]))
        w_ref[...] = a_ref[...] + fold(dot_nn(energy, image_t[...]))
        jump = take_faces(step, 0, traces)
        w = w_ref[...] + fold(dot_nt(parts(jump), pick[...]))
        w_ref[...] = w
        split = parts(w)
        for block in range(NB):
            blocks_a[block] = split[:, block * TILE : (block + 1) * TILE]

        @pl.when(step < ITERS - 1)
        def _():
            image = fold(dot_nn(split, pick[...]))
            tr_w[...] = image
            send_faces(step, 1, image)

        gather_middle(step + 1)

        @pl.when(step < ITERS - 1)
        def _():
            forward(blocks_a, flex_t, flex_cols, blocks_b)
            forward(blocks_b, stiff_t, stiff_cols, blocks_a)
            middle = backward(blocks_a, stiff_t, stiff_s, spread)
            for block in range(NB):
                blocks_b[block] = parts(middle[block])
            local = backward(blocks_b, flex_t, flex_s, spread)
            image = w_ref[...] + jnp.concatenate(local, axis=1)
            bw_ref[...] = image
            jump = take_faces(step, 1, tr_w[...])
            jump_w[...] = jump
            found = operator_coefficients(image, jump)
            gw_ref[0] = turn(found, place)
            gw_ref[1] = pltpu.roll(found, DEFL, 1)

        gathered = gather_end(step + 1)

        def total(index):
            return gathered[:, 3 * DEFL + index : 3 * DEFL + index + 1]

        new_beta = -total(3) / s1_ref[:, 0:1]
        curvature = total(0) + new_beta * total(3)
        new_alpha = (total(1) + new_beta * total(2)) / curvature
        s1_ref[...] = jnp.broadcast_to(curvature, (LOADS, 128))
        alpha_ref[...] = jnp.broadcast_to(new_alpha, (LOADS, 128))
        beta_ref[...] = jnp.broadcast_to(new_beta, (LOADS, 128))
        energy_q = jnp.where(group8 < 3, gathered, 0.0) + new_beta * e_q[...]
        e_q[...] = energy_q
        e_r[...] = e_r[...] - new_alpha * energy_q
        return carry

    lax.fori_loop(0, ITERS, iterate, 0)
    alpha, _, p, _, r = advance()
    x_ref[...] = x_ref[...] + alpha * p
    z_ref[...] = r + fold(dot_nn(energy_parts(), defl_t[0 : 2 * DEFL]))


def publish(x_in, r_in, z_in, x_out, r_out, z_out):
    x_out[...] = x_in[...]
    r_out[...] = r_in[...]
    z_out[...] = z_in[...]


def shards(rhs, flex, flex_cols, stiff, stiff_cols, defl, coarse, face_rows, face_len):
    anywhere = pl.BlockSpec(memory_space=pl.ANY)
    scalars = pl.BlockSpec(memory_space=pltpu.SMEM)
    vector = pl.BlockSpec(memory_space=pltpu.VMEM)
    field = jax.ShapeDtypeStruct((LOADS, M), F32)
    vmem = pltpu.VMEM
    dma = pltpu.SemaphoreType.DMA
    wide = 2 * (LOADS + DEFL)
    found = pl.pallas_call(
        kernel,
        out_shape=(field, field, field),
        in_specs=[
            anywhere, anywhere, scalars, anywhere, scalars, anywhere, anywhere, anywhere, scalars,
        ],
        out_specs=(vector, vector, vector),
        scratch_shapes=[
            vmem((NB * TPR * TILE, TILE), F32),
            vmem((NB * TPR * TILE, TILE), F32),
            vmem((DEFL, M), F32),
            vmem((GRID, DEFL, KROW), F32),
            vmem((4, FACE), jnp.int32),
            vmem((NB, TPR * TILE, 2 * TILE), BF16),
            vmem((NB, TPR * TILE, 2 * TILE), BF16),
            vmem((NB * LOADS, NB * TPR * LOADS), BF16),
            vmem((NB * LOADS, NB * TPR * LOADS), BF16),
            vmem((128, M), BF16),
            vmem((2 * DEFL, M), BF16),
            vmem((128, SLOTS), BF16),
            vmem((KROW, KROW), BF16),
            vmem((KROW, KROW), BF16),
            vmem((M, SLOTS), BF16),
            vmem((256, 128), BF16),
            vmem((NB, wide, TILE), BF16),
            vmem((NB, wide, TILE), BF16),
            vmem((wide // 16, NB * TPR * LOADS, 2 * TILE), BF16),
            vmem((NB, 2 * LOADS, TILE), BF16),
            vmem((NB, 2 * LOADS, TILE), BF16),
            vmem((1, NB * TPR * LOADS, 2 * TILE), BF16),
            *[vmem((LOADS, M), F32)] * 6,
            *[vmem((LOADS, SLOTS), F32)] * 6,
            *[vmem((LOADS, 128), F32)] * 5,
            *[vmem((2, LOADS, 128), F32)] * 3,
            *[vmem((LOADS, 128), F32)] * 3,
            vmem((4, LOADS, 128), F32),
            vmem((ITERS + 1, GRID, 2 * LOADS, 128), F32),
            vmem((GRID, LOADS, 128), F32),
            vmem((ITERS + 1, GRID, LOADS, 128), F32),
            vmem((4, LOADS + DEFL, FACE), F32),
            vmem((4, LOADS + DEFL, FACE), F32),
            vmem((2, 4, LOADS, FACE), F32),
            vmem((ITERS, 2, 4, LOADS, FACE), F32),
            dma((12,)),
            dma,
            dma,
            dma,
            dma((ITERS + 1,)),
            dma,
            dma((ITERS + 1,)),
            dma((4,)),
            dma((4,)),
            dma((2, 4)),
            dma((ITERS, 2, 4)),
        ],
        compiler_params=pltpu.CompilerParams(
            collective_id=0, has_side_effects=True, vmem_limit_bytes=66_500_000
        ),
        name="feti",
    )(rhs, flex, flex_cols.T, stiff, stiff_cols.T, defl, coarse, face_rows, face_len)
    return pl.pallas_call(
        publish,
        out_shape=(field, field, field),
        in_specs=[vector, vector, vector],
        out_specs=(vector, vector, vector),
        compiler_params=pltpu.CompilerParams(vmem_limit_bytes=66_500_000),
        name="publish",
    )(*found)


def solution(mesh):
    return jax.shard_map(
        shards,
        mesh=mesh,
        in_specs=(
            P("row", "col"),
            P("row", "col"),
            P("row", "col"),
            P("row", "col"),
            P("row", "col"),
            P("row", "col"),
            P(("row", "col"), None),
            P("row", "col"),
            P("row", "col"),
        ),
        out_specs=(P("row", "col"), P("row", "col"), P("row", "col")),
        check_vma=False,
    )
```

```python
import functools

import jax
import jax.numpy as jnp
from jax import lax
from jax.experimental import pallas as pl
from jax.experimental.pallas import tpu as pltpu
from jax.sharding import PartitionSpec as P

ITERS = 3
GRID = 16
LOADS = 8
NB = 16
TPR = 4
TILE = 128
M = 2048
DEFL = 32
FACE = 128
SLOTS = 4 * FACE
KROW = GRID * DEFL
MESH = pl.DeviceIdType.MESH
F32 = jnp.float32
BF16 = jnp.bfloat16


def dot_nn(a, b):
    return lax.dot_general(a, b, (((1,), (0,)), ((), ())), preferred_element_type=F32)


def dot_nt(a, b):
    return lax.dot_general(a, b, (((1,), (1,)), ((), ())), preferred_element_type=F32)


def parts(value):
    high = value.astype(BF16).astype(F32)
    return jnp.concatenate([high, value - high], axis=0).astype(BF16)


def fold(value):
    half = value.shape[0] // 2
    return value[:half] + value[half:]


def lane_ids(shape):
    return lax.broadcasted_iota(jnp.int32, shape, 1)


def row_ids(shape):
    return lax.broadcasted_iota(jnp.int32, shape, 0)


def row_sum(value):
    return jnp.sum(value, axis=1, keepdims=True)


def turn(value, place):
    moved = value
    for groups in range(1, 4):
        moved = jnp.where(place == groups, pltpu.roll(value, groups * DEFL, 1), moved)
    return moved


def kernel(
    rhs, flex, flex_cols, stiff, stiff_cols, defl, coarse, face_rows, face_len,
    x_ref, r_ref, z_ref,
    flex_f, stiff_f, defl_f, coarse_own, coarse_f, across_out, across_in, faces,
    flex_t, stiff_t, flex_s, stiff_s, defl_t, image_t, trace_t, coarse_h, coarse_l, across_h, across_l, pick, couple_t,
    wide_a, wide_b, wide_spread, blocks_a, blocks_b, spread,
    a_ref, b_ref, bw_ref, p_ref, q_ref, w_ref, tr_r, tr_w, tr_q, jump_r, jump_w, jump_q,
    e_r, e_q, s1_ref, alpha_ref, beta_ref, gr_ref, gq_ref, gw_ref, own_ref, c_ref, cq_ref,
    row_g, recv1, send2, recv2, first_out, first_in, halo_out, halo_in,
    load_sem, wsend, wrecv, asend, arecv, send1_sem, recv1_sem, send2_sem, recv2_sem, fsend_sem, frecv_sem,
    hsend_sem, hrecv_sem,
):
    i = lax.axis_index("row")
    j = lax.axis_index("col")
    place = j % 4
    pair = j // 4
    odd = (j // 2) % 2
    beside = (pair + 3 + 2 * odd) % 4
    far_groups = ((pair + 2) % 4, (pair + 1 + 2 * odd) % 4)
    chunk = NB * TPR * TILE // 4

    def part_of(ref, index):
        return ref.at[pl.ds(index * chunk, chunk), :]

    load_r = pltpu.make_async_copy(rhs, r_ref, load_sem.at[0])
    load_z = pltpu.make_async_copy(defl, defl_f, load_sem.at[1])
    load_faces = pltpu.make_async_copy(face_rows, faces, load_sem.at[2])
    load_coarse = pltpu.make_async_copy(coarse, coarse_own, load_sem.at[3])
    load_flex = [
        pltpu.make_async_copy(part_of(flex, n), part_of(flex_f, n), load_sem.at[4 + n]) for n in range(4)
    ]
    load_stiff = [
        pltpu.make_async_copy(part_of(stiff, n), part_of(stiff_f, n), load_sem.at[8 + n]) for n in range(4)
    ]

    row_partners = []
    for dy, dx in sorted(
        [(dy, dx) for dy in range(4) for dx in range(4) if dy or dx],
        key=lambda pair: -(min(pair[0], 4 - pair[0]) + min(pair[1], 4 - pair[1])),
    ):
        row_partners.append(((i // 4 + dy) % 4) * 4 + (i % 4 + dx) % 4)
    col_partners = [
        (j + offset) % GRID for offset in sorted(range(1, GRID), key=lambda o: -min(o, GRID - o))
    ]

    load_r.start()
    load_z.start()
    barrier = pltpu.get_barrier_semaphore()
    for there in row_partners:
        pl.semaphore_signal(barrier, inc=1, device_id=(there, j), device_id_type=MESH)
    for there in col_partners:
        pl.semaphore_signal(barrier, inc=1, device_id=(i, there), device_id_type=MESH)
    for load in [load_coarse, load_faces] + load_flex + load_stiff:
        load.start()

    def coarse_lanes(row, group):
        return pl.ds(pl.multiple_of(row * KROW + group * 128, 128), 128)

    def coarse_copy(there, part):
        return pltpu.make_async_remote_copy(
            src_ref=coarse.at[:, coarse_lanes(there, far_groups[part])],
            dst_ref=coarse_f.at[i, part],
            send_sem=wsend,
            recv_sem=wrecv,
            device_id=(there, j),
            device_id_type=MESH,
        )

    lane8 = lane_ids((LOADS, 128))
    group8 = lane8 // DEFL

    def copy1(phase, there):
        return pltpu.make_async_remote_copy(
            src_ref=recv1.at[phase, j],
            dst_ref=recv1.at[phase, j],
            send_sem=send1_sem,
            recv_sem=recv1_sem.at[phase],
            device_id=(i, there),
            device_id_type=MESH,
        )

    def copy2(phase, there):
        return pltpu.make_async_remote_copy(
            src_ref=send2.at[there],
            dst_ref=recv2.at[phase, i],
            send_sem=send2_sem,
            recv_sem=recv2_sem.at[phase],
            device_id=(there, j),
            device_id_type=MESH,
        )

    def whole1(phase):
        slots = recv1.at[phase, pl.ds(0, GRID - 1)]
        return pltpu.make_async_remote_copy(
            src_ref=slots,
            dst_ref=slots,
            send_sem=send1_sem,
            recv_sem=recv1_sem.at[phase],
            device_id=(i, j),
            device_id_type=MESH,
        )

    def whole2(phase):
        return pltpu.make_async_remote_copy(
            src_ref=send2.at[pl.ds(0, GRID - 1)],
            dst_ref=recv2.at[phase, pl.ds(0, GRID - 1)],
            send_sem=send2_sem,
            recv_sem=recv2_sem.at[phase],
            device_id=(i, j),
            device_id_type=MESH,
        )

    def across_copy(piece, there, slot):
        return pltpu.make_async_remote_copy(
            src_ref=across_out.at[piece],
            dst_ref=across_in.at[slot],
            send_sem=asend,
            recv_sem=arecv,
            device_id=(i, there),
            device_id_type=MESH,
        )

    def whole_across():
        return pltpu.make_async_remote_copy(
            src_ref=across_out.at[pl.ds(0, 7)],
            dst_ref=across_in.at[pl.ds(0, 7)],
            send_sem=asend,
            recv_sem=arecv,
            device_id=(i, j),
            device_id_type=MESH,
        )

    def whole_coarse():
        slots = coarse_f.at[pl.ds(0, GRID - 1)]
        return pltpu.make_async_remote_copy(
            src_ref=slots,
            dst_ref=slots,
            send_sem=wsend,
            recv_sem=wrecv,
            device_id=(i, j),
            device_id_type=MESH,
        )

    def gather_start(phase, coefficients, energy, sums):
        recv1[phase, j, 0:LOADS] = coefficients
        second = jnp.where(group8 == 1, energy, 0.0)
        for index, value in enumerate(sums):
            second = jnp.where(lane8 == 3 * DEFL + index, value, second)
        recv1[phase, j, LOADS : 2 * LOADS] = second
        for there in col_partners:
            copy1(phase, there).start()

    def gather_middle(phase, before_matmul=None):
        whole1(phase).wait_recv()
        first = [recv1[phase, source, 0:LOADS] for source in range(GRID)]
        groups = []
        for quarter in range(4):
            gathered = None
            for offset in range(4):
                source = quarter * 4 + offset
                value = first[source]
                if source:
                    value = value + first[source - 1]
                if source < GRID - 1:
                    value = value + first[source + 1]
                gathered = value if gathered is None else jnp.where(group8 == offset, value, gathered)
            groups.append(gathered)
        if before_matmul is not None:
            before_matmul()
        for quarter in range(4):
            row_g[quarter] = groups[quarter]
        near = parts(jnp.concatenate([row_g[pair], row_g[beside]], axis=1))
        far = parts(jnp.concatenate([row_g[far_groups[0]], row_g[far_groups[1]]], axis=1))
        partial = fold(
            dot_nn(near, across_h[...])
            + dot_nn(near, across_l[...])
            + dot_nt(far, coarse_h[...])
            + dot_nt(far, coarse_l[...])
        )
        total = None
        crossed = None
        for quarter in range(4):
            energies = None
            for offset in range(4):
                second = recv1[phase, quarter * 4 + offset, LOADS : 2 * LOADS]
                total = second if total is None else total + second
                shift = ((offset + 3) % 4) * DEFL
                moved = pltpu.roll(second, shift, 1) if shift else second
                energies = moved if energies is None else jnp.where(group8 == offset, moved, energies)
            crossed = groups[quarter] * energies + (0.0 if crossed is None else crossed)
        total = total + jnp.where(lane8 == 3 * DEFL, row_sum(crossed), 0.0)
        tiles = [partial[:, n * 128 : (n + 1) * 128] for n in range(4)]
        turned = [
            [tile if not n else pltpu.roll(tile, 128 - n * DEFL, 1) for n in range(4)] for tile in tiles
        ]
        for target in range(GRID):
            before = (target + GRID - 1) % GRID
            quarter, offset = before // 4, before % 4
            value = turned[quarter][offset]
            if offset > 1:
                value = jnp.where(group8 < 4 - offset, value, turned[(quarter + 1) % 4][offset])
            send2[target] = jnp.where(group8 < 3, value, total)
        for there in row_partners:
            copy2(phase, there).start()
        recv2[phase, i] = send2[i]
        mine = jnp.where(group8 == place, row_g[j // 4], 0.0)
        own_ref[...] = turn(mine, (5 - place) % 4)

    def gather_end(phase):
        whole2(phase).wait_recv()
        level = [recv2[phase, source] for source in range(GRID)]
        while len(level) > 1:
            level = [level[n] + level[n + 1] for n in range(0, len(level), 2)]
        whole1(phase).wait_send()
        whole2(phase).wait_send()
        return level[0]

    def coefficients_of(product):
        summed = fold(product)
        summed = summed + pltpu.roll(summed, 128 - DEFL, 1)
        return jnp.where(lane8 < DEFL, summed, 0.0)

    load_r.wait()
    load_z.wait()
    defl_high = defl_f[...].astype(BF16)
    defl_low = (defl_f[...] - defl_high.astype(F32)).astype(BF16)
    defl_t[0:DEFL] = defl_high
    defl_t[DEFL : 2 * DEFL] = defl_low
    defl_t[2 * DEFL :] = jnp.zeros((128 - 2 * DEFL, M), BF16)
    started = coefficients_of(dot_nt(parts(r_ref[...]), defl_t[...]))
    c_ref[...] = pltpu.roll(started, DEFL, 1)
    pl.semaphore_wait(barrier, 2 * (GRID - 1))
    for there in row_partners:
        for part in range(2):
            coarse_copy(there, part).start()
    gather_start(0, turn(started, place), jnp.zeros((LOADS, 128), F32), ())

    load_coarse.wait()
    group32 = lane_ids((DEFL, 128)) // DEFL
    after, ahead = (pair + 1) % 4, (pair + 3) % 4
    for piece, (group, spot) in enumerate(
        [(pair, 0), (pair, 1), (pair, 2), (pair, 3), (after, 0), (after, 1), (ahead, 2), (ahead, 3)]
    ):
        for quarter in range(4):
            packed = None
            for offset in range(4):
                value = coarse_own[:, coarse_lanes(quarter * 4 + offset, group)]
                shift = ((offset - spot) % 4) * DEFL
                if shift:
                    value = pltpu.roll(value, shift, 1)
                packed = value if packed is None else jnp.where(group32 == offset, value, packed)
            across_out[piece, :, quarter * 128 : (quarter + 1) * 128] = packed
    for piece, there in ((4, after * 4), (5, after * 4 + 1), (6, ahead * 4 + 2), (7, ahead * 4 + 3)):
        across_copy(piece, there, 4 + place).start()
    for step in range(1, 4):
        other = (place + step) % 4
        across_copy(other, pair * 4 + other, place).start()
    across_in[place] = across_out[place]
    for part in range(2):
        coarse_f[i, part] = coarse_own[:, coarse_lanes(i, far_groups[part])]

    sides = (
        (i > 0, (i - 1, j), 1),
        (i < GRID - 1, (i + 1, j), 0),
        (j > 0, (i, j - 1), 3),
        (j < GRID - 1, (i, j + 1), 2),
    )

    def first_copy(face, device, slot):
        return pltpu.make_async_remote_copy(
            src_ref=first_out.at[face],
            dst_ref=first_in.at[slot],
            send_sem=fsend_sem.at[face],
            recv_sem=frecv_sem.at[slot],
            device_id=device,
            device_id_type=MESH,
        )

    def face_copy(step, kind, face, device, slot):
        return pltpu.make_async_remote_copy(
            src_ref=halo_out.at[kind, face],
            dst_ref=halo_in.at[step, kind, slot],
            send_sem=hsend_sem.at[kind, face],
            recv_sem=hrecv_sem.at[step, kind, slot],
            device_id=device,
            device_id_type=MESH,
        )

    def store_faces(kind, traces):
        for face in range(4):
            halo_out[kind, face] = traces[:, face * FACE : (face + 1) * FACE]

    def start_faces(step, kind):
        for face, (inside, device, slot) in enumerate(sides):

            @pl.when(inside)
            def _():
                face_copy(step, kind, face, device, slot).start()

    def take_faces(step, kind, traces):
        for face, (inside, device, slot) in enumerate(sides):

            @pl.when(inside)
            def _():
                face_copy(step, kind, slot, device, face).wait_recv()
                face_copy(step, kind, face, device, slot).wait_send()

        partner = jnp.concatenate([halo_in[step, kind, face] for face in range(4)], axis=1)
        return jnp.where(live > 0.5, traces - partner, 0.0)

    live = jnp.concatenate(
        [jnp.where(lane8 < face_len[0, face], 1.0, 0.0) for face in range(4)], axis=1
    )
    load_faces.wait()

    def build_pick(block, carry):
        start = pl.multiple_of(block * TILE, TILE)
        rows = row_ids((TILE, FACE)) + start
        for face in range(4):
            hit = rows == faces[face : face + 1, :]
            pick[pl.ds(start, TILE), face * FACE : (face + 1) * FACE] = jnp.where(hit, 1.0, 0.0).astype(BF16)
        return carry

    lax.fori_loop(0, NB, build_pick, 0)
    wide = LOADS + DEFL
    basis = parts(jnp.concatenate([r_ref[...], defl_f[...]], axis=0))
    for block in range(NB):
        wide_a[block] = basis[:, block * TILE : (block + 1) * TILE]
    both = fold(dot_nn(basis, pick[...]))
    tr_r[...] = both[0:LOADS]
    trace_t[0 : 2 * DEFL] = parts(both[LOADS:])
    trace_t[2 * DEFL :] = jnp.zeros((128 - 2 * DEFL, SLOTS), BF16)
    for face in range(4):
        first_out[face] = both[:, face * FACE : (face + 1) * FACE]
    for face, (inside, device, slot) in enumerate(sides):

        @pl.when(inside)
        def _():
            first_copy(face, device, slot).start()

    def build_spread(columns, target):
        lanes = lane_ids((LOADS, 128))
        rows = row_ids((NB * LOADS, 128))
        across = lane_ids((NB * LOADS, 128))
        for tile in range(4):
            named = jnp.zeros((LOADS, 128), jnp.int32)
            for spot in range(16):
                index = tile * 16 + spot
                named = jnp.where(lanes // LOADS == spot, columns[index % TPR, index // TPR], named)
            hit = (rows // LOADS == named[0:1, :]) & (rows % LOADS == across % LOADS)
            target[:, tile * 128 : (tile + 1) * 128] = jnp.where(hit, 1.0, 0.0).astype(BF16)

    build_spread(flex_cols, flex_s)
    build_spread(stiff_cols, stiff_s)

    def convert(pending, source, target):
        for n, load in enumerate(pending):
            load.wait()

            def one(block, carry):
                tiles = source[pl.ds(pl.multiple_of(block * TPR * TILE, TPR * TILE), TPR * TILE), :]
                high = tiles.astype(BF16)
                target[block, :, 0:TILE] = high
                target[block, :, TILE : 2 * TILE] = (tiles - high.astype(F32)).astype(BF16)
                return carry

            lax.fori_loop(n * NB // 4, (n + 1) * NB // 4, one, 0)

    convert(load_flex, flex_f, flex_t)
    convert(load_stiff, stiff_f, stiff_t)

    def coarse_ready():
        whole_across().wait_recv()

        def one_across(block, carry):
            rows = across_in[block]
            high = rows.astype(BF16)
            start = pl.multiple_of(block * DEFL, DEFL)
            across_h[pl.ds(start, DEFL), :] = high
            across_l[pl.ds(start, DEFL), :] = (rows - high.astype(F32)).astype(BF16)
            return carry

        lax.fori_loop(0, 8, one_across, 0)
        whole_coarse().wait_recv()

        def one(block, carry):
            start = pl.multiple_of(block * DEFL, DEFL)
            for part in range(2):
                rows = coarse_f[block, part]
                high = rows.astype(BF16)
                lanes = slice(part * 128, (part + 1) * 128)
                coarse_h[pl.ds(start, DEFL), lanes] = high
                coarse_l[pl.ds(start, DEFL), lanes] = (rows - high.astype(F32)).astype(BF16)
            return carry

        lax.fori_loop(0, GRID, one, 0)

    def forward(source, tiles, columns, target):
        for block in range(NB):
            operand = jnp.concatenate([source[columns[k, block]] for k in range(TPR)], axis=1)
            product = fold(dot_nn(operand, tiles[block]))
            target[block] = parts(product[:, 0:TILE] + product[:, TILE : 2 * TILE])

    def backward(source, tiles, selector, space):
        groups = space.shape[0]
        for block in range(NB):
            piece = source[block]
            product = fold(dot_nt(jnp.concatenate([piece, piece], axis=1), tiles[block]))
            rows = slice(block * TPR * LOADS, (block + 1) * TPR * LOADS)
            for group in range(groups):
                loads = product[group * LOADS : (group + 1) * LOADS]
                stacked = jnp.concatenate(
                    [loads[:, k * TILE : (k + 1) * TILE] for k in range(TPR)], axis=0
                )
                high = stacked.astype(BF16)
                space[group, rows, 0:TILE] = high
                space[group, rows, TILE : 2 * TILE] = (stacked - high.astype(F32)).astype(BF16)
        summed = []
        for group in range(groups):
            product = dot_nn(selector[...], space[group])
            summed.append(product[:, 0:TILE] + product[:, TILE : 2 * TILE])
        return [
            jnp.concatenate([one[block * LOADS : (block + 1) * LOADS] for one in summed], axis=0)
            for block in range(NB)
        ]

    forward(wide_a, flex_t, flex_cols, wide_b)
    forward(wide_b, stiff_t, stiff_cols, wide_a)
    gather_middle(0, coarse_ready)
    middle = backward(wide_a, stiff_t, stiff_s, wide_spread)
    for block in range(NB):
        wide_b[block] = parts(middle[block])
    applied = backward(wide_b, flex_t, flex_s, wide_spread)
    for block in range(NB):
        span = slice(block * TILE, (block + 1) * TILE)
        a_ref[:, span] = r_ref[:, span] + applied[block][0:LOADS]
        image_t[:, span] = parts(defl_f[:, span] + applied[block][LOADS:wide])

    for face, (inside, device, slot) in enumerate(sides):

        @pl.when(inside)
        def _():
            first_copy(slot, device, face).wait_recv()
            first_copy(face, device, slot).wait_send()

    def operator_coefficients(field, jump):
        return coefficients_of(dot_nt(parts(field), defl_t[...]) + dot_nt(parts(jump), trace_t[...]))

    partner = jnp.concatenate([first_in[face, 0:LOADS] for face in range(4)], axis=1)
    jump = jnp.where(live > 0.5, tr_r[...] - partner, 0.0)
    jump_r[...] = jump
    found = operator_coefficients(a_ref[...], jump)
    gr_ref[0] = turn(found, place)
    gr_ref[1] = pltpu.roll(found, DEFL, 1)

    traces = [first_out[face, LOADS:wide] for face in range(4)]
    others = [
        jnp.where(live[0:1, face * FACE : (face + 1) * FACE] > 0.5, first_in[face, LOADS:wide], 0.0)
        for face in range(4)
    ]
    masked = [
        jnp.where(live[0:1, face * FACE : (face + 1) * FACE] > 0.5, traces[face], 0.0)
        for face in range(4)
    ]
    lane32 = lane_ids((DEFL, 128))

    def paired(product):
        summed = fold(product)
        summed = summed + pltpu.roll(summed, 128 - DEFL, 1)
        return jnp.where(lane32 < DEFL, summed, 0.0)

    def against(value):
        return jnp.concatenate([parts(value), jnp.zeros((2 * DEFL, FACE), BF16)], axis=0)

    own = dot_nt(image_t[...], defl_t[...])
    for face in range(4):
        own = own + dot_nt(parts(masked[face]), trace_t[:, face * FACE : (face + 1) * FACE])
    north = paired(dot_nt(parts(others[0]), trace_t[:, 0:FACE]))
    south = paired(dot_nt(parts(others[1]), trace_t[:, FACE : 2 * FACE]))
    west = paired(dot_nt(parts(masked[2]), against(others[2])))
    east = paired(dot_nt(parts(masked[3]), against(others[3])))
    couple = jnp.concatenate(
        [
            -turn(north, place),
            turn(paired(own), place) - turn(west, (place + 3) % 4) - turn(east, (place + 1) % 4),
            -turn(south, place),
            jnp.zeros((DEFL, 128), F32),
        ],
        axis=0,
    )
    couple_t[...] = parts(couple)

    zeros = jnp.zeros((LOADS, M), F32)
    for ref in (b_ref, bw_ref, p_ref, q_ref, w_ref, x_ref, z_ref):
        ref[...] = zeros
    short = jnp.zeros((LOADS, SLOTS), F32)
    for ref in (tr_w, tr_q, jump_w, jump_q):
        ref[...] = short
    none = jnp.zeros((LOADS, 128), F32)
    for ref in (e_q, alpha_ref, beta_ref, cq_ref):
        ref[...] = none
    for layout in range(2):
        gq_ref[layout] = none
        gw_ref[layout] = none
    s1_ref[...] = jnp.ones((LOADS, 128), F32)

    e_r[...] = jnp.where(group8 < 3, gather_end(0), 0.0)
    own_ref[...] = none
    whole_coarse().wait_send()
    whole_across().wait_send()

    def energy_parts():
        energy = jnp.where(group8 == 1, e_r[...], 0.0)
        return parts(energy + pltpu.roll(energy, 128 - DEFL, 1))[:, 0 : 2 * DEFL]

    def advance():
        alpha = alpha_ref[:, 0:1]
        beta = beta_ref[:, 0:1]
        direction = z_ref[...] + beta * p_ref[...]
        image = w_ref[...] + beta * q_ref[...]
        p_ref[...] = direction
        q_ref[...] = image
        residual = r_ref[...] - alpha * image
        r_ref[...] = residual
        return alpha, beta, direction, image, residual

    def iterate(step, carry):
        energies = e_r[...]
        doubled = parts(energies)
        coefficients = fold(dot_nn(jnp.concatenate([doubled, doubled], axis=1), couple_t[...]))
        alpha, beta, p, q, r = advance()
        applied = bw_ref[...] + beta * b_ref[...]
        b_ref[...] = applied
        a = a_ref[...] - alpha * applied
        a_ref[...] = a
        for layout in range(2):
            image = gw_ref[layout] + beta * gq_ref[layout]
            gq_ref[layout] = image
            gr_ref[layout] = gr_ref[layout] - alpha * image
        image = own_ref[...] + beta * cq_ref[...]
        cq_ref[...] = image
        c = c_ref[...] - alpha * image
        c_ref[...] = c
        trace_q = tr_w[...] + beta * tr_q[...]
        tr_q[...] = trace_q
        tr = tr_r[...] - alpha * trace_q
        tr_r[...] = tr
        jump_q_now = jump_w[...] + beta * jump_q[...]
        jump_q[...] = jump_q_now
        jump_now = jump_r[...] - alpha * jump_q_now
        jump_r[...] = jump_now
        sum_zar = row_sum(r * a) + row_sum(tr * jump_now) + row_sum(energies * gr_ref[1])
        sum_rz = row_sum(r * r) + row_sum(energies * c)
        sum_rp = row_sum(r * p)
        sum_zq = row_sum(r * q) + row_sum(energies * image)
        energy = energy_parts()
        traces = tr + fold(dot_nn(energy, trace_t[0 : 2 * DEFL]))
        store_faces(0, traces)
        gather_start(
            step + 1, coefficients + gr_ref[0], energies, (sum_zar, sum_rz, sum_rp, sum_zq)
        )

        start_faces(step, 0)
        x_ref[...] = x_ref[...] + alpha * p
        z_ref[...] = r_ref[...] + fold(dot_nn(energy, defl_t[0 : 2 * DEFL]))
        w_ref[...] = a_ref[...] + fold(dot_nn(energy, image_t[...]))
        jump = take_faces(step, 0, traces)
        w = w_ref[...] + fold(dot_nt(parts(jump), pick[...]))
        w_ref[...] = w
        split = parts(w)
        for block in range(NB):
            blocks_a[block] = split[:, block * TILE : (block + 1) * TILE]

        @pl.when(step < ITERS - 1)
        def _():
            image = fold(dot_nn(split, pick[...]))
            tr_w[...] = image
            store_faces(1, image)
            start_faces(step, 1)

        gather_middle(step + 1)

        @pl.when(step < ITERS - 1)
        def _():
            forward(blocks_a, flex_t, flex_cols, blocks_b)
            forward(blocks_b, stiff_t, stiff_cols, blocks_a)
            middle = backward(blocks_a, stiff_t, stiff_s, spread)
            for block in range(NB):
                blocks_b[block] = parts(middle[block])
            local = backward(blocks_b, flex_t, flex_s, spread)
            image = w_ref[...] + jnp.concatenate(local, axis=1)
            bw_ref[...] = image
            jump = take_faces(step, 1, tr_w[...])
            jump_w[...] = jump
            found = operator_coefficients(image, jump)
            gw_ref[0] = turn(found, place)
            gw_ref[1] = pltpu.roll(found, DEFL, 1)

        gathered = gather_end(step + 1)

        def total(index):
            return gathered[:, 3 * DEFL + index : 3 * DEFL + index + 1]

        new_beta = -total(3) / s1_ref[:, 0:1]
        curvature = total(0) + new_beta * total(3)
        new_alpha = (total(1) + new_beta * total(2)) / curvature
        s1_ref[...] = jnp.broadcast_to(curvature, (LOADS, 128))
        alpha_ref[...] = jnp.broadcast_to(new_alpha, (LOADS, 128))
        beta_ref[...] = jnp.broadcast_to(new_beta, (LOADS, 128))
        energy_q = jnp.where(group8 < 3, gathered, 0.0) + new_beta * e_q[...]
        e_q[...] = energy_q
        e_r[...] = e_r[...] - new_alpha * energy_q
        return carry

    lax.fori_loop(0, ITERS, iterate, 0)
    alpha, _, p, _, r = advance()
    x_ref[...] = x_ref[...] + alpha * p
    z_ref[...] = r + fold(dot_nn(energy_parts(), defl_t[0 : 2 * DEFL]))


def publish(x_in, r_in, z_in, x_out, r_out, z_out):
    x_out[...] = x_in[...]
    r_out[...] = r_in[...]
    z_out[...] = z_in[...]


def shards(rhs, flex, flex_cols, stiff, stiff_cols, defl, coarse, face_rows, face_len):
    anywhere = pl.BlockSpec(memory_space=pl.ANY)
    scalars = pl.BlockSpec(memory_space=pltpu.SMEM)
    vector = pl.BlockSpec(memory_space=pltpu.VMEM)
    field = jax.ShapeDtypeStruct((LOADS, M), F32)
    vmem = pltpu.VMEM
    dma = pltpu.SemaphoreType.DMA
    wide = 2 * (LOADS + DEFL)
    found = pl.pallas_call(
        kernel,
        out_shape=(field, field, field),
        in_specs=[
            anywhere, anywhere, scalars, anywhere, scalars, anywhere, anywhere, anywhere, scalars,
        ],
        out_specs=(vector, vector, vector),
        scratch_shapes=[
            vmem((NB * TPR * TILE, TILE), F32),
            vmem((NB * TPR * TILE, TILE), F32),
            vmem((DEFL, M), F32),
            vmem((DEFL, GRID * KROW), F32),
            vmem((GRID, 2, DEFL, 128), F32),
            vmem((8, DEFL, KROW), F32),
            vmem((8, DEFL, KROW), F32),
            vmem((4, FACE), jnp.int32),
            vmem((NB, TPR * TILE, 2 * TILE), BF16),
            vmem((NB, TPR * TILE, 2 * TILE), BF16),
            vmem((NB * LOADS, NB * TPR * LOADS), BF16),
            vmem((NB * LOADS, NB * TPR * LOADS), BF16),
            vmem((128, M), BF16),
            vmem((2 * DEFL, M), BF16),
            vmem((128, SLOTS), BF16),
            vmem((KROW, KROW // 2), BF16),
            vmem((KROW, KROW // 2), BF16),
            vmem((KROW // 2, KROW), BF16),
            vmem((KROW // 2, KROW), BF16),
            vmem((M, SLOTS), BF16),
            vmem((256, 128), BF16),
            vmem((NB, wide, TILE), BF16),
            vmem((NB, wide, TILE), BF16),
            vmem((wide // 16, NB * TPR * LOADS, 2 * TILE), BF16),
            vmem((NB, 2 * LOADS, TILE), BF16),
            vmem((NB, 2 * LOADS, TILE), BF16),
            vmem((1, NB * TPR * LOADS, 2 * TILE), BF16),
            *[vmem((LOADS, M), F32)] * 6,
            *[vmem((LOADS, SLOTS), F32)] * 6,
            *[vmem((LOADS, 128), F32)] * 5,
            *[vmem((2, LOADS, 128), F32)] * 3,
            *[vmem((LOADS, 128), F32)] * 3,
            vmem((4, LOADS, 128), F32),
            vmem((ITERS + 1, GRID, 2 * LOADS, 128), F32),
            vmem((GRID, LOADS, 128), F32),
            vmem((ITERS + 1, GRID, LOADS, 128), F32),
            vmem((4, LOADS + DEFL, FACE), F32),
            vmem((4, LOADS + DEFL, FACE), F32),
            vmem((2, 4, LOADS, FACE), F32),
            vmem((ITERS, 2, 4, LOADS, FACE), F32),
            dma((12,)),
            dma,
            dma,
            dma,
            dma,
            dma,
            dma((ITERS + 1,)),
            dma,
            dma((ITERS + 1,)),
            dma((4,)),
            dma((4,)),
            dma((2, 4)),
            dma((ITERS, 2, 4)),
        ],
        compiler_params=pltpu.CompilerParams(
            collective_id=0, has_side_effects=True, vmem_limit_bytes=66_500_000
        ),
        name="feti",
    )(rhs, flex, flex_cols.T, stiff, stiff_cols.T, defl, coarse, face_rows, face_len)
    return pl.pallas_call(
        publish,
        out_shape=(field, field, field),
        in_specs=[vector, vector, vector],
        out_specs=(vector, vector, vector),
        compiler_params=pltpu.CompilerParams(vmem_limit_bytes=66_500_000),
        name="publish",
    )(*found)


def solution(mesh):
    return jax.shard_map(
        shards,
        mesh=mesh,
        in_specs=(
            P("row", "col"),
            P("row", "col"),
            P("row", "col"),
            P("row", "col"),
            P("row", "col"),
            P("row", "col"),
            P(("row", "col"), None),
            P("row", "col"),
            P("row", "col"),
        ),
        out_specs=(P("row", "col"), P("row", "col"), P("row", "col")),
        check_vma=False,
    )
```

```python
import functools

import jax
import jax.numpy as jnp
from jax import lax
from jax.experimental import pallas as pl
from jax.experimental.pallas import tpu as pltpu
from jax.sharding import PartitionSpec as P

ITERS = 3
GRID = 16
LOADS = 8
NB = 16
TPR = 4
TILE = 128
M = 2048
DEFL = 32
FACE = 128
SLOTS = 4 * FACE
KROW = GRID * DEFL
MESH = pl.DeviceIdType.MESH
F32 = jnp.float32
BF16 = jnp.bfloat16


def dot_nn(a, b):
    return lax.dot_general(a, b, (((1,), (0,)), ((), ())), preferred_element_type=F32)


def dot_nt(a, b):
    return lax.dot_general(a, b, (((1,), (1,)), ((), ())), preferred_element_type=F32)


def parts(value):
    high = value.astype(BF16).astype(F32)
    return jnp.concatenate([high, value - high], axis=0).astype(BF16)


def fold(value):
    half = value.shape[0] // 2
    return value[:half] + value[half:]


def lane_ids(shape):
    return lax.broadcasted_iota(jnp.int32, shape, 1)


def row_ids(shape):
    return lax.broadcasted_iota(jnp.int32, shape, 0)


def row_sum(value):
    return jnp.sum(value, axis=1, keepdims=True)


def turn(value, place):
    moved = value
    for groups in range(1, 4):
        moved = jnp.where(place == groups, pltpu.roll(value, groups * DEFL, 1), moved)
    return moved


def kernel(
    rhs, flex, flex_cols, stiff, stiff_cols, defl, coarse, face_rows, face_len,
    x_ref, r_ref, z_ref,
    flex_f, stiff_f, defl_f, coarse_own, coarse_f, across_out, across_in, faces,
    flex_t, stiff_t, flex_s, stiff_s, defl_t, image_t, trace_t, coarse_h, coarse_l, across_h, across_l, pick, couple_t,
    wide_a, wide_b, wide_spread, blocks_a, blocks_b, spread,
    a_ref, b_ref, bw_ref, p_ref, q_ref, w_ref, tr_r, tr_w, tr_q, jump_r, jump_w, jump_q,
    e_r, e_q, s1_ref, alpha_ref, beta_ref, gr_ref, gq_ref, gw_ref, own_ref, c_ref, cq_ref,
    row_g, recv1, send2, recv2, first_out, first_in, halo_out, halo_in,
    load_sem, wsend, wrecv, asend, arecv, send1_sem, recv1_sem, send2_sem, recv2_sem, fsend_sem, frecv_sem,
    hsend_sem, hrecv_sem,
):
    i = lax.axis_index("row")
    j = lax.axis_index("col")
    place = j % 4
    pair = j // 4
    odd = (j // 2) % 2
    beside = (pair + 3 + 2 * odd) % 4
    far_groups = ((pair + 2) % 4, (pair + 1 + 2 * odd) % 4)
    chunk = NB * TPR * TILE // 4

    def part_of(ref, index):
        return ref.at[pl.ds(index * chunk, chunk), :]

    load_r = pltpu.make_async_copy(rhs, r_ref, load_sem.at[0])
    load_z = pltpu.make_async_copy(defl, defl_f, load_sem.at[1])
    load_faces = pltpu.make_async_copy(face_rows, faces, load_sem.at[2])
    load_coarse = pltpu.make_async_copy(coarse, coarse_own, load_sem.at[3])
    load_flex = [
        pltpu.make_async_copy(part_of(flex, n), part_of(flex_f, n), load_sem.at[4 + n]) for n in range(4)
    ]
    load_stiff = [
        pltpu.make_async_copy(part_of(stiff, n), part_of(stiff_f, n), load_sem.at[8 + n]) for n in range(4)
    ]

    row_partners = []
    for dy, dx in sorted(
        [(dy, dx) for dy in range(4) for dx in range(4) if dy or dx],
        key=lambda pair: -(min(pair[0], 4 - pair[0]) + min(pair[1], 4 - pair[1])),
    ):
        row_partners.append(((i // 4 + dy) % 4) * 4 + (i % 4 + dx) % 4)
    col_partners = [
        (j + offset) % GRID for offset in sorted(range(1, GRID), key=lambda o: -min(o, GRID - o))
    ]

    load_r.start()
    load_z.start()
    barrier = pltpu.get_barrier_semaphore()
    for there in row_partners:
        pl.semaphore_signal(barrier, inc=1, device_id=(there, j), device_id_type=MESH)
    for there in col_partners:
        pl.semaphore_signal(barrier, inc=1, device_id=(i, there), device_id_type=MESH)
    for load in [load_coarse, load_faces] + load_flex + load_stiff:
        load.start()

    def coarse_lanes(row, group):
        return pl.ds(pl.multiple_of(row * KROW + group * 128, 128), 128)

    def coarse_copy(there, part):
        return pltpu.make_async_remote_copy(
            src_ref=coarse.at[:, coarse_lanes(there, far_groups[part])],
            dst_ref=coarse_f.at[i, part],
            send_sem=wsend,
            recv_sem=wrecv,
            device_id=(there, j),
            device_id_type=MESH,
        )

    lane8 = lane_ids((LOADS, 128))
    group8 = lane8 // DEFL

    def copy1(phase, there):
        return pltpu.make_async_remote_copy(
            src_ref=recv1.at[phase, j],
            dst_ref=recv1.at[phase, j],
            send_sem=send1_sem,
            recv_sem=recv1_sem.at[phase],
            device_id=(i, there),
            device_id_type=MESH,
        )

    def copy2(phase, there):
        return pltpu.make_async_remote_copy(
            src_ref=send2.at[there],
            dst_ref=recv2.at[phase, i],
            send_sem=send2_sem,
            recv_sem=recv2_sem.at[phase],
            device_id=(there, j),
            device_id_type=MESH,
        )

    def whole1(phase):
        slots = recv1.at[phase, pl.ds(0, GRID - 1)]
        return pltpu.make_async_remote_copy(
            src_ref=slots,
            dst_ref=slots,
            send_sem=send1_sem,
            recv_sem=recv1_sem.at[phase],
            device_id=(i, j),
            device_id_type=MESH,
        )

    def whole2(phase):
        return pltpu.make_async_remote_copy(
            src_ref=send2.at[pl.ds(0, GRID - 1)],
            dst_ref=recv2.at[phase, pl.ds(0, GRID - 1)],
            send_sem=send2_sem,
            recv_sem=recv2_sem.at[phase],
            device_id=(i, j),
            device_id_type=MESH,
        )

    def across_copy(piece, there, slot):
        return pltpu.make_async_remote_copy(
            src_ref=across_out.at[piece],
            dst_ref=across_in.at[slot],
            send_sem=asend,
            recv_sem=arecv,
            device_id=(i, there),
            device_id_type=MESH,
        )

    def whole_across():
        return pltpu.make_async_remote_copy(
            src_ref=across_out.at[pl.ds(0, 7)],
            dst_ref=across_in.at[pl.ds(0, 7)],
            send_sem=asend,
            recv_sem=arecv,
            device_id=(i, j),
            device_id_type=MESH,
        )

    def whole_coarse():
        slots = coarse_f.at[pl.ds(0, GRID - 1)]
        return pltpu.make_async_remote_copy(
            src_ref=slots,
            dst_ref=slots,
            send_sem=wsend,
            recv_sem=wrecv,
            device_id=(i, j),
            device_id_type=MESH,
        )

    def gather_start(phase, coefficients, energy, sums):
        recv1[phase, j, 0:LOADS] = coefficients
        second = jnp.where(group8 == 1, energy, 0.0)
        for index, value in enumerate(sums):
            second = jnp.where(lane8 == 3 * DEFL + index, value, second)
        recv1[phase, j, LOADS : 2 * LOADS] = second
        for there in col_partners:
            copy1(phase, there).start()

    def gather_middle(phase, before_matmul=None):
        whole1(phase).wait_recv()
        first = [recv1[phase, source, 0:LOADS] for source in range(GRID)]
        groups = []
        for quarter in range(4):
            gathered = None
            for offset in range(4):
                source = quarter * 4 + offset
                value = first[source]
                if source:
                    value = value + first[source - 1]
                if source < GRID - 1:
                    value = value + first[source + 1]
                gathered = value if gathered is None else jnp.where(group8 == offset, value, gathered)
            groups.append(gathered)
        if before_matmul is not None:
            before_matmul()
        for quarter in range(4):
            row_g[quarter] = groups[quarter]
        near = parts(jnp.concatenate([row_g[pair], row_g[beside]], axis=1))
        far = parts(jnp.concatenate([row_g[far_groups[0]], row_g[far_groups[1]]], axis=1))
        partial = fold(
            dot_nn(near, across_h[...])
            + dot_nn(near, across_l[...])
            + dot_nt(far, coarse_h[...])
            + dot_nt(far, coarse_l[...])
        )
        total = None
        crossed = None
        for quarter in range(4):
            energies = None
            for offset in range(4):
                second = recv1[phase, quarter * 4 + offset, LOADS : 2 * LOADS]
                total = second if total is None else total + second
                shift = ((offset + 3) % 4) * DEFL
                moved = pltpu.roll(second, shift, 1) if shift else second
                energies = moved if energies is None else jnp.where(group8 == offset, moved, energies)
            crossed = groups[quarter] * energies + (0.0 if crossed is None else crossed)
        total = total + jnp.where(lane8 == 3 * DEFL, row_sum(crossed), 0.0)
        tiles = [partial[:, n * 128 : (n + 1) * 128] for n in range(4)]
        turned = [
            [tile if not n else pltpu.roll(tile, 128 - n * DEFL, 1) for n in range(4)] for tile in tiles
        ]
        for target in range(GRID):
            before = (target + GRID - 1) % GRID
            quarter, offset = before // 4, before % 4
            value = turned[quarter][offset]
            if offset > 1:
                value = jnp.where(group8 < 4 - offset, value, turned[(quarter + 1) % 4][offset])
            send2[target] = jnp.where(group8 < 3, value, total)
        for there in row_partners:
            copy2(phase, there).start()
        recv2[phase, i] = send2[i]
        mine = jnp.where(group8 == place, row_g[j // 4], 0.0)
        own_ref[...] = turn(mine, (5 - place) % 4)

    def gather_end(phase):
        whole2(phase).wait_recv()
        level = [recv2[phase, source] for source in range(GRID)]
        while len(level) > 1:
            level = [level[n] + level[n + 1] for n in range(0, len(level), 2)]
        whole1(phase).wait_send()
        whole2(phase).wait_send()
        return level[0]

    def coefficients_of(product):
        summed = fold(product)
        summed = summed + pltpu.roll(summed, 128 - DEFL, 1)
        return jnp.where(lane8 < DEFL, summed, 0.0)

    load_r.wait()
    load_z.wait()
    defl_high = defl_f[...].astype(BF16)
    defl_low = (defl_f[...] - defl_high.astype(F32)).astype(BF16)
    defl_t[0:DEFL] = defl_high
    defl_t[DEFL : 2 * DEFL] = defl_low
    defl_t[2 * DEFL :] = jnp.zeros((128 - 2 * DEFL, M), BF16)
    started = coefficients_of(dot_nt(parts(r_ref[...]), defl_t[...]))
    c_ref[...] = pltpu.roll(started, DEFL, 1)
    load_coarse.wait()
    group32 = lane_ids((DEFL, 128)) // DEFL
    after, ahead = (pair + 1) % 4, (pair + 3) % 4
    for piece, (group, spot) in enumerate(
        [(pair, 0), (pair, 1), (pair, 2), (pair, 3), (after, 0), (after, 1), (ahead, 2), (ahead, 3)]
    ):
        for quarter in range(4):
            packed = None
            for offset in range(4):
                value = coarse_own[:, coarse_lanes(quarter * 4 + offset, group)]
                shift = ((offset - spot) % 4) * DEFL
                if shift:
                    value = pltpu.roll(value, shift, 1)
                packed = value if packed is None else jnp.where(group32 == offset, value, packed)
            across_out[piece, :, quarter * 128 : (quarter + 1) * 128] = packed
    pl.semaphore_wait(barrier, 2 * (GRID - 1))
    for piece, there in ((4, after * 4), (5, after * 4 + 1), (6, ahead * 4 + 2), (7, ahead * 4 + 3)):
        across_copy(piece, there, 4 + place).start()
    for step in range(1, 4):
        other = (place + step) % 4
        across_copy(other, pair * 4 + other, place).start()
    for there in row_partners:
        for part in range(2):
            coarse_copy(there, part).start()
    gather_start(0, turn(started, place), jnp.zeros((LOADS, 128), F32), ())

    across_in[place] = across_out[place]
    for part in range(2):
        coarse_f[i, part] = coarse_own[:, coarse_lanes(i, far_groups[part])]

    sides = (
        (i > 0, (i - 1, j), 1),
        (i < GRID - 1, (i + 1, j), 0),
        (j > 0, (i, j - 1), 3),
        (j < GRID - 1, (i, j + 1), 2),
    )

    def first_copy(face, device, slot):
        return pltpu.make_async_remote_copy(
            src_ref=first_out.at[face],
            dst_ref=first_in.at[slot],
            send_sem=fsend_sem.at[face],
            recv_sem=frecv_sem.at[slot],
            device_id=device,
            device_id_type=MESH,
        )

    def face_copy(step, kind, face, device, slot):
        return pltpu.make_async_remote_copy(
            src_ref=halo_out.at[kind, face],
            dst_ref=halo_in.at[step, kind, slot],
            send_sem=hsend_sem.at[kind, face],
            recv_sem=hrecv_sem.at[step, kind, slot],
            device_id=device,
            device_id_type=MESH,
        )

    def store_faces(kind, traces):
        for face in range(4):
            halo_out[kind, face] = traces[:, face * FACE : (face + 1) * FACE]

    def start_faces(step, kind):
        for face, (inside, device, slot) in enumerate(sides):

            @pl.when(inside)
            def _():
                face_copy(step, kind, face, device, slot).start()

    def take_faces(step, kind, traces):
        for face, (inside, device, slot) in enumerate(sides):

            @pl.when(inside)
            def _():
                face_copy(step, kind, slot, device, face).wait_recv()
                face_copy(step, kind, face, device, slot).wait_send()

        partner = jnp.concatenate([halo_in[step, kind, face] for face in range(4)], axis=1)
        return jnp.where(live > 0.5, traces - partner, 0.0)

    live = jnp.concatenate(
        [jnp.where(lane8 < face_len[0, face], 1.0, 0.0) for face in range(4)], axis=1
    )
    load_faces.wait()

    def build_pick(block, carry):
        start = pl.multiple_of(block * TILE, TILE)
        rows = row_ids((TILE, FACE)) + start
        for face in range(4):
            hit = rows == faces[face : face + 1, :]
            pick[pl.ds(start, TILE), face * FACE : (face + 1) * FACE] = jnp.where(hit, 1.0, 0.0).astype(BF16)
        return carry

    lax.fori_loop(0, NB, build_pick, 0)
    wide = LOADS + DEFL
    basis = parts(jnp.concatenate([r_ref[...], defl_f[...]], axis=0))
    for block in range(NB):
        wide_a[block] = basis[:, block * TILE : (block + 1) * TILE]
    both = fold(dot_nn(basis, pick[...]))
    tr_r[...] = both[0:LOADS]
    trace_t[0 : 2 * DEFL] = parts(both[LOADS:])
    trace_t[2 * DEFL :] = jnp.zeros((128 - 2 * DEFL, SLOTS), BF16)
    for face in range(4):
        first_out[face] = both[:, face * FACE : (face + 1) * FACE]
    for face, (inside, device, slot) in enumerate(sides):

        @pl.when(inside)
        def _():
            first_copy(face, device, slot).start()

    def build_spread(columns, target):
        lanes = lane_ids((LOADS, 128))
        rows = row_ids((NB * LOADS, 128))
        across = lane_ids((NB * LOADS, 128))
        for tile in range(4):
            named = jnp.zeros((LOADS, 128), jnp.int32)
            for spot in range(16):
                index = tile * 16 + spot
                named = jnp.where(lanes // LOADS == spot, columns[index % TPR, index // TPR], named)
            hit = (rows // LOADS == named[0:1, :]) & (rows % LOADS == across % LOADS)
            target[:, tile * 128 : (tile + 1) * 128] = jnp.where(hit, 1.0, 0.0).astype(BF16)

    build_spread(flex_cols, flex_s)
    build_spread(stiff_cols, stiff_s)

    def convert(pending, source, target):
        for n, load in enumerate(pending):
            load.wait()

            def one(block, carry):
                tiles = source[pl.ds(pl.multiple_of(block * TPR * TILE, TPR * TILE), TPR * TILE), :]
                high = tiles.astype(BF16)
                target[block, :, 0:TILE] = high
                target[block, :, TILE : 2 * TILE] = (tiles - high.astype(F32)).astype(BF16)
                return carry

            lax.fori_loop(n * NB // 4, (n + 1) * NB // 4, one, 0)

    convert(load_flex, flex_f, flex_t)
    convert(load_stiff, stiff_f, stiff_t)

    def coarse_ready():
        whole_across().wait_recv()

        def one_across(block, carry):
            rows = across_in[block]
            high = rows.astype(BF16)
            start = pl.multiple_of(block * DEFL, DEFL)
            across_h[pl.ds(start, DEFL), :] = high
            across_l[pl.ds(start, DEFL), :] = (rows - high.astype(F32)).astype(BF16)
            return carry

        lax.fori_loop(0, 8, one_across, 0)
        whole_coarse().wait_recv()

        def one(block, carry):
            start = pl.multiple_of(block * DEFL, DEFL)
            for part in range(2):
                rows = coarse_f[block, part]
                high = rows.astype(BF16)
                lanes = slice(part * 128, (part + 1) * 128)
                coarse_h[pl.ds(start, DEFL), lanes] = high
                coarse_l[pl.ds(start, DEFL), lanes] = (rows - high.astype(F32)).astype(BF16)
            return carry

        lax.fori_loop(0, GRID, one, 0)

    def forward(source, tiles, columns, target):
        for block in range(NB):
            operand = jnp.concatenate([source[columns[k, block]] for k in range(TPR)], axis=1)
            product = fold(dot_nn(operand, tiles[block]))
            target[block] = parts(product[:, 0:TILE] + product[:, TILE : 2 * TILE])

    def backward(source, tiles, selector, space):
        groups = space.shape[0]
        for block in range(NB):
            piece = source[block]
            product = fold(dot_nt(jnp.concatenate([piece, piece], axis=1), tiles[block]))
            rows = slice(block * TPR * LOADS, (block + 1) * TPR * LOADS)
            for group in range(groups):
                loads = product[group * LOADS : (group + 1) * LOADS]
                stacked = jnp.concatenate(
                    [loads[:, k * TILE : (k + 1) * TILE] for k in range(TPR)], axis=0
                )
                high = stacked.astype(BF16)
                space[group, rows, 0:TILE] = high
                space[group, rows, TILE : 2 * TILE] = (stacked - high.astype(F32)).astype(BF16)
        summed = []
        for group in range(groups):
            product = dot_nn(selector[...], space[group])
            summed.append(product[:, 0:TILE] + product[:, TILE : 2 * TILE])
        return [
            jnp.concatenate([one[block * LOADS : (block + 1) * LOADS] for one in summed], axis=0)
            for block in range(NB)
        ]

    forward(wide_a, flex_t, flex_cols, wide_b)
    forward(wide_b, stiff_t, stiff_cols, wide_a)
    gather_middle(0, coarse_ready)
    middle = backward(wide_a, stiff_t, stiff_s, wide_spread)
    for block in range(NB):
        wide_b[block] = parts(middle[block])
    applied = backward(wide_b, flex_t, flex_s, wide_spread)
    for block in range(NB):
        span = slice(block * TILE, (block + 1) * TILE)
        a_ref[:, span] = r_ref[:, span] + applied[block][0:LOADS]
        image_t[0 : 2 * DEFL, span] = parts(defl_f[:, span] + applied[block][LOADS:wide])
    image_t[2 * DEFL :] = jnp.zeros((128 - 2 * DEFL, M), BF16)

    for face, (inside, device, slot) in enumerate(sides):

        @pl.when(inside)
        def _():
            first_copy(slot, device, face).wait_recv()
            first_copy(face, device, slot).wait_send()

    def operator_coefficients(field, jump):
        return coefficients_of(dot_nt(parts(field), defl_t[...]) + dot_nt(parts(jump), trace_t[...]))

    partner = jnp.concatenate([first_in[face, 0:LOADS] for face in range(4)], axis=1)
    jump = jnp.where(live > 0.5, tr_r[...] - partner, 0.0)
    jump_r[...] = jump
    found = operator_coefficients(a_ref[...], jump)
    gr_ref[0] = turn(found, place)
    gr_ref[1] = pltpu.roll(found, DEFL, 1)

    traces = [first_out[face, LOADS:wide] for face in range(4)]
    others = [
        jnp.where(live[0:1, face * FACE : (face + 1) * FACE] > 0.5, first_in[face, LOADS:wide], 0.0)
        for face in range(4)
    ]
    masked = [
        jnp.where(live[0:1, face * FACE : (face + 1) * FACE] > 0.5, traces[face], 0.0)
        for face in range(4)
    ]
    lane32 = lane_ids((DEFL, 128))

    def paired(product):
        summed = fold(product)
        summed = summed + pltpu.roll(summed, 128 - DEFL, 1)
        return jnp.where(lane32 < DEFL, summed, 0.0)

    def against(value):
        return jnp.concatenate([parts(value), jnp.zeros((2 * DEFL, FACE), BF16)], axis=0)

    own = dot_nt(image_t[0 : 2 * DEFL], defl_t[...])
    for face in range(4):
        own = own + dot_nt(parts(masked[face]), trace_t[:, face * FACE : (face + 1) * FACE])
    north = paired(dot_nt(parts(others[0]), trace_t[:, 0:FACE]))
    south = paired(dot_nt(parts(others[1]), trace_t[:, FACE : 2 * FACE]))
    west = paired(dot_nt(parts(masked[2]), against(others[2])))
    east = paired(dot_nt(parts(masked[3]), against(others[3])))
    couple = jnp.concatenate(
        [
            -turn(north, place),
            turn(paired(own), place) - turn(west, (place + 3) % 4) - turn(east, (place + 1) % 4),
            -turn(south, place),
            jnp.zeros((DEFL, 128), F32),
        ],
        axis=0,
    )
    couple_t[...] = parts(couple)

    zeros = jnp.zeros((LOADS, M), F32)
    for ref in (b_ref, bw_ref, p_ref, q_ref, w_ref, x_ref, z_ref):
        ref[...] = zeros
    short = jnp.zeros((LOADS, SLOTS), F32)
    for ref in (tr_w, tr_q, jump_w, jump_q):
        ref[...] = short
    none = jnp.zeros((LOADS, 128), F32)
    for ref in (e_q, alpha_ref, beta_ref, cq_ref):
        ref[...] = none
    for layout in range(2):
        gq_ref[layout] = none
        gw_ref[layout] = none
    s1_ref[...] = jnp.ones((LOADS, 128), F32)

    e_r[...] = jnp.where(group8 < 3, gather_end(0), 0.0)
    own_ref[...] = none
    whole_coarse().wait_send()
    whole_across().wait_send()

    def energy_parts():
        energy = jnp.where(group8 == 1, e_r[...], 0.0)
        return parts(energy + pltpu.roll(energy, 128 - DEFL, 1))[:, 0 : 2 * DEFL]

    def advance():
        alpha = alpha_ref[:, 0:1]
        beta = beta_ref[:, 0:1]
        direction = z_ref[...] + beta * p_ref[...]
        image = w_ref[...] + beta * q_ref[...]
        p_ref[...] = direction
        q_ref[...] = image
        residual = r_ref[...] - alpha * image
        r_ref[...] = residual
        return alpha, beta, direction, image, residual

    def iterate(step, carry):
        energies = e_r[...]
        doubled = parts(energies)
        coefficients = fold(dot_nn(jnp.concatenate([doubled, doubled], axis=1), couple_t[...]))
        alpha, beta, p, q, r = advance()
        applied = bw_ref[...] + beta * b_ref[...]
        b_ref[...] = applied
        a = a_ref[...] - alpha * applied
        a_ref[...] = a
        for layout in range(2):
            image = gw_ref[layout] + beta * gq_ref[layout]
            gq_ref[layout] = image
            gr_ref[layout] = gr_ref[layout] - alpha * image
        image = own_ref[...] + beta * cq_ref[...]
        cq_ref[...] = image
        c = c_ref[...] - alpha * image
        c_ref[...] = c
        trace_q = tr_w[...] + beta * tr_q[...]
        tr_q[...] = trace_q
        tr = tr_r[...] - alpha * trace_q
        tr_r[...] = tr
        jump_q_now = jump_w[...] + beta * jump_q[...]
        jump_q[...] = jump_q_now
        jump_now = jump_r[...] - alpha * jump_q_now
        jump_r[...] = jump_now
        sum_zar = row_sum(r * a) + row_sum(tr * jump_now) + row_sum(energies * gr_ref[1])
        sum_rz = row_sum(r * r) + row_sum(energies * c)
        sum_rp = row_sum(r * p)
        sum_zq = row_sum(r * q) + row_sum(energies * image)
        energy = energy_parts()
        traces = tr + fold(dot_nn(energy, trace_t[0 : 2 * DEFL]))
        store_faces(0, traces)
        gather_start(
            step + 1, coefficients + gr_ref[0], energies, (sum_zar, sum_rz, sum_rp, sum_zq)
        )

        start_faces(step, 0)
        x_ref[...] = x_ref[...] + alpha * p
        z_ref[...] = r_ref[...] + fold(dot_nn(energy, defl_t[0 : 2 * DEFL]))
        w_ref[...] = a_ref[...] + fold(dot_nn(energy, image_t[0 : 2 * DEFL]))
        jump = take_faces(step, 0, traces)
        w = w_ref[...] + fold(dot_nt(parts(jump), pick[...]))
        w_ref[...] = w
        split = parts(w)
        for block in range(NB):
            blocks_a[block] = split[:, block * TILE : (block + 1) * TILE]

        @pl.when(step < ITERS - 1)
        def _():
            image = fold(dot_nn(split, pick[...]))
            tr_w[...] = image
            store_faces(1, image)
            start_faces(step, 1)

        gather_middle(step + 1)

        @pl.when(step < ITERS - 1)
        def _():
            forward(blocks_a, flex_t, flex_cols, blocks_b)
            forward(blocks_b, stiff_t, stiff_cols, blocks_a)
            middle = backward(blocks_a, stiff_t, stiff_s, spread)
            for block in range(NB):
                blocks_b[block] = parts(middle[block])
            jump = take_faces(step, 1, tr_w[...])
            jump_w[...] = jump
            found = coefficients_of(
                dot_nt(split, image_t[...]) + dot_nt(parts(jump), trace_t[...])
            )
            gw_ref[0] = turn(found, place)
            gw_ref[1] = pltpu.roll(found, DEFL, 1)
            local = backward(blocks_b, flex_t, flex_s, spread)
            bw_ref[...] = w_ref[...] + jnp.concatenate(local, axis=1)

        gathered = gather_end(step + 1)

        def total(index):
            return gathered[:, 3 * DEFL + index : 3 * DEFL + index + 1]

        new_beta = -total(3) / s1_ref[:, 0:1]
        curvature = total(0) + new_beta * total(3)
        new_alpha = (total(1) + new_beta * total(2)) / curvature
        s1_ref[...] = jnp.broadcast_to(curvature, (LOADS, 128))
        alpha_ref[...] = jnp.broadcast_to(new_alpha, (LOADS, 128))
        beta_ref[...] = jnp.broadcast_to(new_beta, (LOADS, 128))
        energy_q = jnp.where(group8 < 3, gathered, 0.0) + new_beta * e_q[...]
        e_q[...] = energy_q
        e_r[...] = e_r[...] - new_alpha * energy_q
        return carry

    lax.fori_loop(0, ITERS, iterate, 0)
    alpha, _, p, _, r = advance()
    x_ref[...] = x_ref[...] + alpha * p
    z_ref[...] = r + fold(dot_nn(energy_parts(), defl_t[0 : 2 * DEFL]))


def publish(x_in, r_in, z_in, x_out, r_out, z_out):
    x_out[...] = x_in[...]
    r_out[...] = r_in[...]
    z_out[...] = z_in[...]


def shards(rhs, flex, flex_cols, stiff, stiff_cols, defl, coarse, face_rows, face_len):
    anywhere = pl.BlockSpec(memory_space=pl.ANY)
    scalars = pl.BlockSpec(memory_space=pltpu.SMEM)
    vector = pl.BlockSpec(memory_space=pltpu.VMEM)
    field = jax.ShapeDtypeStruct((LOADS, M), F32)
    vmem = pltpu.VMEM
    dma = pltpu.SemaphoreType.DMA
    wide = 2 * (LOADS + DEFL)
    found = pl.pallas_call(
        kernel,
        out_shape=(field, field, field),
        in_specs=[
            anywhere, anywhere, scalars, anywhere, scalars, anywhere, anywhere, anywhere, scalars,
        ],
        out_specs=(vector, vector, vector),
        scratch_shapes=[
            vmem((NB * TPR * TILE, TILE), F32),
            vmem((NB * TPR * TILE, TILE), F32),
            vmem((DEFL, M), F32),
            vmem((DEFL, GRID * KROW), F32),
            vmem((GRID, 2, DEFL, 128), F32),
            vmem((8, DEFL, KROW), F32),
            vmem((8, DEFL, KROW), F32),
            vmem((4, FACE), jnp.int32),
            vmem((NB, TPR * TILE, 2 * TILE), BF16),
            vmem((NB, TPR * TILE, 2 * TILE), BF16),
            vmem((NB * LOADS, NB * TPR * LOADS), BF16),
            vmem((NB * LOADS, NB * TPR * LOADS), BF16),
            vmem((128, M), BF16),
            vmem((128, M), BF16),
            vmem((128, SLOTS), BF16),
            vmem((KROW, KROW // 2), BF16),
            vmem((KROW, KROW // 2), BF16),
            vmem((KROW // 2, KROW), BF16),
            vmem((KROW // 2, KROW), BF16),
            vmem((M, SLOTS), BF16),
            vmem((256, 128), BF16),
            vmem((NB, wide, TILE), BF16),
            vmem((NB, wide, TILE), BF16),
            vmem((wide // 16, NB * TPR * LOADS, 2 * TILE), BF16),
            vmem((NB, 2 * LOADS, TILE), BF16),
            vmem((NB, 2 * LOADS, TILE), BF16),
            vmem((1, NB * TPR * LOADS, 2 * TILE), BF16),
            *[vmem((LOADS, M), F32)] * 6,
            *[vmem((LOADS, SLOTS), F32)] * 6,
            *[vmem((LOADS, 128), F32)] * 5,
            *[vmem((2, LOADS, 128), F32)] * 3,
            *[vmem((LOADS, 128), F32)] * 3,
            vmem((4, LOADS, 128), F32),
            vmem((ITERS + 1, GRID, 2 * LOADS, 128), F32),
            vmem((GRID, LOADS, 128), F32),
            vmem((ITERS + 1, GRID, LOADS, 128), F32),
            vmem((4, LOADS + DEFL, FACE), F32),
            vmem((4, LOADS + DEFL, FACE), F32),
            vmem((2, 4, LOADS, FACE), F32),
            vmem((ITERS, 2, 4, LOADS, FACE), F32),
            dma((12,)),
            dma,
            dma,
            dma,
            dma,
            dma,
            dma((ITERS + 1,)),
            dma,
            dma((ITERS + 1,)),
            dma((4,)),
            dma((4,)),
            dma((2, 4)),
            dma((ITERS, 2, 4)),
        ],
        compiler_params=pltpu.CompilerParams(
            collective_id=0, has_side_effects=True, vmem_limit_bytes=66_500_000
        ),
        name="feti",
    )(rhs, flex, flex_cols.T, stiff, stiff_cols.T, defl, coarse, face_rows, face_len)
    return pl.pallas_call(
        publish,
        out_shape=(field, field, field),
        in_specs=[vector, vector, vector],
        out_specs=(vector, vector, vector),
        compiler_params=pltpu.CompilerParams(vmem_limit_bytes=66_500_000),
        name="publish",
    )(*found)


def solution(mesh):
    return jax.shard_map(
        shards,
        mesh=mesh,
        in_specs=(
            P("row", "col"),
            P("row", "col"),
            P("row", "col"),
            P("row", "col"),
            P("row", "col"),
            P("row", "col"),
            P(("row", "col"), None),
            P("row", "col"),
            P("row", "col"),
        ),
        out_specs=(P("row", "col"), P("row", "col"), P("row", "col")),
        check_vma=False,
    )
```

```python
import functools

import jax
import jax.numpy as jnp
from jax import lax
from jax.experimental import pallas as pl
from jax.experimental.pallas import tpu as pltpu
from jax.sharding import PartitionSpec as P

ITERS = 3
GRID = 16
LOADS = 8
NB = 16
TPR = 4
TILE = 128
M = 2048
DEFL = 32
FACE = 128
SLOTS = 4 * FACE
KROW = GRID * DEFL
MESH = pl.DeviceIdType.MESH
F32 = jnp.float32
BF16 = jnp.bfloat16


def dot_nn(a, b):
    return lax.dot_general(a, b, (((1,), (0,)), ((), ())), preferred_element_type=F32)


def dot_nt(a, b):
    return lax.dot_general(a, b, (((1,), (1,)), ((), ())), preferred_element_type=F32)


def parts(value):
    high = value.astype(BF16).astype(F32)
    return jnp.concatenate([high, value - high], axis=0).astype(BF16)


def fold(value):
    half = value.shape[0] // 2
    return value[:half] + value[half:]


def lane_ids(shape):
    return lax.broadcasted_iota(jnp.int32, shape, 1)


def row_ids(shape):
    return lax.broadcasted_iota(jnp.int32, shape, 0)


def row_sum(value):
    return jnp.sum(value, axis=1, keepdims=True)


def turn(value, place):
    moved = value
    for groups in range(1, 4):
        moved = jnp.where(place == groups, pltpu.roll(value, groups * DEFL, 1), moved)
    return moved


def kernel(
    rhs, flex, flex_cols, stiff, stiff_cols, defl, coarse, face_rows, face_len,
    x_ref, r_ref, z_ref,
    flex_f, stiff_f, defl_f, coarse_own, coarse_f, across_out, across_in, faces,
    flex_t, stiff_t, flex_s, stiff_s, defl_t, image_t, trace_t, coarse_h, coarse_l, across_h, across_l, pick, couple_t,
    wide_a, wide_b, wide_spread, blocks_a, blocks_b, spread,
    a_ref, b_ref, bw_ref, p_ref, q_ref, w_ref, tr_r, tr_w, tr_q, jump_r, jump_w, jump_q,
    e_r, e_q, s1_ref, alpha_ref, beta_ref, gr_ref, gq_ref, gw_ref, own_ref, c_ref, cq_ref,
    row_g, recv1, send2, recv2, first_out, first_in, halo_out, halo_in,
    load_sem, wsend, wrecv, asend, arecv, send1_sem, recv1_sem, send2_sem, recv2_sem, fsend_sem, frecv_sem,
    hsend_sem, hrecv_sem,
):
    i = lax.axis_index("row")
    j = lax.axis_index("col")
    place = j % 4
    pair = j // 4
    odd = (j // 2) % 2
    beside = (pair + 3 + 2 * odd) % 4
    far_groups = ((pair + 2) % 4, (pair + 1 + 2 * odd) % 4)
    chunk = NB * TPR * TILE // 4

    def part_of(ref, index):
        return ref.at[pl.ds(index * chunk, chunk), :]

    load_r = pltpu.make_async_copy(rhs, r_ref, load_sem.at[0])
    load_z = pltpu.make_async_copy(defl, defl_f, load_sem.at[1])
    load_faces = pltpu.make_async_copy(face_rows, faces, load_sem.at[2])
    load_coarse = pltpu.make_async_copy(coarse, coarse_own, load_sem.at[3])
    load_flex = [
        pltpu.make_async_copy(part_of(flex, n), part_of(flex_f, n), load_sem.at[4 + n]) for n in range(4)
    ]
    load_stiff = [
        pltpu.make_async_copy(part_of(stiff, n), part_of(stiff_f, n), load_sem.at[8 + n]) for n in range(4)
    ]

    row_partners = []
    for dy, dx in sorted(
        [(dy, dx) for dy in range(4) for dx in range(4) if dy or dx],
        key=lambda pair: -(min(pair[0], 4 - pair[0]) + min(pair[1], 4 - pair[1])),
    ):
        row_partners.append(((i // 4 + dy) % 4) * 4 + (i % 4 + dx) % 4)
    col_partners = [
        (j + offset) % GRID for offset in sorted(range(1, GRID), key=lambda o: -min(o, GRID - o))
    ]

    load_r.start()
    load_z.start()
    barrier = pltpu.get_barrier_semaphore()
    for there in row_partners:
        pl.semaphore_signal(barrier, inc=1, device_id=(there, j), device_id_type=MESH)
    for there in col_partners:
        pl.semaphore_signal(barrier, inc=1, device_id=(i, there), device_id_type=MESH)
    for load in [load_coarse, load_faces] + load_flex + load_stiff:
        load.start()

    def coarse_lanes(row, group):
        return pl.ds(pl.multiple_of(row * KROW + group * 128, 128), 128)

    def coarse_copy(there, part):
        return pltpu.make_async_remote_copy(
            src_ref=coarse.at[:, coarse_lanes(there, far_groups[part])],
            dst_ref=coarse_f.at[i, part],
            send_sem=wsend,
            recv_sem=wrecv,
            device_id=(there, j),
            device_id_type=MESH,
        )

    lane8 = lane_ids((LOADS, 128))
    group8 = lane8 // DEFL

    def copy1(phase, there):
        return pltpu.make_async_remote_copy(
            src_ref=recv1.at[phase, j],
            dst_ref=recv1.at[phase, j],
            send_sem=send1_sem,
            recv_sem=recv1_sem.at[phase],
            device_id=(i, there),
            device_id_type=MESH,
        )

    def copy2(phase, there):
        return pltpu.make_async_remote_copy(
            src_ref=send2.at[there],
            dst_ref=recv2.at[phase, i],
            send_sem=send2_sem,
            recv_sem=recv2_sem.at[phase],
            device_id=(there, j),
            device_id_type=MESH,
        )

    def whole1(phase):
        slots = recv1.at[phase, pl.ds(0, GRID - 1)]
        return pltpu.make_async_remote_copy(
            src_ref=slots,
            dst_ref=slots,
            send_sem=send1_sem,
            recv_sem=recv1_sem.at[phase],
            device_id=(i, j),
            device_id_type=MESH,
        )

    def whole2(phase):
        return pltpu.make_async_remote_copy(
            src_ref=send2.at[pl.ds(0, GRID - 1)],
            dst_ref=recv2.at[phase, pl.ds(0, GRID - 1)],
            send_sem=send2_sem,
            recv_sem=recv2_sem.at[phase],
            device_id=(i, j),
            device_id_type=MESH,
        )

    def across_copy(piece, there, slot):
        return pltpu.make_async_remote_copy(
            src_ref=across_out.at[piece],
            dst_ref=across_in.at[slot],
            send_sem=asend,
            recv_sem=arecv,
            device_id=(i, there),
            device_id_type=MESH,
        )

    def whole_across():
        return pltpu.make_async_remote_copy(
            src_ref=across_out.at[pl.ds(0, 7)],
            dst_ref=across_in.at[pl.ds(0, 7)],
            send_sem=asend,
            recv_sem=arecv,
            device_id=(i, j),
            device_id_type=MESH,
        )

    def whole_coarse():
        slots = coarse_f.at[pl.ds(0, GRID - 1)]
        return pltpu.make_async_remote_copy(
            src_ref=slots,
            dst_ref=slots,
            send_sem=wsend,
            recv_sem=wrecv,
            device_id=(i, j),
            device_id_type=MESH,
        )

    def gather_start(phase, coefficients, energy, sums):
        recv1[phase, j, 0:LOADS] = coefficients
        second = jnp.where(group8 == 1, energy, 0.0)
        for index, value in enumerate(sums):
            second = jnp.where(lane8 == 3 * DEFL + index, value, second)
        recv1[phase, j, LOADS : 2 * LOADS] = second
        for there in col_partners:
            copy1(phase, there).start()

    def gather_middle(phase, before_matmul=None):
        whole1(phase).wait_recv()
        first = [recv1[phase, source, 0:LOADS] for source in range(GRID)]
        groups = []
        for quarter in range(4):
            gathered = None
            for offset in range(4):
                source = quarter * 4 + offset
                value = first[source]
                if source:
                    value = value + first[source - 1]
                if source < GRID - 1:
                    value = value + first[source + 1]
                gathered = value if gathered is None else jnp.where(group8 == offset, value, gathered)
            groups.append(gathered)
        if before_matmul is not None:
            before_matmul()
        for quarter in range(4):
            row_g[quarter] = groups[quarter]
        near = parts(jnp.concatenate([row_g[pair], row_g[beside]], axis=1))
        far = parts(jnp.concatenate([row_g[far_groups[0]], row_g[far_groups[1]]], axis=1))
        partial = fold(
            dot_nn(near, across_h[...])
            + dot_nn(near, across_l[...])
            + dot_nt(far, coarse_h[...])
            + dot_nt(far, coarse_l[...])
        )
        total = None
        crossed = None
        for quarter in range(4):
            energies = None
            for offset in range(4):
                second = recv1[phase, quarter * 4 + offset, LOADS : 2 * LOADS]
                total = second if total is None else total + second
                shift = ((offset + 3) % 4) * DEFL
                moved = pltpu.roll(second, shift, 1) if shift else second
                energies = moved if energies is None else jnp.where(group8 == offset, moved, energies)
            crossed = groups[quarter] * energies + (0.0 if crossed is None else crossed)
        total = total + jnp.where(lane8 == 3 * DEFL, row_sum(crossed), 0.0)
        tiles = [partial[:, n * 128 : (n + 1) * 128] for n in range(4)]
        turned = [
            [tile if not n else pltpu.roll(tile, 128 - n * DEFL, 1) for n in range(4)] for tile in tiles
        ]
        for target in range(GRID):
            before = (target + GRID - 1) % GRID
            quarter, offset = before // 4, before % 4
            value = turned[quarter][offset]
            if offset > 1:
                value = jnp.where(group8 < 4 - offset, value, turned[(quarter + 1) % 4][offset])
            send2[target] = jnp.where(group8 < 3, value, total)
        for there in row_partners:
            copy2(phase, there).start()
        recv2[phase, i] = send2[i]
        mine = jnp.where(group8 == place, row_g[j // 4], 0.0)
        own_ref[...] = turn(mine, (5 - place) % 4)

    def gather_end(phase):
        whole2(phase).wait_recv()
        level = [recv2[phase, source] for source in range(GRID)]
        while len(level) > 1:
            level = [level[n] + level[n + 1] for n in range(0, len(level), 2)]
        whole1(phase).wait_send()
        whole2(phase).wait_send()
        return level[0]

    def coefficients_of(product):
        summed = fold(product)
        summed = summed + pltpu.roll(summed, 128 - DEFL, 1)
        return jnp.where(lane8 < DEFL, summed, 0.0)

    load_r.wait()
    load_z.wait()
    defl_high = defl_f[...].astype(BF16)
    defl_low = (defl_f[...] - defl_high.astype(F32)).astype(BF16)
    defl_t[0:DEFL] = defl_high
    defl_t[DEFL : 2 * DEFL] = defl_low
    defl_t[2 * DEFL :] = jnp.zeros((128 - 2 * DEFL, M), BF16)
    started = coefficients_of(dot_nt(parts(r_ref[...]), defl_t[...]))
    c_ref[...] = pltpu.roll(started, DEFL, 1)
    pl.semaphore_wait(barrier, 2 * (GRID - 1))
    for there in row_partners:
        for part in range(2):
            coarse_copy(there, part).start()
    gather_start(0, turn(started, place), jnp.zeros((LOADS, 128), F32), ())

    load_coarse.wait()
    group32 = lane_ids((DEFL, 128)) // DEFL
    after, ahead = (pair + 1) % 4, (pair + 3) % 4
    for piece, (group, spot) in enumerate(
        [(pair, 0), (pair, 1), (pair, 2), (pair, 3), (after, 0), (after, 1), (ahead, 2), (ahead, 3)]
    ):
        for quarter in range(4):
            packed = None
            for offset in range(4):
                value = coarse_own[:, coarse_lanes(quarter * 4 + offset, group)]
                shift = ((offset - spot) % 4) * DEFL
                if shift:
                    value = pltpu.roll(value, shift, 1)
                packed = value if packed is None else jnp.where(group32 == offset, value, packed)
            across_out[piece, :, quarter * 128 : (quarter + 1) * 128] = packed
    for piece, there in ((4, after * 4), (5, after * 4 + 1), (6, ahead * 4 + 2), (7, ahead * 4 + 3)):
        across_copy(piece, there, 4 + place).start()
    for step in range(1, 4):
        other = (place + step) % 4
        across_copy(other, pair * 4 + other, place).start()
    across_in[place] = across_out[place]
    for part in range(2):
        coarse_f[i, part] = coarse_own[:, coarse_lanes(i, far_groups[part])]

    sides = (
        (i > 0, (i - 1, j), 1),
        (i < GRID - 1, (i + 1, j), 0),
        (j > 0, (i, j - 1), 3),
        (j < GRID - 1, (i, j + 1), 2),
    )

    def first_copy(face, device, slot):
        return pltpu.make_async_remote_copy(
            src_ref=first_out.at[face],
            dst_ref=first_in.at[slot],
            send_sem=fsend_sem.at[face],
            recv_sem=frecv_sem.at[slot],
            device_id=device,
            device_id_type=MESH,
        )

    def face_copy(step, kind, face, device, slot):
        return pltpu.make_async_remote_copy(
            src_ref=halo_out.at[kind, face],
            dst_ref=halo_in.at[step, kind, slot],
            send_sem=hsend_sem.at[kind, face],
            recv_sem=hrecv_sem.at[step, kind, slot],
            device_id=device,
            device_id_type=MESH,
        )

    def store_faces(kind, traces):
        for face in range(4):
            halo_out[kind, face] = traces[:, face * FACE : (face + 1) * FACE]

    def start_faces(step, kind):
        for face, (inside, device, slot) in enumerate(sides):

            @pl.when(inside)
            def _():
                face_copy(step, kind, face, device, slot).start()

    def take_faces(step, kind, traces):
        for face, (inside, device, slot) in enumerate(sides):

            @pl.when(inside)
            def _():
                face_copy(step, kind, slot, device, face).wait_recv()
                face_copy(step, kind, face, device, slot).wait_send()

        partner = jnp.concatenate([halo_in[step, kind, face] for face in range(4)], axis=1)
        return jnp.where(live > 0.5, traces - partner, 0.0)

    live = jnp.concatenate(
        [jnp.where(lane8 < face_len[0, face], 1.0, 0.0) for face in range(4)], axis=1
    )
    load_faces.wait()

    def build_pick(block, carry):
        start = pl.multiple_of(block * TILE, TILE)
        rows = row_ids((TILE, FACE)) + start
        for face in range(4):
            hit = rows == faces[face : face + 1, :]
            pick[pl.ds(start, TILE), face * FACE : (face + 1) * FACE] = jnp.where(hit, 1.0, 0.0).astype(BF16)
        return carry

    lax.fori_loop(0, NB, build_pick, 0)
    wide = LOADS + DEFL
    basis = parts(jnp.concatenate([r_ref[...], defl_f[...]], axis=0))
    for block in range(NB):
        wide_a[block] = basis[:, block * TILE : (block + 1) * TILE]
    both = fold(dot_nn(basis, pick[...]))
    tr_r[...] = both[0:LOADS]
    trace_t[0 : 2 * DEFL] = parts(both[LOADS:])
    trace_t[2 * DEFL :] = jnp.zeros((128 - 2 * DEFL, SLOTS), BF16)
    for face in range(4):
        first_out[face] = both[:, face * FACE : (face + 1) * FACE]
    for face, (inside, device, slot) in enumerate(sides):

        @pl.when(inside)
        def _():
            first_copy(face, device, slot).start()

    def build_spread(columns, target):
        lanes = lane_ids((LOADS, 128))
        rows = row_ids((NB * LOADS, 128))
        across = lane_ids((NB * LOADS, 128))
        for tile in range(4):
            named = jnp.zeros((LOADS, 128), jnp.int32)
            for spot in range(16):
                index = tile * 16 + spot
                named = jnp.where(lanes // LOADS == spot, columns[index % TPR, index // TPR], named)
            hit = (rows // LOADS == named[0:1, :]) & (rows % LOADS == across % LOADS)
            target[:, tile * 128 : (tile + 1) * 128] = jnp.where(hit, 1.0, 0.0).astype(BF16)

    build_spread(flex_cols, flex_s)
    build_spread(stiff_cols, stiff_s)

    def convert(pending, source, target):
        for n, load in enumerate(pending):
            load.wait()

            def one(block, carry):
                tiles = source[pl.ds(pl.multiple_of(block * TPR * TILE, TPR * TILE), TPR * TILE), :]
                high = tiles.astype(BF16)
                target[block, :, 0:TILE] = high
                target[block, :, TILE : 2 * TILE] = (tiles - high.astype(F32)).astype(BF16)
                return carry

            lax.fori_loop(n * NB // 4, (n + 1) * NB // 4, one, 0)

    convert(load_flex, flex_f, flex_t)
    convert(load_stiff, stiff_f, stiff_t)

    def coarse_ready():
        whole_across().wait_recv()

        def one_across(block, carry):
            rows = across_in[block]
            high = rows.astype(BF16)
            start = pl.multiple_of(block * DEFL, DEFL)
            across_h[pl.ds(start, DEFL), :] = high
            across_l[pl.ds(start, DEFL), :] = (rows - high.astype(F32)).astype(BF16)
            return carry

        lax.fori_loop(0, 8, one_across, 0)
        whole_coarse().wait_recv()

        def one(block, carry):
            start = pl.multiple_of(block * DEFL, DEFL)
            for part in range(2):
                rows = coarse_f[block, part]
                high = rows.astype(BF16)
                lanes = slice(part * 128, (part + 1) * 128)
                coarse_h[pl.ds(start, DEFL), lanes] = high
                coarse_l[pl.ds(start, DEFL), lanes] = (rows - high.astype(F32)).astype(BF16)
            return carry

        lax.fori_loop(0, GRID, one, 0)

    def forward(source, tiles, columns, target):
        for block in range(NB):
            operand = jnp.concatenate([source[columns[k, block]] for k in range(TPR)], axis=1)
            product = fold(dot_nn(operand, tiles[block]))
            target[block] = parts(product[:, 0:TILE] + product[:, TILE : 2 * TILE])

    def backward(source, tiles, selector, space):
        groups = space.shape[0]
        for block in range(NB):
            piece = source[block]
            product = fold(dot_nt(jnp.concatenate([piece, piece], axis=1), tiles[block]))
            rows = slice(block * TPR * LOADS, (block + 1) * TPR * LOADS)
            for group in range(groups):
                loads = product[group * LOADS : (group + 1) * LOADS]
                stacked = jnp.concatenate(
                    [loads[:, k * TILE : (k + 1) * TILE] for k in range(TPR)], axis=0
                )
                high = stacked.astype(BF16)
                space[group, rows, 0:TILE] = high
                space[group, rows, TILE : 2 * TILE] = (stacked - high.astype(F32)).astype(BF16)
        summed = []
        for group in range(groups):
            product = dot_nn(selector[...], space[group])
            summed.append(product[:, 0:TILE] + product[:, TILE : 2 * TILE])
        return [
            jnp.concatenate([one[block * LOADS : (block + 1) * LOADS] for one in summed], axis=0)
            for block in range(NB)
        ]

    forward(wide_a, flex_t, flex_cols, wide_b)
    forward(wide_b, stiff_t, stiff_cols, wide_a)
    gather_middle(0, coarse_ready)
    middle = backward(wide_a, stiff_t, stiff_s, wide_spread)
    for block in range(NB):
        wide_b[block] = parts(middle[block])
    applied = backward(wide_b, flex_t, flex_s, wide_spread)
    for block in range(NB):
        span = slice(block * TILE, (block + 1) * TILE)
        a_ref[:, span] = r_ref[:, span] + applied[block][0:LOADS]
        image_t[0 : 2 * DEFL, span] = parts(defl_f[:, span] + applied[block][LOADS:wide])
    image_t[2 * DEFL :] = jnp.zeros((128 - 2 * DEFL, M), BF16)

    for face, (inside, device, slot) in enumerate(sides):

        @pl.when(inside)
        def _():
            first_copy(slot, device, face).wait_recv()
            first_copy(face, device, slot).wait_send()

    def operator_coefficients(field, jump):
        return coefficients_of(dot_nt(parts(field), defl_t[...]) + dot_nt(parts(jump), trace_t[...]))

    partner = jnp.concatenate([first_in[face, 0:LOADS] for face in range(4)], axis=1)
    jump = jnp.where(live > 0.5, tr_r[...] - partner, 0.0)
    jump_r[...] = jump
    found = operator_coefficients(a_ref[...], jump)
    gr_ref[0] = turn(found, place)
    gr_ref[1] = pltpu.roll(found, DEFL, 1)

    traces = [first_out[face, LOADS:wide] for face in range(4)]
    others = [
        jnp.where(live[0:1, face * FACE : (face + 1) * FACE] > 0.5, first_in[face, LOADS:wide], 0.0)
        for face in range(4)
    ]
    masked = [
        jnp.where(live[0:1, face * FACE : (face + 1) * FACE] > 0.5, traces[face], 0.0)
        for face in range(4)
    ]
    lane32 = lane_ids((DEFL, 128))

    def paired(product):
        summed = fold(product)
        summed = summed + pltpu.roll(summed, 128 - DEFL, 1)
        return jnp.where(lane32 < DEFL, summed, 0.0)

    def against(value):
        return jnp.concatenate([parts(value), jnp.zeros((2 * DEFL, FACE), BF16)], axis=0)

    own = dot_nt(image_t[0 : 2 * DEFL], defl_t[...])
    for face in range(4):
        own = own + dot_nt(parts(masked[face]), trace_t[:, face * FACE : (face + 1) * FACE])
    north = paired(dot_nt(parts(others[0]), trace_t[:, 0:FACE]))
    south = paired(dot_nt(parts(others[1]), trace_t[:, FACE : 2 * FACE]))
    west = paired(dot_nt(parts(masked[2]), against(others[2])))
    east = paired(dot_nt(parts(masked[3]), against(others[3])))
    couple = jnp.concatenate(
        [
            -turn(north, place),
            turn(paired(own), place) - turn(west, (place + 3) % 4) - turn(east, (place + 1) % 4),
            -turn(south, place),
            jnp.zeros((DEFL, 128), F32),
        ],
        axis=0,
    )
    couple_t[...] = parts(couple)

    zeros = jnp.zeros((LOADS, M), F32)
    for ref in (b_ref, bw_ref, p_ref, q_ref, w_ref, x_ref, z_ref):
        ref[...] = zeros
    short = jnp.zeros((LOADS, SLOTS), F32)
    for ref in (tr_w, tr_q, jump_w, jump_q):
        ref[...] = short
    none = jnp.zeros((LOADS, 128), F32)
    for ref in (e_q, alpha_ref, beta_ref, cq_ref):
        ref[...] = none
    for layout in range(2):
        gq_ref[layout] = none
        gw_ref[layout] = none
    s1_ref[...] = jnp.ones((LOADS, 128), F32)

    e_r[...] = jnp.where(group8 < 3, gather_end(0), 0.0)
    own_ref[...] = none
    whole_coarse().wait_send()
    whole_across().wait_send()

    def energy_parts():
        energy = jnp.where(group8 == 1, e_r[...], 0.0)
        return parts(energy + pltpu.roll(energy, 128 - DEFL, 1))[:, 0 : 2 * DEFL]

    def across(ref, width):
        return jnp.concatenate([ref[...]] * (width // 128), axis=1)

    def advance():
        alpha = across(alpha_ref, M)
        beta = across(beta_ref, M)
        direction = z_ref[...] + beta * p_ref[...]
        image = w_ref[...] + beta * q_ref[...]
        p_ref[...] = direction
        q_ref[...] = image
        residual = r_ref[...] - alpha * image
        r_ref[...] = residual
        return alpha, beta, direction, image, residual

    def iterate(step, carry):
        energies = e_r[...]
        doubled = parts(energies)
        coefficients = fold(dot_nn(jnp.concatenate([doubled, doubled], axis=1), couple_t[...]))
        alpha, beta, p, q, r = advance()
        applied = bw_ref[...] + beta * b_ref[...]
        b_ref[...] = applied
        a = a_ref[...] - alpha * applied
        a_ref[...] = a
        for layout in range(2):
            image = gw_ref[layout] + beta_ref[...] * gq_ref[layout]
            gq_ref[layout] = image
            gr_ref[layout] = gr_ref[layout] - alpha_ref[...] * image
        image = own_ref[...] + beta_ref[...] * cq_ref[...]
        cq_ref[...] = image
        c = c_ref[...] - alpha_ref[...] * image
        c_ref[...] = c
        alpha_s = across(alpha_ref, SLOTS)
        beta_s = across(beta_ref, SLOTS)
        trace_q = tr_w[...] + beta_s * tr_q[...]
        tr_q[...] = trace_q
        tr = tr_r[...] - alpha_s * trace_q
        tr_r[...] = tr
        jump_q_now = jump_w[...] + beta_s * jump_q[...]
        jump_q[...] = jump_q_now
        jump_now = jump_r[...] - alpha_s * jump_q_now
        jump_r[...] = jump_now
        sum_zar = row_sum(r * a) + row_sum(tr * jump_now) + row_sum(energies * gr_ref[1])
        sum_rz = row_sum(r * r) + row_sum(energies * c)
        sum_rp = row_sum(r * p)
        sum_zq = row_sum(r * q) + row_sum(energies * image)
        energy = energy_parts()
        traces = tr + fold(dot_nn(energy, trace_t[0 : 2 * DEFL]))
        store_faces(0, traces)
        gather_start(
            step + 1, coefficients + gr_ref[0], energies, (sum_zar, sum_rz, sum_rp, sum_zq)
        )

        start_faces(step, 0)
        x_ref[...] = x_ref[...] + alpha * p
        z_ref[...] = r_ref[...] + fold(dot_nn(energy, defl_t[0 : 2 * DEFL]))
        w_ref[...] = a_ref[...] + fold(dot_nn(energy, image_t[0 : 2 * DEFL]))
        jump = take_faces(step, 0, traces)
        w = w_ref[...] + fold(dot_nt(parts(jump), pick[...]))
        w_ref[...] = w
        split = parts(w)
        for block in range(NB):
            blocks_a[block] = split[:, block * TILE : (block + 1) * TILE]

        @pl.when(step < ITERS - 1)
        def _():
            image = fold(dot_nn(split, pick[...]))
            tr_w[...] = image
            store_faces(1, image)
            start_faces(step, 1)

        gather_middle(step + 1)

        @pl.when(step < ITERS - 1)
        def _():
            forward(blocks_a, flex_t, flex_cols, blocks_b)
            forward(blocks_b, stiff_t, stiff_cols, blocks_a)
            middle = backward(blocks_a, stiff_t, stiff_s, spread)
            for block in range(NB):
                blocks_b[block] = parts(middle[block])
            jump = take_faces(step, 1, tr_w[...])
            jump_w[...] = jump
            found = coefficients_of(
                dot_nt(split, image_t[...]) + dot_nt(parts(jump), trace_t[...])
            )
            gw_ref[0] = turn(found, place)
            gw_ref[1] = pltpu.roll(found, DEFL, 1)
            local = backward(blocks_b, flex_t, flex_s, spread)
            bw_ref[...] = w_ref[...] + jnp.concatenate(local, axis=1)

        gathered = gather_end(step + 1)

        sum_zw, sum_rz, sum_rp, sum_zq = [
            jnp.broadcast_to(
                gathered[:, 3 * DEFL + index : 3 * DEFL + index + 1], (LOADS, 128)
            )
            for index in range(4)
        ]
        new_beta = -sum_zq / s1_ref[...]
        curvature = sum_zw + new_beta * sum_zq
        new_alpha = (sum_rz + new_beta * sum_rp) / curvature
        s1_ref[...] = curvature
        alpha_ref[...] = new_alpha
        beta_ref[...] = new_beta
        energy_q = jnp.where(group8 < 3, gathered, 0.0) + new_beta * e_q[...]
        e_q[...] = energy_q
        e_r[...] = e_r[...] - new_alpha * energy_q
        return carry

    lax.fori_loop(0, ITERS, iterate, 0)
    alpha, _, p, _, r = advance()
    x_ref[...] = x_ref[...] + alpha * p
    z_ref[...] = r + fold(dot_nn(energy_parts(), defl_t[0 : 2 * DEFL]))


def publish(x_in, r_in, z_in, x_out, r_out, z_out):
    x_out[...] = x_in[...]
    r_out[...] = r_in[...]
    z_out[...] = z_in[...]


def shards(rhs, flex, flex_cols, stiff, stiff_cols, defl, coarse, face_rows, face_len):
    anywhere = pl.BlockSpec(memory_space=pl.ANY)
    scalars = pl.BlockSpec(memory_space=pltpu.SMEM)
    vector = pl.BlockSpec(memory_space=pltpu.VMEM)
    field = jax.ShapeDtypeStruct((LOADS, M), F32)
    vmem = pltpu.VMEM
    dma = pltpu.SemaphoreType.DMA
    wide = 2 * (LOADS + DEFL)
    found = pl.pallas_call(
        kernel,
        out_shape=(field, field, field),
        in_specs=[
            anywhere, anywhere, scalars, anywhere, scalars, anywhere, anywhere, anywhere, scalars,
        ],
        out_specs=(vector, vector, vector),
        scratch_shapes=[
            vmem((NB * TPR * TILE, TILE), F32),
            vmem((NB * TPR * TILE, TILE), F32),
            vmem((DEFL, M), F32),
            vmem((DEFL, GRID * KROW), F32),
            vmem((GRID, 2, DEFL, 128), F32),
            vmem((8, DEFL, KROW), F32),
            vmem((8, DEFL, KROW), F32),
            vmem((4, FACE), jnp.int32),
            vmem((NB, TPR * TILE, 2 * TILE), BF16),
            vmem((NB, TPR * TILE, 2 * TILE), BF16),
            vmem((NB * LOADS, NB * TPR * LOADS), BF16),
            vmem((NB * LOADS, NB * TPR * LOADS), BF16),
            vmem((128, M), BF16),
            vmem((128, M), BF16),
            vmem((128, SLOTS), BF16),
            vmem((KROW, KROW // 2), BF16),
            vmem((KROW, KROW // 2), BF16),
            vmem((KROW // 2, KROW), BF16),
            vmem((KROW // 2, KROW), BF16),
            vmem((M, SLOTS), BF16),
            vmem((256, 128), BF16),
            vmem((NB, wide, TILE), BF16),
            vmem((NB, wide, TILE), BF16),
            vmem((wide // 16, NB * TPR * LOADS, 2 * TILE), BF16),
            vmem((NB, 2 * LOADS, TILE), BF16),
            vmem((NB, 2 * LOADS, TILE), BF16),
            vmem((1, NB * TPR * LOADS, 2 * TILE), BF16),
            *[vmem((LOADS, M), F32)] * 6,
            *[vmem((LOADS, SLOTS), F32)] * 6,
            *[vmem((LOADS, 128), F32)] * 5,
            *[vmem((2, LOADS, 128), F32)] * 3,
            *[vmem((LOADS, 128), F32)] * 3,
            vmem((4, LOADS, 128), F32),
            vmem((ITERS + 1, GRID, 2 * LOADS, 128), F32),
            vmem((GRID, LOADS, 128), F32),
            vmem((ITERS + 1, GRID, LOADS, 128), F32),
            vmem((4, LOADS + DEFL, FACE), F32),
            vmem((4, LOADS + DEFL, FACE), F32),
            vmem((2, 4, LOADS, FACE), F32),
            vmem((ITERS, 2, 4, LOADS, FACE), F32),
            dma((12,)),
            dma,
            dma,
            dma,
            dma,
            dma,
            dma((ITERS + 1,)),
            dma,
            dma((ITERS + 1,)),
            dma((4,)),
            dma((4,)),
            dma((2, 4)),
            dma((ITERS, 2, 4)),
        ],
        compiler_params=pltpu.CompilerParams(
            collective_id=0, has_side_effects=True, vmem_limit_bytes=66_500_000
        ),
        name="feti",
    )(rhs, flex, flex_cols.T, stiff, stiff_cols.T, defl, coarse, face_rows, face_len)
    return pl.pallas_call(
        publish,
        out_shape=(field, field, field),
        in_specs=[vector, vector, vector],
        out_specs=(vector, vector, vector),
        compiler_params=pltpu.CompilerParams(vmem_limit_bytes=66_500_000),
        name="publish",
    )(*found)


def solution(mesh):
    return jax.shard_map(
        shards,
        mesh=mesh,
        in_specs=(
            P("row", "col"),
            P("row", "col"),
            P("row", "col"),
            P("row", "col"),
            P("row", "col"),
            P("row", "col"),
            P(("row", "col"), None),
            P("row", "col"),
            P("row", "col"),
        ),
        out_specs=(P("row", "col"), P("row", "col"), P("row", "col")),
        check_vma=False,
    )
```

```python
import functools

import jax
import jax.numpy as jnp
from jax import lax
from jax.experimental import pallas as pl
from jax.experimental.pallas import tpu as pltpu
from jax.sharding import PartitionSpec as P

ITERS = 3
GRID = 16
LOADS = 8
NB = 16
TPR = 4
TILE = 128
M = 2048
DEFL = 32
FACE = 128
SLOTS = 4 * FACE
KROW = GRID * DEFL
MESH = pl.DeviceIdType.MESH
F32 = jnp.float32
BF16 = jnp.bfloat16


def dot_nn(a, b):
    return lax.dot_general(a, b, (((1,), (0,)), ((), ())), preferred_element_type=F32)


def dot_nt(a, b):
    return lax.dot_general(a, b, (((1,), (1,)), ((), ())), preferred_element_type=F32)


def parts(value):
    high = value.astype(BF16).astype(F32)
    return jnp.concatenate([high, value - high], axis=0).astype(BF16)


def fold(value):
    half = value.shape[0] // 2
    return value[:half] + value[half:]


def lane_ids(shape):
    return lax.broadcasted_iota(jnp.int32, shape, 1)


def row_ids(shape):
    return lax.broadcasted_iota(jnp.int32, shape, 0)


def row_sum(value):
    return jnp.sum(value, axis=1, keepdims=True)


def turn(value, place):
    moved = value
    for groups in range(1, 4):
        moved = jnp.where(place == groups, pltpu.roll(value, groups * DEFL, 1), moved)
    return moved


def kernel(
    rhs, flex, flex_cols, stiff, stiff_cols, defl, coarse, face_rows, face_len,
    x_ref, r_ref, z_ref,
    flex_f, stiff_f, defl_f, coarse_own, coarse_f, across_out, across_in, faces,
    flex_t, stiff_t, flex_s, stiff_s, defl_t, image_t, trace_t, coarse_h, coarse_l, across_h, across_l, pick, couple_t,
    wide_a, wide_b, wide_spread, blocks_a, blocks_b, spread,
    a_ref, b_ref, bw_ref, p_ref, q_ref, w_ref, tr_r, tr_w, tr_q, jump_r, jump_w, jump_q,
    e_r, e_q, s1_ref, alpha_ref, beta_ref, gr_ref, gq_ref, gw_ref, own_ref, c_ref, cq_ref,
    row_g, recv1, send2, recv2, first_out, first_in, halo_out, halo_in,
    load_sem, wsend, wrecv, asend, arecv, send1_sem, recv1_sem, send2_sem, recv2_sem, fsend_sem, frecv_sem,
    hsend_sem, hrecv_sem,
):
    i = lax.axis_index("row")
    j = lax.axis_index("col")
    place = j % 4
    pair = j // 4
    odd = (j // 2) % 2
    beside = (pair + 3 + 2 * odd) % 4
    far_groups = ((pair + 2) % 4, (pair + 1 + 2 * odd) % 4)
    chunk = NB * TPR * TILE // 4

    def part_of(ref, index):
        return ref.at[pl.ds(index * chunk, chunk), :]

    load_r = pltpu.make_async_copy(rhs, r_ref, load_sem.at[0])
    load_z = pltpu.make_async_copy(defl, defl_f, load_sem.at[1])
    load_faces = pltpu.make_async_copy(face_rows, faces, load_sem.at[2])
    load_coarse = pltpu.make_async_copy(coarse, coarse_own, load_sem.at[3])
    load_flex = [
        pltpu.make_async_copy(part_of(flex, n), part_of(flex_f, n), load_sem.at[4 + n]) for n in range(4)
    ]
    load_stiff = [
        pltpu.make_async_copy(part_of(stiff, n), part_of(stiff_f, n), load_sem.at[8 + n]) for n in range(4)
    ]

    row_partners = []
    for dy, dx in sorted(
        [(dy, dx) for dy in range(4) for dx in range(4) if dy or dx],
        key=lambda pair: -(min(pair[0], 4 - pair[0]) + min(pair[1], 4 - pair[1])),
    ):
        row_partners.append(((i // 4 + dy) % 4) * 4 + (i % 4 + dx) % 4)
    col_partners = [
        (j + offset) % GRID for offset in sorted(range(1, GRID), key=lambda o: -min(o, GRID - o))
    ]

    load_r.start()
    load_z.start()
    barrier = pltpu.get_barrier_semaphore()
    for there in row_partners:
        pl.semaphore_signal(barrier, inc=1, device_id=(there, j), device_id_type=MESH)
    for there in col_partners:
        pl.semaphore_signal(barrier, inc=1, device_id=(i, there), device_id_type=MESH)
    for load in [load_coarse, load_faces] + load_flex + load_stiff:
        load.start()

    def coarse_lanes(row, group):
        return pl.ds(pl.multiple_of(row * KROW + group * 128, 128), 128)

    def coarse_copy(there, part):
        return pltpu.make_async_remote_copy(
            src_ref=coarse.at[:, coarse_lanes(there, far_groups[part])],
            dst_ref=coarse_f.at[i, part],
            send_sem=wsend,
            recv_sem=wrecv,
            device_id=(there, j),
            device_id_type=MESH,
        )

    lane8 = lane_ids((LOADS, 128))
    group8 = lane8 // DEFL

    def copy1(phase, there):
        return pltpu.make_async_remote_copy(
            src_ref=recv1.at[phase, j],
            dst_ref=recv1.at[phase, j],
            send_sem=send1_sem,
            recv_sem=recv1_sem.at[phase],
            device_id=(i, there),
            device_id_type=MESH,
        )

    def copy2(phase, there):
        return pltpu.make_async_remote_copy(
            src_ref=send2.at[there],
            dst_ref=recv2.at[phase, i],
            send_sem=send2_sem,
            recv_sem=recv2_sem.at[phase],
            device_id=(there, j),
            device_id_type=MESH,
        )

    def whole1(phase):
        slots = recv1.at[phase, pl.ds(0, GRID - 1)]
        return pltpu.make_async_remote_copy(
            src_ref=slots,
            dst_ref=slots,
            send_sem=send1_sem,
            recv_sem=recv1_sem.at[phase],
            device_id=(i, j),
            device_id_type=MESH,
        )

    def whole2(phase):
        return pltpu.make_async_remote_copy(
            src_ref=send2.at[pl.ds(0, GRID - 1)],
            dst_ref=recv2.at[phase, pl.ds(0, GRID - 1)],
            send_sem=send2_sem,
            recv_sem=recv2_sem.at[phase],
            device_id=(i, j),
            device_id_type=MESH,
        )

    def across_copy(piece, there, slot):
        return pltpu.make_async_remote_copy(
            src_ref=across_out.at[piece],
            dst_ref=across_in.at[slot],
            send_sem=asend,
            recv_sem=arecv,
            device_id=(i, there),
            device_id_type=MESH,
        )

    def whole_across():
        return pltpu.make_async_remote_copy(
            src_ref=across_out.at[pl.ds(0, 7)],
            dst_ref=across_in.at[pl.ds(0, 7)],
            send_sem=asend,
            recv_sem=arecv,
            device_id=(i, j),
            device_id_type=MESH,
        )

    def whole_coarse():
        slots = coarse_f.at[pl.ds(0, GRID - 1)]
        return pltpu.make_async_remote_copy(
            src_ref=slots,
            dst_ref=slots,
            send_sem=wsend,
            recv_sem=wrecv,
            device_id=(i, j),
            device_id_type=MESH,
        )

    def gather_start(phase, coefficients, energy, sums):
        recv1[phase, j, 0:LOADS] = coefficients
        second = jnp.where(group8 == 1, energy, 0.0)
        for index, value in enumerate(sums):
            second = jnp.where(lane8 == 3 * DEFL + index, value, second)
        recv1[phase, j, LOADS : 2 * LOADS] = second
        for there in col_partners:
            copy1(phase, there).start()

    def gather_middle(phase, before_matmul=None):
        whole1(phase).wait_recv()
        first = [recv1[phase, source, 0:LOADS] for source in range(GRID)]
        groups = []
        for quarter in range(4):
            gathered = None
            for offset in range(4):
                source = quarter * 4 + offset
                value = first[source]
                if source:
                    value = value + first[source - 1]
                if source < GRID - 1:
                    value = value + first[source + 1]
                gathered = value if gathered is None else jnp.where(group8 == offset, value, gathered)
            groups.append(gathered)
        if before_matmul is not None:
            before_matmul()
        for quarter in range(4):
            row_g[quarter] = groups[quarter]
        near = parts(jnp.concatenate([row_g[pair], row_g[beside]], axis=1))
        far = parts(jnp.concatenate([row_g[far_groups[0]], row_g[far_groups[1]]], axis=1))
        partial = fold(
            dot_nn(near, across_h[...])
            + dot_nn(near, across_l[...])
            + dot_nt(far, coarse_h[...])
            + dot_nt(far, coarse_l[...])
        )
        total = None
        crossed = None
        for quarter in range(4):
            energies = None
            for offset in range(4):
                second = recv1[phase, quarter * 4 + offset, LOADS : 2 * LOADS]
                total = second if total is None else total + second
                shift = ((offset + 3) % 4) * DEFL
                moved = pltpu.roll(second, shift, 1) if shift else second
                energies = moved if energies is None else jnp.where(group8 == offset, moved, energies)
            crossed = groups[quarter] * energies + (0.0 if crossed is None else crossed)
        total = total + jnp.where(lane8 == 3 * DEFL, row_sum(crossed), 0.0)
        tiles = [partial[:, n * 128 : (n + 1) * 128] for n in range(4)]
        turned = [
            [tile if not n else pltpu.roll(tile, 128 - n * DEFL, 1) for n in range(4)] for tile in tiles
        ]
        for target in range(GRID):
            before = (target + GRID - 1) % GRID
            quarter, offset = before // 4, before % 4
            value = turned[quarter][offset]
            if offset > 1:
                value = jnp.where(group8 < 4 - offset, value, turned[(quarter + 1) % 4][offset])
            send2[target] = jnp.where(group8 < 3, value, total)
        for there in row_partners:
            copy2(phase, there).start()
        recv2[phase, i] = send2[i]
        mine = jnp.where(group8 == place, row_g[j // 4], 0.0)
        own_ref[...] = turn(mine, (5 - place) % 4)

    def gather_end(phase):
        whole2(phase).wait_recv()
        level = [recv2[phase, source] for source in range(GRID)]
        while len(level) > 1:
            level = [level[n] + level[n + 1] for n in range(0, len(level), 2)]
        whole1(phase).wait_send()
        whole2(phase).wait_send()
        return level[0]

    def coefficients_of(product):
        summed = fold(product)
        summed = summed + pltpu.roll(summed, 128 - DEFL, 1)
        return jnp.where(lane8 < DEFL, summed, 0.0)

    load_r.wait()
    load_z.wait()
    defl_high = defl_f[...].astype(BF16)
    defl_low = (defl_f[...] - defl_high.astype(F32)).astype(BF16)
    defl_t[0:DEFL] = defl_high
    defl_t[DEFL : 2 * DEFL] = defl_low
    defl_t[2 * DEFL :] = jnp.zeros((128 - 2 * DEFL, M), BF16)
    started = coefficients_of(dot_nt(parts(r_ref[...]), defl_t[...]))
    c_ref[...] = pltpu.roll(started, DEFL, 1)
    pl.semaphore_wait(barrier, 2 * (GRID - 1))
    for there in row_partners:
        for part in range(2):
            coarse_copy(there, part).start()
    gather_start(0, turn(started, place), jnp.zeros((LOADS, 128), F32), ())

    load_coarse.wait()
    group32 = lane_ids((DEFL, 128)) // DEFL
    after, ahead = (pair + 1) % 4, (pair + 3) % 4
    for piece, (group, spot) in enumerate(
        [(pair, 0), (pair, 1), (pair, 2), (pair, 3), (after, 0), (after, 1), (ahead, 2), (ahead, 3)]
    ):
        for quarter in range(4):
            packed = None
            for offset in range(4):
                value = coarse_own[:, coarse_lanes(quarter * 4 + offset, group)]
                shift = ((offset - spot) % 4) * DEFL
                if shift:
                    value = pltpu.roll(value, shift, 1)
                packed = value if packed is None else jnp.where(group32 == offset, value, packed)
            across_out[piece, :, quarter * 128 : (quarter + 1) * 128] = packed
    for piece, there in ((4, after * 4), (5, after * 4 + 1), (6, ahead * 4 + 2), (7, ahead * 4 + 3)):
        across_copy(piece, there, 4 + place).start()
    for step in range(1, 4):
        other = (place + step) % 4
        across_copy(other, pair * 4 + other, place).start()
    across_in[place] = across_out[place]
    for part in range(2):
        coarse_f[i, part] = coarse_own[:, coarse_lanes(i, far_groups[part])]

    sides = (
        (i > 0, (i - 1, j), 1),
        (i < GRID - 1, (i + 1, j), 0),
        (j > 0, (i, j - 1), 3),
        (j < GRID - 1, (i, j + 1), 2),
    )

    def first_copy(face, device, slot):
        return pltpu.make_async_remote_copy(
            src_ref=first_out.at[face],
            dst_ref=first_in.at[slot],
            send_sem=fsend_sem.at[face],
            recv_sem=frecv_sem.at[slot],
            device_id=device,
            device_id_type=MESH,
        )

    def face_copy(step, kind, face, device, slot):
        return pltpu.make_async_remote_copy(
            src_ref=halo_out.at[kind, face],
            dst_ref=halo_in.at[step, kind, slot],
            send_sem=hsend_sem.at[kind, face],
            recv_sem=hrecv_sem.at[step, kind, slot],
            device_id=device,
            device_id_type=MESH,
        )

    def store_faces(kind, traces):
        for face in range(4):
            halo_out[kind, face] = traces[:, face * FACE : (face + 1) * FACE]

    def start_faces(step, kind):
        for face, (inside, device, slot) in enumerate(sides):

            @pl.when(inside)
            def _():
                face_copy(step, kind, face, device, slot).start()

    def take_faces(step, kind, traces):
        for face, (inside, device, slot) in enumerate(sides):

            @pl.when(inside)
            def _():
                face_copy(step, kind, slot, device, face).wait_recv()
                face_copy(step, kind, face, device, slot).wait_send()

        partner = jnp.concatenate([halo_in[step, kind, face] for face in range(4)], axis=1)
        return jnp.where(live > 0.5, traces - partner, 0.0)

    live = jnp.concatenate(
        [jnp.where(lane8 < face_len[0, face], 1.0, 0.0) for face in range(4)], axis=1
    )
    load_faces.wait()

    def build_pick(block, carry):
        start = pl.multiple_of(block * TILE, TILE)
        rows = row_ids((TILE, FACE)) + start
        for face in range(4):
            hit = rows == faces[face : face + 1, :]
            pick[pl.ds(start, TILE), face * FACE : (face + 1) * FACE] = jnp.where(hit, 1.0, 0.0).astype(BF16)
        return carry

    lax.fori_loop(0, NB, build_pick, 0)
    wide = LOADS + DEFL
    basis = parts(jnp.concatenate([r_ref[...], defl_f[...]], axis=0))
    for block in range(NB):
        wide_a[block] = basis[:, block * TILE : (block + 1) * TILE]
    both = fold(dot_nn(basis, pick[...]))
    tr_r[...] = both[0:LOADS]
    trace_t[0 : 2 * DEFL] = parts(both[LOADS:])
    trace_t[2 * DEFL :] = jnp.zeros((128 - 2 * DEFL, SLOTS), BF16)
    for face in range(4):
        first_out[face] = both[:, face * FACE : (face + 1) * FACE]
    for face, (inside, device, slot) in enumerate(sides):

        @pl.when(inside)
        def _():
            first_copy(face, device, slot).start()

    def build_spread(columns, target):
        lanes = lane_ids((LOADS, 128))
        rows = row_ids((NB * LOADS, 128))
        across = lane_ids((NB * LOADS, 128))
        for tile in range(4):
            named = jnp.zeros((LOADS, 128), jnp.int32)
            for spot in range(16):
                index = tile * 16 + spot
                named = jnp.where(lanes // LOADS == spot, columns[index % TPR, index // TPR], named)
            hit = (rows // LOADS == named[0:1, :]) & (rows % LOADS == across % LOADS)
            target[:, tile * 128 : (tile + 1) * 128] = jnp.where(hit, 1.0, 0.0).astype(BF16)

    build_spread(flex_cols, flex_s)
    build_spread(stiff_cols, stiff_s)

    def convert(pending, source, target):
        for n, load in enumerate(pending):
            load.wait()

            def one(block, carry):
                tiles = source[pl.ds(pl.multiple_of(block * TPR * TILE, TPR * TILE), TPR * TILE), :]
                high = tiles.astype(BF16)
                target[block, :, 0:TILE] = high
                target[block, :, TILE : 2 * TILE] = (tiles - high.astype(F32)).astype(BF16)
                return carry

            lax.fori_loop(n * NB // 4, (n + 1) * NB // 4, one, 0)

    convert(load_flex, flex_f, flex_t)
    convert(load_stiff, stiff_f, stiff_t)

    def coarse_ready():
        whole_across().wait_recv()

        def one_across(block, carry):
            rows = across_in[block]
            high = rows.astype(BF16)
            start = pl.multiple_of(block * DEFL, DEFL)
            across_h[pl.ds(start, DEFL), :] = high
            across_l[pl.ds(start, DEFL), :] = (rows - high.astype(F32)).astype(BF16)
            return carry

        lax.fori_loop(0, 8, one_across, 0)
        whole_coarse().wait_recv()

        def one(block, carry):
            start = pl.multiple_of(block * DEFL, DEFL)
            for part in range(2):
                rows = coarse_f[block, part]
                high = rows.astype(BF16)
                lanes = slice(part * 128, (part + 1) * 128)
                coarse_h[pl.ds(start, DEFL), lanes] = high
                coarse_l[pl.ds(start, DEFL), lanes] = (rows - high.astype(F32)).astype(BF16)
            return carry

        lax.fori_loop(0, GRID, one, 0)

    def forward(source, tiles, columns, target):
        for block in range(NB):
            operand = jnp.concatenate([source[columns[k, block]] for k in range(TPR)], axis=1)
            product = fold(dot_nn(operand, tiles[block]))
            target[block] = parts(product[:, 0:TILE] + product[:, TILE : 2 * TILE])

    def backward(source, tiles, selector, space):
        groups = space.shape[0]
        for block in range(NB):
            piece = source[block]
            product = fold(dot_nt(jnp.concatenate([piece, piece], axis=1), tiles[block]))
            rows = slice(block * TPR * LOADS, (block + 1) * TPR * LOADS)
            for group in range(groups):
                loads = product[group * LOADS : (group + 1) * LOADS]
                stacked = jnp.concatenate(
                    [loads[:, k * TILE : (k + 1) * TILE] for k in range(TPR)], axis=0
                )
                high = stacked.astype(BF16)
                space[group, rows, 0:TILE] = high
                space[group, rows, TILE : 2 * TILE] = (stacked - high.astype(F32)).astype(BF16)
        summed = []
        for group in range(groups):
            product = dot_nn(selector[...], space[group])
            summed.append(product[:, 0:TILE] + product[:, TILE : 2 * TILE])
        return [
            jnp.concatenate([one[block * LOADS : (block + 1) * LOADS] for one in summed], axis=0)
            for block in range(NB)
        ]

    forward(wide_a, flex_t, flex_cols, wide_b)
    forward(wide_b, stiff_t, stiff_cols, wide_a)
    gather_middle(0, coarse_ready)
    middle = backward(wide_a, stiff_t, stiff_s, wide_spread)
    for block in range(NB):
        wide_b[block] = parts(middle[block])
    applied = backward(wide_b, flex_t, flex_s, wide_spread)
    for block in range(NB):
        span = slice(block * TILE, (block + 1) * TILE)
        a_ref[:, span] = r_ref[:, span] + applied[block][0:LOADS]
        image_t[0 : 2 * DEFL, span] = parts(defl_f[:, span] + applied[block][LOADS:wide])
    image_t[2 * DEFL :] = jnp.zeros((128 - 2 * DEFL, M), BF16)

    for face, (inside, device, slot) in enumerate(sides):

        @pl.when(inside)
        def _():
            first_copy(slot, device, face).wait_recv()
            first_copy(face, device, slot).wait_send()

    def operator_coefficients(field, jump):
        return coefficients_of(dot_nt(parts(field), defl_t[...]) + dot_nt(parts(jump), trace_t[...]))

    partner = jnp.concatenate([first_in[face, 0:LOADS] for face in range(4)], axis=1)
    jump = jnp.where(live > 0.5, tr_r[...] - partner, 0.0)
    jump_r[...] = jump
    found = operator_coefficients(a_ref[...], jump)
    gr_ref[0] = turn(found, place)
    gr_ref[1] = pltpu.roll(found, DEFL, 1)

    traces = [first_out[face, LOADS:wide] for face in range(4)]
    others = [
        jnp.where(live[0:1, face * FACE : (face + 1) * FACE] > 0.5, first_in[face, LOADS:wide], 0.0)
        for face in range(4)
    ]
    masked = [
        jnp.where(live[0:1, face * FACE : (face + 1) * FACE] > 0.5, traces[face], 0.0)
        for face in range(4)
    ]
    lane32 = lane_ids((DEFL, 128))

    def paired(product):
        summed = fold(product)
        summed = summed + pltpu.roll(summed, 128 - DEFL, 1)
        return jnp.where(lane32 < DEFL, summed, 0.0)

    def against(value):
        return jnp.concatenate([parts(value), jnp.zeros((2 * DEFL, FACE), BF16)], axis=0)

    own = dot_nt(image_t[0 : 2 * DEFL], defl_t[...])
    for face in range(4):
        own = own + dot_nt(parts(masked[face]), trace_t[:, face * FACE : (face + 1) * FACE])
    north = paired(dot_nt(parts(others[0]), trace_t[:, 0:FACE]))
    south = paired(dot_nt(parts(others[1]), trace_t[:, FACE : 2 * FACE]))
    west = paired(dot_nt(parts(masked[2]), against(others[2])))
    east = paired(dot_nt(parts(masked[3]), against(others[3])))
    couple = jnp.concatenate(
        [
            -turn(north, place),
            turn(paired(own), place) - turn(west, (place + 3) % 4) - turn(east, (place + 1) % 4),
            -turn(south, place),
            jnp.zeros((DEFL, 128), F32),
        ],
        axis=0,
    )
    couple_t[...] = parts(couple)

    zeros = jnp.zeros((LOADS, M), F32)
    for ref in (b_ref, bw_ref, p_ref, q_ref, w_ref, x_ref, z_ref):
        ref[...] = zeros
    short = jnp.zeros((LOADS, SLOTS), F32)
    for ref in (tr_w, tr_q, jump_w, jump_q):
        ref[...] = short
    none = jnp.zeros((LOADS, 128), F32)
    for ref in (e_q, alpha_ref, beta_ref, cq_ref):
        ref[...] = none
    for layout in range(2):
        gq_ref[layout] = none
        gw_ref[layout] = none
    s1_ref[...] = jnp.ones((LOADS, 128), F32)

    e_r[...] = jnp.where(group8 < 3, gather_end(0), 0.0)
    own_ref[...] = none
    whole_coarse().wait_send()
    whole_across().wait_send()

    def energy_parts():
        energy = jnp.where(group8 == 1, e_r[...], 0.0)
        return parts(energy + pltpu.roll(energy, 128 - DEFL, 1))[:, 0 : 2 * DEFL]

    def across(ref, width):
        return jnp.concatenate([ref[...]] * (width // 128), axis=1)

    def advance():
        alpha = across(alpha_ref, M)
        beta = across(beta_ref, M)
        direction = z_ref[...] + beta * p_ref[...]
        image = w_ref[...] + beta * q_ref[...]
        p_ref[...] = direction
        q_ref[...] = image
        residual = r_ref[...] - alpha * image
        r_ref[...] = residual
        return alpha, beta, direction, image, residual

    def iterate(step, carry):
        energies = e_r[...]
        doubled = parts(energies)
        coefficients = fold(dot_nn(jnp.concatenate([doubled, doubled], axis=1), couple_t[...]))
        alpha, beta, p, q, r = advance()
        applied = bw_ref[...] + beta * b_ref[...]
        b_ref[...] = applied
        a = a_ref[...] - alpha * applied
        a_ref[...] = a
        for layout in range(2):
            image = gw_ref[layout] + beta_ref[...] * gq_ref[layout]
            gq_ref[layout] = image
            gr_ref[layout] = gr_ref[layout] - alpha_ref[...] * image
        image = own_ref[...] + beta_ref[...] * cq_ref[...]
        cq_ref[...] = image
        c = c_ref[...] - alpha_ref[...] * image
        c_ref[...] = c
        alpha_s = across(alpha_ref, SLOTS)
        beta_s = across(beta_ref, SLOTS)
        trace_q = tr_w[...] + beta_s * tr_q[...]
        tr_q[...] = trace_q
        tr = tr_r[...] - alpha_s * trace_q
        tr_r[...] = tr
        jump_q_now = jump_w[...] + beta_s * jump_q[...]
        jump_q[...] = jump_q_now
        jump_now = jump_r[...] - alpha_s * jump_q_now
        jump_r[...] = jump_now
        sum_zar = row_sum(r * a) + row_sum(tr * jump_now) + row_sum(energies * gr_ref[1])
        sum_rz = row_sum(r * r) + row_sum(energies * c)
        sum_rp = row_sum(r * p)
        sum_zq = row_sum(r * q) + row_sum(energies * image)
        energy = energy_parts()
        traces = tr + fold(dot_nn(energy, trace_t[0 : 2 * DEFL]))
        store_faces(0, traces)
        start_faces(step, 0)
        gather_start(
            step + 1, coefficients + gr_ref[0], energies, (sum_zar, sum_rz, sum_rp, sum_zq)
        )

        x_ref[...] = x_ref[...] + alpha * p
        z_ref[...] = r_ref[...] + fold(dot_nn(energy, defl_t[0 : 2 * DEFL]))
        w_ref[...] = a_ref[...] + fold(dot_nn(energy, image_t[0 : 2 * DEFL]))
        jump = take_faces(step, 0, traces)
        w = w_ref[...] + fold(dot_nt(parts(jump), pick[...]))
        w_ref[...] = w
        split = parts(w)
        for block in range(NB):
            blocks_a[block] = split[:, block * TILE : (block + 1) * TILE]

        @pl.when(step < ITERS - 1)
        def _():
            image = fold(dot_nn(split, pick[...]))
            tr_w[...] = image
            store_faces(1, image)
            start_faces(step, 1)

        gather_middle(step + 1)

        @pl.when(step < ITERS - 1)
        def _():
            forward(blocks_a, flex_t, flex_cols, blocks_b)
            forward(blocks_b, stiff_t, stiff_cols, blocks_a)
            middle = backward(blocks_a, stiff_t, stiff_s, spread)
            for block in range(NB):
                blocks_b[block] = parts(middle[block])
            jump = take_faces(step, 1, tr_w[...])
            jump_w[...] = jump
            found = coefficients_of(
                dot_nt(split, image_t[...]) + dot_nt(parts(jump), trace_t[...])
            )
            gw_ref[0] = turn(found, place)
            gw_ref[1] = pltpu.roll(found, DEFL, 1)
            local = backward(blocks_b, flex_t, flex_s, spread)
            bw_ref[...] = w_ref[...] + jnp.concatenate(local, axis=1)

        gathered = gather_end(step + 1)

        sum_zw, sum_rz, sum_rp, sum_zq = [
            jnp.broadcast_to(
                gathered[:, 3 * DEFL + index : 3 * DEFL + index + 1], (LOADS, 128)
            )
            for index in range(4)
        ]
        new_beta = -sum_zq / s1_ref[...]
        curvature = sum_zw + new_beta * sum_zq
        new_alpha = (sum_rz + new_beta * sum_rp) / curvature
        s1_ref[...] = curvature
        alpha_ref[...] = new_alpha
        beta_ref[...] = new_beta
        energy_q = jnp.where(group8 < 3, gathered, 0.0) + new_beta * e_q[...]
        e_q[...] = energy_q
        e_r[...] = e_r[...] - new_alpha * energy_q
        return carry

    lax.fori_loop(0, ITERS, iterate, 0)
    alpha, _, p, _, r = advance()
    x_ref[...] = x_ref[...] + alpha * p
    z_ref[...] = r + fold(dot_nn(energy_parts(), defl_t[0 : 2 * DEFL]))


def publish(x_in, r_in, z_in, x_out, r_out, z_out):
    x_out[...] = x_in[...]
    r_out[...] = r_in[...]
    z_out[...] = z_in[...]


def shards(rhs, flex, flex_cols, stiff, stiff_cols, defl, coarse, face_rows, face_len):
    anywhere = pl.BlockSpec(memory_space=pl.ANY)
    scalars = pl.BlockSpec(memory_space=pltpu.SMEM)
    vector = pl.BlockSpec(memory_space=pltpu.VMEM)
    field = jax.ShapeDtypeStruct((LOADS, M), F32)
    vmem = pltpu.VMEM
    dma = pltpu.SemaphoreType.DMA
    wide = 2 * (LOADS + DEFL)
    found = pl.pallas_call(
        kernel,
        out_shape=(field, field, field),
        in_specs=[
            anywhere, anywhere, scalars, anywhere, scalars, anywhere, anywhere, anywhere, scalars,
        ],
        out_specs=(vector, vector, vector),
        scratch_shapes=[
            vmem((NB * TPR * TILE, TILE), F32),
            vmem((NB * TPR * TILE, TILE), F32),
            vmem((DEFL, M), F32),
            vmem((DEFL, GRID * KROW), F32),
            vmem((GRID, 2, DEFL, 128), F32),
            vmem((8, DEFL, KROW), F32),
            vmem((8, DEFL, KROW), F32),
            vmem((4, FACE), jnp.int32),
            vmem((NB, TPR * TILE, 2 * TILE), BF16),
            vmem((NB, TPR * TILE, 2 * TILE), BF16),
            vmem((NB * LOADS, NB * TPR * LOADS), BF16),
            vmem((NB * LOADS, NB * TPR * LOADS), BF16),
            vmem((128, M), BF16),
            vmem((128, M), BF16),
            vmem((128, SLOTS), BF16),
            vmem((KROW, KROW // 2), BF16),
            vmem((KROW, KROW // 2), BF16),
            vmem((KROW // 2, KROW), BF16),
            vmem((KROW // 2, KROW), BF16),
            vmem((M, SLOTS), BF16),
            vmem((256, 128), BF16),
            vmem((NB, wide, TILE), BF16),
            vmem((NB, wide, TILE), BF16),
            vmem((wide // 16, NB * TPR * LOADS, 2 * TILE), BF16),
            vmem((NB, 2 * LOADS, TILE), BF16),
            vmem((NB, 2 * LOADS, TILE), BF16),
            vmem((1, NB * TPR * LOADS, 2 * TILE), BF16),
            *[vmem((LOADS, M), F32)] * 6,
            *[vmem((LOADS, SLOTS), F32)] * 6,
            *[vmem((LOADS, 128), F32)] * 5,
            *[vmem((2, LOADS, 128), F32)] * 3,
            *[vmem((LOADS, 128), F32)] * 3,
            vmem((4, LOADS, 128), F32),
            vmem((ITERS + 1, GRID, 2 * LOADS, 128), F32),
            vmem((GRID, LOADS, 128), F32),
            vmem((ITERS + 1, GRID, LOADS, 128), F32),
            vmem((4, LOADS + DEFL, FACE), F32),
            vmem((4, LOADS + DEFL, FACE), F32),
            vmem((2, 4, LOADS, FACE), F32),
            vmem((ITERS, 2, 4, LOADS, FACE), F32),
            dma((12,)),
            dma,
            dma,
            dma,
            dma,
            dma,
            dma((ITERS + 1,)),
            dma,
            dma((ITERS + 1,)),
            dma((4,)),
            dma((4,)),
            dma((2, 4)),
            dma((ITERS, 2, 4)),
        ],
        compiler_params=pltpu.CompilerParams(
            collective_id=0, has_side_effects=True, vmem_limit_bytes=66_500_000
        ),
        name="feti",
    )(rhs, flex, flex_cols.T, stiff, stiff_cols.T, defl, coarse, face_rows, face_len)
    return pl.pallas_call(
        publish,
        out_shape=(field, field, field),
        in_specs=[vector, vector, vector],
        out_specs=(vector, vector, vector),
        compiler_params=pltpu.CompilerParams(vmem_limit_bytes=66_500_000),
        name="publish",
    )(*found)


def solution(mesh):
    return jax.shard_map(
        shards,
        mesh=mesh,
        in_specs=(
            P("row", "col"),
            P("row", "col"),
            P("row", "col"),
            P("row", "col"),
            P("row", "col"),
            P("row", "col"),
            P(("row", "col"), None),
            P("row", "col"),
            P("row", "col"),
        ),
        out_specs=(P("row", "col"), P("row", "col"), P("row", "col")),
        check_vma=False,
    )
```
